512 devices in a mesh: freq: 16 (over y, x_hi, core), gx: 32 (over z, x_lo).
Axes of the slice: x: 4 (x_hi: 2, x_lo: 2; x = x_hi * 2 + x_lo), y: 4, z: 16, core: 2. Of those that a mesh axis runs over, the one named last changes fastest.
Arguments:
- sigma_h: float32 [128, 64, 256], P('gx'), may hold values from 0.3 to 3
- sigma_v: float32 [128, 64, 256], P('gx'), may hold values from 0.3 to 3
- wave_scale: float32 [16], P('freq'), may hold values from 0.25 to 4
- field_start: bfloat16 [16, 2, 3, 128, 64, 256], P('freq', None, None, 'gx'), may hold values from -6 to 6
- adjoint_start: bfloat16 [16, 2, 3, 128, 64, 256], P('freq', None, None, 'gx'), may hold values from -6 to 6
- observed: bfloat16 [16, 2, 3, 128, 64, 256], P('freq', None, None, 'gx'), may hold values from -6 to 6
- tx_count: int32 [1], replicated, may hold values from 1 to 64
- tx_cells: int32 [64], replicated, may hold values from 0 to 2097151
Outputs:
- gradient: float32 [2, 128, 64, 256], P(None, 'gx', 'freq')
- final_field: float32 [16, 2, 3, 128, 64, 256], P('freq', None, None, 'gx')
The draws below stay inside these ranges and needn't reach their ends.
All inputs are finite; a program needn't handle non-finite values.
Results may differ from the reference program's by a relative error of at most 0.0003.
Values sent between devices are 32-bit elements; how exact they have to be, the bound alone decides.
No kernel may reach another device: no remote copies, remote signals or barrier semaphores. Data moves between devices by JAX's collectives and lax.ppermute only.
A program may use at most 64 MiB of HBM per device.

```python
import math
import jax
import jax.numpy as jnp
from jax import lax

NY = 64
NZ = 256
ITERS = 2
TX_MAX = 64
FREQS = 16
NX = 128


def with_ends(array, rng, low, high):
    spot = [jax.random.randint(jax.random.fold_in(rng, axis), (), 0, length) for axis, length in enumerate(array.shape)]
    main_axis = array.shape.index(max(array.shape))
    next_to = spot[:main_axis] + [(spot[main_axis] + 1) % array.shape[main_axis]] + spot[main_axis + 1:]
    return array.at[tuple(spot)].set(low).at[tuple(next_to)].set(high)


def shard_levels(key, extent, pieces, low, high):
    def one(position, shards_of):
        heights = jax.random.uniform(jax.random.fold_in(jax.random.fold_in(key, 6), position), (shards_of,), jnp.float32, low / len(pieces), high / len(pieces))
        return jnp.repeat(jnp.exp(heights), extent[position] // shards_of).reshape((-1,) + (1,) * (len(extent) - position - 1))

    factor_of = one(*pieces[0])
    for cut in pieces[1:]:
        factor_of = factor_of * one(*cut)
    return factor_of


def normal_values(rng, extent, deviation, reach, pieces=(), kind=jnp.bfloat16):
    result = jax.random.normal(rng, extent, jnp.float32) * deviation
    if len(pieces) > 0:
        result = shard_levels(rng, extent, pieces, -0.22, 0.18) * result
    return jnp.clip(result, min=-reach, max=reach).astype(kind)


def setup_inputs(seed: int = 0) -> dict:
    keys = jax.random.split(jax.random.key(seed), 9)
    return {
        "sigma_h": jnp.clip(jnp.exp(math.log(3.0) - 2.3025851 * jax.random.uniform(keys[0], (NX, NY, NZ), jnp.float32) ** shard_levels(keys[0], (NX, NY, NZ), ((0, 32),), -0.2, 0.2)), 0.3, 3.0),
        "sigma_v": jnp.clip(jnp.exp(math.log(3.0) - 2.3025851 * jax.random.uniform(keys[1], (NX, NY, NZ), jnp.float32) ** shard_levels(keys[1], (NX, NY, NZ), ((0, 32),), -0.2, 0.2)), 0.3, 3.0),
        "wave_scale": jnp.clip(jnp.exp(math.log(4.0) - 2.7725887 * jax.random.uniform(keys[2], (FREQS,), jnp.float32) ** shard_levels(keys[2], (FREQS,), ((0, 16),), -0.2, 0.2)), 0.25, 4.0),
        "field_start": normal_values(keys[3], (FREQS, 2, 3, NX, NY, NZ), 1.0, 6.0, ((0, 16), (3, 32))),
        "adjoint_start": normal_values(keys[4], (FREQS, 2, 3, NX, NY, NZ), 1.0, 6.0, ((0, 16), (3, 32))),
        "observed": normal_values(keys[5], (FREQS, 2, 3, NX, NY, NZ), 1.0, 6.0, ((0, 16), (3, 32))),
        "tx_count": jax.random.randint(keys[6], (1,), 1, TX_MAX + 1).astype(jnp.int32),
        "tx_cells": with_ends(jax.random.randint(keys[7], (TX_MAX,), 0, NX * NY * NZ), jax.random.fold_in(keys[7], 1), 0, (NX * NY * NZ) - 1).astype(jnp.int32),
    }


THETA = 0.5
SOURCE_GAIN = 8.0


def ahead_diff(values, along):
    along = values.ndim + along
    widths = [(0, 0)] * values.ndim
    widths[along] = (0, 1)
    padded = jnp.pad(values, widths)
    return lax.slice_in_dim(padded, 1, values.shape[along] + 1, axis=along) - values


def behind_diff(values, along):
    along = values.ndim + along
    widths = [(0, 0)] * values.ndim
    widths[along] = (1, 0)
    padded = jnp.pad(values, widths)
    return values - lax.slice_in_dim(padded, 0, values.shape[along], axis=along)


def curl_curl(efield):
    comp_x = efield[..., 0, :, :, :]
    comp_y = efield[..., 1, :, :, :]
    comp_z = efield[..., 2, :, :, :]
    twist_x = ahead_diff(comp_z, -2) - ahead_diff(comp_y, -1)
    twist_y = ahead_diff(comp_x, -1) - ahead_diff(comp_z, -3)
    twist_z = ahead_diff(comp_y, -3) - ahead_diff(comp_x, -2)
    back_x = behind_diff(twist_z, -2) - behind_diff(twist_y, -1)
    back_y = behind_diff(twist_x, -1) - behind_diff(twist_z, -3)
    back_z = behind_diff(twist_y, -3) - behind_diff(twist_x, -2)
    return jnp.stack([back_x, back_y, back_z], axis=-4)


def relax(efield, curled, source_term, sig_pair, wave_scale):
    sigma_comp = jnp.stack([sig_pair[0], sig_pair[0], sig_pair[1]])
    coupling = wave_scale[:, None, None, None, None] * sigma_comp[None]
    real_part = efield[:, 0]
    imag_part = efield[:, 1]
    resid_real = source_term[:, 0] - (curled[:, 0] - coupling * imag_part)
    resid_imag = source_term[:, 1] - (curled[:, 1] + coupling * real_part)
    modulus = 16.0 + coupling * coupling
    update_real = (4.0 * resid_real + coupling * resid_imag) / modulus
    update_imag = (4.0 * resid_imag - coupling * resid_real) / modulus
    return efield + THETA * jnp.stack([update_real, update_imag], axis=1)


def make_source(tx_cells, tx_count, wave_scale, x_start, slab_width, size_y, size_z):
    plane_size = size_y * size_z
    cell_x = tx_cells // plane_size - x_start
    remainder = tx_cells % plane_size
    cell_y = remainder // size_z
    cell_z = remainder % size_z
    active = (jnp.arange(tx_cells.shape[0]) < tx_count[0]) & (cell_x >= 0) & (cell_x < slab_width)
    weights = jnp.where(active, 1.0, 0.0).astype(jnp.float32)
    counts = jnp.zeros((slab_width, size_y, size_z), jnp.float32)
    counts = counts.at[jnp.clip(cell_x, 0, slab_width - 1), cell_y, cell_z].add(weights)
    imag_x = SOURCE_GAIN * wave_scale[:, None, None, None] * counts[None]
    blank = jnp.zeros_like(imag_x)
    real_block = jnp.stack([blank, blank, blank], axis=1)
    imag_block = jnp.stack([imag_x, blank, blank], axis=1)
    return jnp.stack([real_block, imag_block], axis=1)


def adjoint_source(efield, observed):
    differ = efield - observed.astype(jnp.float32)
    return jnp.stack([differ[:, 0], -differ[:, 1]], axis=1)


def gradient_terms(efield, adjoint, wave_scale):
    product = adjoint[:, 0] * efield[:, 1] + adjoint[:, 1] * efield[:, 0]
    weighted = wave_scale[:, None, None, None, None] * product
    horizontal = jnp.sum(weighted[:, 0] + weighted[:, 1], axis=0)
    vertical = jnp.sum(weighted[:, 2], axis=0)
    return jnp.stack([horizontal, vertical])


def reference(sigma_h, sigma_v, wave_scale, field_start, adjoint_start, observed, tx_count, tx_cells):
    sig_pair = jnp.stack([sigma_h, sigma_v])

    def per_freq(gradient, inputs):
        wave_one, start_one, adjoint_one, observed_one = inputs
        wave_vec = wave_one[None]
        source_term = make_source(tx_cells, tx_count, wave_vec, 0, NX, NY, NZ)
        efield = start_one[None].astype(jnp.float32)
        for sweep in range(ITERS):
            efield = relax(efield, curl_curl(efield), source_term, sig_pair, wave_vec)
        adjoint_rhs = adjoint_source(efield, observed_one[None])
        adjoint = adjoint_one[None].astype(jnp.float32)
        for sweep in range(ITERS):
            adjoint = relax(adjoint, curl_curl(adjoint), adjoint_rhs, sig_pair, wave_vec)
        gradient = gradient + gradient_terms(efield, adjoint, wave_vec)
        return gradient, efield[0]

    initial = jnp.zeros((2, NX, NY, NZ), jnp.float32)
    gradient, fields = lax.scan(per_freq, initial, (wave_scale, field_start, adjoint_start, observed))
    return gradient, fields
```

```python
import jax
import jax.numpy as jnp
from jax import lax
from jax.sharding import PartitionSpec as P

ITERS = 2


THETA = 0.5
SOURCE_GAIN = 8.0


def padded_2(cells, sides, width):
    for axis, dim in sides:
        count = lax.axis_size(axis)
        ends = count - 1
        head = lax.slice_in_dim(cells, 0, width, axis=dim)
        tail = lax.slice_in_dim(cells, cells.shape[dim] - width, cells.shape[dim], axis=dim)
        cells = jnp.concatenate(
            [
                lax.ppermute(tail, axis, [(i, (i + 1) % count) for i in range(ends)]),
                cells,
                lax.ppermute(head, axis, [((i + 1) % count, i) for i in range(ends)]),
            ],
            axis=dim,
        )
    return cells


def ahead_diff(values, along):
    along = values.ndim + along
    widths = [(0, 0)] * values.ndim
    widths[along] = (0, 1)
    padded = jnp.pad(values, widths)
    return lax.slice_in_dim(padded, 1, values.shape[along] + 1, axis=along) - values


def behind_diff(values, along):
    along = values.ndim + along
    widths = [(0, 0)] * values.ndim
    widths[along] = (1, 0)
    padded = jnp.pad(values, widths)
    return values - lax.slice_in_dim(padded, 0, values.shape[along], axis=along)


def curl_masked(efield, inside):
    comp_x = efield[..., 0, :, :, :]
    comp_y = efield[..., 1, :, :, :]
    comp_z = efield[..., 2, :, :, :]
    twist_x = (ahead_diff(comp_z, -2) - ahead_diff(comp_y, -1)) * inside
    twist_y = (ahead_diff(comp_x, -1) - ahead_diff(comp_z, -3)) * inside
    twist_z = (ahead_diff(comp_y, -3) - ahead_diff(comp_x, -2)) * inside
    back_x = behind_diff(twist_z, -2) - behind_diff(twist_y, -1)
    back_y = behind_diff(twist_x, -1) - behind_diff(twist_z, -3)
    back_z = behind_diff(twist_y, -3) - behind_diff(twist_x, -2)
    return jnp.stack([back_x, back_y, back_z], axis=-4)


def relax(efield, curled, source_term, sig_pair, wave_scale):
    sigma_comp = jnp.stack([sig_pair[0], sig_pair[0], sig_pair[1]])
    coupling = wave_scale[:, None, None, None, None] * sigma_comp[None]
    real_part = efield[:, 0]
    imag_part = efield[:, 1]
    resid_real = source_term[:, 0] - (curled[:, 0] - coupling * imag_part)
    resid_imag = source_term[:, 1] - (curled[:, 1] + coupling * real_part)
    modulus = 16.0 + coupling * coupling
    update_real = (4.0 * resid_real + coupling * resid_imag) / modulus
    update_imag = (4.0 * resid_imag - coupling * resid_real) / modulus
    return efield + THETA * jnp.stack([update_real, update_imag], axis=1)


def make_source(tx_cells, tx_count, wave_scale, x_start, slab_width, size_y, size_z):
    plane_size = size_y * size_z
    cell_x = tx_cells // plane_size - x_start
    remainder = tx_cells % plane_size
    cell_y = remainder // size_z
    cell_z = remainder % size_z
    active = (jnp.arange(tx_cells.shape[0]) < tx_count[0]) & (cell_x >= 0) & (cell_x < slab_width)
    weights = jnp.where(active, 1.0, 0.0).astype(jnp.float32)
    counts = jnp.zeros((slab_width, size_y, size_z), jnp.float32)
    counts = counts.at[jnp.clip(cell_x, 0, slab_width - 1), cell_y, cell_z].add(weights)
    imag_x = SOURCE_GAIN * wave_scale[:, None, None, None] * counts[None]
    blank = jnp.zeros_like(imag_x)
    real_block = jnp.stack([blank, blank, blank], axis=1)
    imag_block = jnp.stack([imag_x, blank, blank], axis=1)
    return jnp.stack([real_block, imag_block], axis=1)


def adjoint_source(efield, observed):
    differ = efield - observed.astype(jnp.float32)
    return jnp.stack([differ[:, 0], -differ[:, 1]], axis=1)


def gradient_terms(efield, adjoint, wave_scale):
    product = adjoint[:, 0] * efield[:, 1] + adjoint[:, 1] * efield[:, 0]
    weighted = wave_scale[:, None, None, None, None] * product
    horizontal = jnp.sum(weighted[:, 0] + weighted[:, 1], axis=0)
    vertical = jnp.sum(weighted[:, 2], axis=0)
    return jnp.stack([horizontal, vertical])


def inside_mask(first, width, total_x):
    positions = first + jnp.arange(width)
    return ((positions >= 0) & (positions < total_x)).astype(jnp.float32)[:, None, None]


def local_sweep(efield, source_term, sig_pair, wave_scale, inside_pad):
    padded = padded_2(efield, (("gx", 3),), 1)
    curled = curl_masked(padded, inside_pad)[:, :, :, 1:-1]
    return relax(efield, curled, source_term, sig_pair, wave_scale)


def on_device(
    sigma_h, sigma_v, wave_scale, field_start, adjoint_start, observed, tx_count, tx_cells
):
    slab_width = sigma_h.shape[0]
    size_y = sigma_h.shape[1]
    size_z = sigma_h.shape[2]
    slab_index = lax.axis_index("gx")
    total_x = slab_width * lax.axis_size("gx")
    slab_first = slab_index * slab_width
    sig_pair = jnp.stack([sigma_h, sigma_v])
    efield = field_start.astype(jnp.float32)
    adjoint = adjoint_start.astype(jnp.float32)
    inside_pad = inside_mask(slab_first - 1, slab_width + 2, total_x)
    source_term = make_source(
        tx_cells, tx_count, wave_scale, slab_first, slab_width, size_y, size_z
    )
    for sweep in range(ITERS):
        efield = local_sweep(efield, source_term, sig_pair, wave_scale, inside_pad)
    adjoint_rhs = adjoint_source(efield, observed)
    for sweep in range(ITERS):
        adjoint = local_sweep(adjoint, adjoint_rhs, sig_pair, wave_scale, inside_pad)
    local_grad = gradient_terms(efield, adjoint, wave_scale)
    count = lax.axis_size("freq")
    share_rows = size_y // count
    blocks = local_grad.reshape(2, slab_width, count, share_rows, size_z)
    blocks = jnp.moveaxis(blocks, 2, 0)
    gathered = lax.all_to_all(blocks, "freq", 0, 0)
    gradient = jnp.sum(gathered, axis=0)
    return (gradient, efield)


def solution(mesh):
    placed = (
        P("gx", None, None),
        P("gx", None, None),
        P("freq"),
        P("freq", None, None, "gx", None, None),
        P("freq", None, None, "gx", None, None),
        P("freq", None, None, "gx", None, None),
        P(),
        P(),
    )
    return jax.shard_map(
        on_device,
        mesh=mesh,
        in_specs=placed,
        out_specs=(P(None, "gx", "freq", None), P("freq", None, None, "gx", None, None)),
        check_vma=False,
    )
```

```python
import jax
import jax.numpy as jnp
from jax import lax
from jax.experimental import pallas as pl
from jax.experimental.pallas import tpu as pltpu
from jax.sharding import PartitionSpec as P

ITERS = 2
THETA = 0.5
SOURCE_GAIN = 8.0
ROWS = 8

VMEM = pl.BlockSpec(memory_space=pltpu.VMEM)
SMEM = pl.BlockSpec(memory_space=pltpu.SMEM)


def position(axis):
    index = lax.axis_index(axis)
    even = 1 - lax.rem(index, 2)
    return index, even


def side_layer(side, even, last):
    right = even if side == 0 else 1 - even
    return last * right, right.astype(jnp.float32)


def lane_of(shape):
    return lax.broadcasted_iota(jnp.int32, shape, len(shape) - 1)


def next_z(values):
    size = values.shape[-1]
    moved = pltpu.roll(values, size - 1, 1)
    return jnp.where(lane_of(values.shape) == size - 1, 0.0, moved)


def last_z(values):
    moved = pltpu.roll(values, 1, 1)
    return jnp.where(lane_of(values.shape) == 0, 0.0, moved)


def factors(sigma, wave):
    coupling = wave * sigma
    inverse = THETA / (16.0 + coupling * coupling)
    return coupling, 4.0 * inverse, coupling * inverse


def chunks(size_y):
    return [slice(y, y + ROWS) for y in range(0, size_y, ROWS)]


def behind_row(ref, index, y, size_y):
    now = ref[index + (slice(y, y + ROWS),)]
    if y == 0:
        row = lax.broadcasted_iota(jnp.int32, now.shape, 0)
        return now, jnp.where(row == 0, 0.0, pltpu.roll(now, 1, 0))
    return now, ref[index + (slice(y - 1, y - 1 + ROWS),)]


def ahead_row(ref, index, y, size_y):
    now = ref[index + (slice(y, y + ROWS),)]
    if y + ROWS == size_y:
        row = lax.broadcasted_iota(jnp.int32, now.shape, 0)
        return now, jnp.where(row == ROWS - 1, 0.0, pltpu.roll(now, ROWS - 1, 0))
    return now, ref[index + (slice(y + 1, y + 1 + ROWS),)]


def write_faces(face, out, right, size_y):
    for part in range(2):
        for y in range(0, size_y, ROWS):
            rows = slice(y, y + ROWS)
            ex, ex_next = ahead_row(face, (part, 0), y, size_y)
            out[part, 0, rows] = face[part, 1, rows] + right * (ex_next - ex)
            out[part, 1, rows] = face[part, 2, rows] + right * (next_z(ex) - ex)


def fix(halo, y, right, wave, sig_h, sig_v, size_y):
    _, h_four, h_coup = factors(sig_h, wave)
    _, v_four, v_coup = factors(sig_v, wave)
    extra = []
    for part in range(2):
        u, u_last = behind_row(halo, (part, 0), y, size_y)
        v = halo[part, 1, y : y + ROWS]
        extra.append((right * ((last_z(v) - v) - (u - u_last)), u, v))
    real, imag = [], []
    for comp in range(3):
        four, coup = (h_four, h_coup) if comp < 2 else (v_four, v_coup)
        real.append(four * extra[0][comp] + coup * extra[1][comp])
        imag.append(four * extra[1][comp] - coup * extra[0][comp])
    return real, imag


def twists(field, twist, edge, layers, size_y):
    def one(layer, carry):
        for part in range(2):
            for y in range(0, size_y, ROWS):
                rows = slice(y, y + ROWS)
                ex, ex_next = ahead_row(field, (layer, part, 0), y, size_y)
                ey = field[layer, part, 1, rows]
                ez, ez_next = ahead_row(field, (layer, part, 2), y, size_y)
                ey_right = field[layer + 1, part, 1, rows]
                ez_right = field[layer + 1, part, 2, rows]
                twist[layer + 1, part, 0, rows] = (ez_next - ez) - (next_z(ey) - ey)
                twist[layer + 1, part, 1, rows] = (next_z(ex) - ex) - (ez_right - ez)
                twist[layer + 1, part, 2, rows] = (ey_right - ey) - (ex_next - ex)
        return carry

    lax.fori_loop(0, layers, one, 0)
    for part in range(2):
        for rows in chunks(size_y):
            twist[0, part, 1, rows] = -edge * field[0, part, 2, rows]
            twist[0, part, 2, rows] = edge * field[0, part, 1, rows]


def curled(twist, layer, y, size_y):
    rows = slice(y, y + ROWS)
    result = []
    for part in range(2):
        hx, hx_last = behind_row(twist, (layer + 1, part, 0), y, size_y)
        hz, hz_last = behind_row(twist, (layer + 1, part, 2), y, size_y)
        hy = twist[layer + 1, part, 1, rows]
        hy_left = twist[layer, part, 1, rows]
        hz_left = twist[layer, part, 2, rows]
        result.append(
            (
                (hz - hz_last) - (hy - last_z(hy)),
                (hx - last_z(hx)) - (hz - hz_left),
                (hy - hy_left) - (hx - hx_last),
            )
        )
    return result


def relaxed(field, twist, layer, y, size_y, wave, sig_h, sig_v, source):
    rows = slice(y, y + ROWS)
    sides = (factors(sig_h, wave), factors(sig_v, wave))
    curl = curled(twist, layer, y, size_y)
    real, imag = [], []
    for comp in range(3):
        coupling, four, coup = sides[0] if comp < 2 else sides[1]
        er = field[layer, 0, comp, rows]
        ei = field[layer, 1, comp, rows]
        rr = coupling * ei - curl[0][comp]
        ri = -(coupling * er) - curl[1][comp]
        br, bi = source(0, comp), source(1, comp)
        if br is not None:
            rr = rr + br
        if bi is not None:
            ri = ri + bi
        real.append(er + (four * rr + coup * ri))
        imag.append(ei + (four * ri - coup * rr))
    return real, imag


def zero_layer(field, layer, size_y):
    for part in range(2):
        for comp in (1, 2):
            for rows in chunks(size_y):
                field[layer, part, comp, rows] = jnp.zeros((ROWS, field.shape[-1]), jnp.float32)


def widen(start, field, layers, size_y):
    for layer in range(layers):
        for part in range(2):
            for comp in range(3):
                field[layer, part, comp] = start[part, comp, layer].astype(jnp.float32)


def first_faces_kernel(start, adjoint, e_p, e_z, a_p, a_z, face):
    _, even = position("gx")
    layers, size_y = start.shape[2], start.shape[3]
    for values, outs in ((start, (e_p, e_z)), (adjoint, (a_p, a_z))):
        for side in range(2):
            layer, right = side_layer(side, even, layers - 1)
            for part in range(2):
                for comp in range(3):
                    face[part, comp] = values[part, comp, layer].astype(jnp.float32)
            write_faces(face, outs[side], right, size_y)


def first_sweep_kernel(
    wave_ref, count_ref, cells_ref, start, adjoint, sigma_h, sigma_v, e_out, a_out, src, field, twist
):
    index, _ = position("gx")
    layers, size_y, size_z = sigma_h.shape
    wave = wave_ref[0]
    edge = jnp.where(index > 0, 1.0, 0.0)
    src[...] = jnp.zeros_like(src)
    gain = SOURCE_GAIN * wave

    def slot(t, carry):
        cell = cells_ref[t]
        layer = cell // (size_y * size_z) - index * layers

        @pl.when((t < count_ref[0]) & (layer >= 0) & (layer < layers))
        def _():
            row = lax.rem(cell // size_z, size_y)
            spot = lane_of((1, size_z)) == lax.rem(cell, size_z)
            old = src[layer, pl.ds(row, 1), :]
            src[layer, pl.ds(row, 1), :] = old + jnp.where(spot, gain, 0.0)

        return carry

    lax.fori_loop(0, cells_ref.shape[0], slot, 0)

    zero_layer(field, layers, size_y)
    for values, out in ((start, e_out), (adjoint, a_out)):
        widen(values, field, layers, size_y)
        twists(field, twist, edge, layers, size_y)

        def one(layer, carry, out=out):
            for y in range(0, size_y, ROWS):
                rows = slice(y, y + ROWS)

                def source(part, comp):
                    return src[layer, rows] if out is e_out and part == 1 and comp == 0 else None

                new = relaxed(field, twist, layer, y, size_y, wave, sigma_h[layer, rows], sigma_v[layer, rows], source)
                for part in range(2):
                    for comp in range(3):
                        out[layer, part, comp, rows] = new[part][comp]
            return carry

        lax.fori_loop(0, layers, one, 0)


def second_faces_kernel(side, wave_ref, halo, part_new, sigma_h, sigma_v, face, send):
    _, even = position("gx")
    layers, size_y, _ = sigma_h.shape
    layer, right = side_layer(side, even, layers - 1)
    wave = wave_ref[0]
    for y in range(0, size_y, ROWS):
        rows = slice(y, y + ROWS)
        add = fix(halo, y, right, wave, sigma_h[layer, rows], sigma_v[layer, rows], size_y)
        for part in range(2):
            for comp in range(3):
                face[part, comp, rows] = part_new[layer, part, comp, rows] + add[part][comp]
    write_faces(face, send, right, size_y)


def gather_layers(body, face_p, face_z, field, even, layers):
    p_layer, _ = side_layer(0, even, layers - 1)
    z_layer, _ = side_layer(1, even, layers - 1)
    for part in range(2):
        for comp in range(3):
            for layer in range(1, layers - 1):
                field[layer, part, comp] = body[layer, part, comp]
            field[p_layer, part, comp] = face_p[part, comp]
            field[z_layer, part, comp] = face_z[part, comp]


def rhs_of(part, new, seen):
    return new - seen if part == 0 else seen - new


def second_sweep_kernel(
    wave_ref, e_body, e_p, e_z, a_part, src, observed, sigma_h, sigma_v, e_out, a_out, field, twist
):
    index, even = position("gx")
    layers, size_y, _ = sigma_h.shape
    wave = wave_ref[0]
    edge = jnp.where(index > 0, 1.0, 0.0)
    zero_layer(field, layers, size_y)
    gather_layers(e_body, e_p, e_z, field, even, layers)
    twists(field, twist, edge, layers, size_y)

    def one(layer, carry):
        for y in range(0, size_y, ROWS):
            rows = slice(y, y + ROWS)

            def source(part, comp):
                return src[layer, rows] if part == 1 and comp == 0 else None

            new = relaxed(field, twist, layer, y, size_y, wave, sigma_h[layer, rows], sigma_v[layer, rows], source)
            for part in range(2):
                for comp in range(3):
                    e_out[layer, part, comp, rows] = new[part][comp]
        return carry

    lax.fori_loop(0, layers, one, 0)

    def inner(layer, carry):
        add_rhs(layer, e_out, (layer,), a_part, observed, wave, sigma_h, sigma_v, a_out, (layer,), size_y, None)
        return carry

    lax.fori_loop(1, layers - 1, inner, 0)


def add_rhs(layer, new, at, a_part, observed, wave, sigma_h, sigma_v, a_out, out_at, size_y, extra):
    for y in range(0, size_y, ROWS):
        rows = slice(y, y + ROWS)
        sides = (factors(sigma_h[layer, rows], wave), factors(sigma_v[layer, rows], wave))
        add = extra(y) if extra is not None else None
        for comp in range(3):
            _, four, coup = sides[0] if comp < 2 else sides[1]
            br = rhs_of(0, new[at + (0, comp, rows)], observed[0, comp, layer, rows].astype(jnp.float32))
            bi = rhs_of(1, new[at + (1, comp, rows)], observed[1, comp, layer, rows].astype(jnp.float32))
            real = a_part[layer, 0, comp, rows] + (four * br + coup * bi)
            imag = a_part[layer, 1, comp, rows] + (four * bi - coup * br)
            if add is not None:
                real = real + add[0][comp]
                imag = imag + add[1][comp]
            a_out[out_at + (0, comp, rows)] = real
            a_out[out_at + (1, comp, rows)] = imag


def third_faces_kernel(
    side, wave_ref, e_halo, a_halo, e_part, a_part, observed, sigma_h, sigma_v, e_face, a_face, send
):
    _, even = position("gx")
    layers, size_y, _ = sigma_h.shape
    layer, right = side_layer(side, even, layers - 1)
    wave = wave_ref[0]
    for y in range(0, size_y, ROWS):
        rows = slice(y, y + ROWS)
        add = fix(e_halo, y, right, wave, sigma_h[layer, rows], sigma_v[layer, rows], size_y)
        for part in range(2):
            for comp in range(3):
                e_face[part, comp, rows] = e_part[layer, part, comp, rows] + add[part][comp]

    def extra(y):
        rows = slice(y, y + ROWS)
        return fix(a_halo, y, right, wave, sigma_h[layer, rows], sigma_v[layer, rows], size_y)

    add_rhs(layer, e_face, (), a_part, observed, wave, sigma_h, sigma_v, a_face, (), size_y, extra)
    write_faces(a_face, send, right, size_y)


def grad_rows(wave, field, adjoint):
    terms = [adjoint[0][comp] * field[1][comp] + adjoint[1][comp] * field[0][comp] for comp in range(3)]
    return wave * (terms[0] + terms[1]), wave * terms[2]


def put_rows(out, layers, layer, y, pair, share):
    for which in range(2):
        for k in range(ROWS // share):
            out[y // share + k, which, layer] = pair[which][k * share : (k + 1) * share]


def last_sweep_kernel(
    wave_ref, e_body, e_p, e_z, a_body, a_p, a_z, observed, sigma_h, sigma_v, final, faces, grad, field, twist
):
    index, even = position("gx")
    layers, size_y, _ = sigma_h.shape
    share = grad.shape[3]
    wave = wave_ref[0]
    edge = jnp.where(index > 0, 1.0, 0.0)
    sides = [side_layer(side, even, layers - 1)[0] for side in range(2)]
    for part in range(2):
        for comp in range(3):
            for layer in range(1, layers - 1):
                final[part, comp, layer] = e_body[layer, part, comp]
            final[part, comp, sides[0]] = e_p[part, comp]
            final[part, comp, sides[1]] = e_z[part, comp]
    zero_layer(field, layers, size_y)
    gather_layers(a_body, a_p, a_z, field, even, layers)
    twists(field, twist, edge, layers, size_y)

    def sweep(layer, y):
        rows = slice(y, y + ROWS)
        now = [[final[part, comp, layer, rows] for comp in range(3)] for part in range(2)]

        def source(part, comp):
            return rhs_of(part, now[part][comp], observed[part, comp, layer, rows].astype(jnp.float32))

        return now, relaxed(field, twist, layer, y, size_y, wave, sigma_h[layer, rows], sigma_v[layer, rows], source)

    def inner(layer, carry):
        for y in range(0, size_y, ROWS):
            now, new = sweep(layer, y)
            put_rows(grad, layers, layer, y, grad_rows(wave, now, new), share)
        return carry

    lax.fori_loop(1, layers - 1, inner, 0)

    def outer(side, carry):
        layer = jnp.where(side == 0, sides[0], sides[1])
        for y in range(0, size_y, ROWS):
            _, new = sweep(layer, y)
            for part in range(2):
                for comp in range(3):
                    faces[side, part, comp, y : y + ROWS] = new[part][comp]
        return carry

    lax.fori_loop(0, 2, outer, 0)


def gradient_kernel(wave_ref, halo_p, halo_z, e_p, e_z, faces, inner, sigma_h, sigma_v, grad):
    _, even = position("gx")
    layers, size_y, _ = sigma_h.shape
    share = grad.shape[3]
    wave = wave_ref[0]
    for layer in range(1, layers - 1):
        for which in range(2):
            grad[:, which, layer] = inner[:, which, layer]
    for side, (halo, now) in enumerate(((halo_p, e_p), (halo_z, e_z))):
        layer, right = side_layer(side, even, layers - 1)
        for y in range(0, size_y, ROWS):
            rows = slice(y, y + ROWS)
            add = fix(halo, y, right, wave, sigma_h[layer, rows], sigma_v[layer, rows], size_y)
            new = [[faces[side, part, comp, rows] + add[part][comp] for comp in range(3)] for part in range(2)]
            old = [[now[part, comp, rows] for comp in range(3)] for part in range(2)]
            put_rows(grad, layers, layer, y, grad_rows(wave, old, new), share)


def call(kernel, name, n_smem, n_vmem, outs, scratch=()):
    return pl.pallas_call(
        kernel,
        name=name,
        out_shape=tuple(jax.ShapeDtypeStruct(shape, jnp.float32) for shape in outs),
        in_specs=[SMEM] * n_smem + [VMEM] * n_vmem,
        out_specs=tuple(VMEM for _ in outs),
        scratch_shapes=[pltpu.VMEM(shape, jnp.float32) for shape in scratch],
        compiler_params=pltpu.CompilerParams(vmem_limit_bytes=24 << 20),
    )


def on_device(
    sigma_h, sigma_v, wave_scale, field_start, adjoint_start, observed, tx_count, tx_cells
):
    layers, size_y, size_z = sigma_h.shape
    slabs = lax.axis_size("gx")
    freqs = lax.axis_size("freq")
    share = size_y // freqs
    start = field_start[0]
    adjoint = adjoint_start[0]
    seen = observed[0]

    ends = (
        [(i, i + 1) for i in range(0, slabs - 1, 2)],
        [(i, i + 1) for i in range(1, slabs - 1, 2)],
    )
    swaps = [pairs + [(b, a) for a, b in pairs] for pairs in ends]

    def swap(values, side):
        return lax.ppermute(values, "gx", swaps[side])

    plane = (size_y, size_z)
    half = (2, 2) + plane
    face = (2, 3) + plane
    body = (layers,) + face
    more = (layers + 1,) + face

    e_p, e_z, a_p, a_z = call(first_faces_kernel, "first_faces", 0, 2, [half] * 4, [face])(start, adjoint)
    e_p_in, e_z_in = swap(e_p, 0), swap(e_z, 1)
    e1, a1, src = call(
        first_sweep_kernel, "first_sweep", 3, 4, [body, body, (layers,) + plane], [more, more]
    )(wave_scale, tx_count, tx_cells, start, adjoint, sigma_h, sigma_v)
    e1, e_p_in = lax.optimization_barrier((e1, e_p_in))

    def second(side, halo):
        return call(
            lambda *refs: second_faces_kernel(side, *refs), "second_faces_%d" % side, 1, 4, [face, half]
        )(wave_scale, halo, e1, sigma_h, sigma_v)

    e1_p, e1_p_out = second(0, e_p_in)
    a_p, e1_p_out = lax.optimization_barrier((a_p, e1_p_out))
    e1_p_in = swap(e1_p_out, 0)
    a_p_in = swap(a_p, 0)
    e1_z, e1_z_out = second(1, e_z_in)
    a_z, e1_z_out = lax.optimization_barrier((a_z, e1_z_out))
    e1_z_in = swap(e1_z_out, 1)
    a_z_in = swap(a_z, 1)
    e2, a1_body = call(second_sweep_kernel, "second_sweep", 1, 8, [body, body], [more, more])(
        wave_scale, e1, e1_p, e1_z, a1, src, seen, sigma_h, sigma_v
    )
    e2, e1_p_in = lax.optimization_barrier((e2, e1_p_in))

    def third(side, e_halo, a_halo):
        return call(
            lambda *refs: third_faces_kernel(side, *refs), "third_faces_%d" % side, 1, 7, [face, face, half]
        )(wave_scale, e_halo, a_halo, e2, a1, seen, sigma_h, sigma_v)

    e2_p, a1_p, a1_p_out = third(0, e1_p_in, a_p_in)
    a1_p_in = swap(a1_p_out, 0)
    e2_z, a1_z, a1_z_out = third(1, e1_z_in, a_z_in)
    a1_z_in = swap(a1_z_out, 1)
    blocks = (freqs, 2, layers, share, size_z)
    final, faces, inner = call(
        last_sweep_kernel,
        "last_sweep",
        1,
        9,
        [(2, 3, layers) + plane, (2,) + face, blocks],
        [more, more],
    )(wave_scale, e2, e2_p, e2_z, a1_body, a1_p, a1_z, seen, sigma_h, sigma_v)
    faces, a1_p_in = lax.optimization_barrier((faces, a1_p_in))
    (terms,) = call(gradient_kernel, "gradient", 1, 8, [blocks])(
        wave_scale, a1_p_in, a1_z_in, e2_p, e2_z, faces, inner, sigma_h, sigma_v
    )
    gathered = lax.all_to_all(terms, "freq", 0, 0)
    return (jnp.sum(gathered, axis=0), final[None])


def solution(mesh):
    placed = (
        P("gx", None, None),
        P("gx", None, None),
        P("freq"),
        P("freq", None, None, "gx", None, None),
        P("freq", None, None, "gx", None, None),
        P("freq", None, None, "gx", None, None),
        P(),
        P(),
    )
    return jax.shard_map(
        on_device,
        mesh=mesh,
        in_specs=placed,
        out_specs=(P(None, "gx", "freq", None), P("freq", None, None, "gx", None, None)),
        check_vma=False,
    )
```

```python
import jax
import jax.numpy as jnp
from jax import lax
from jax.experimental import pallas as pl
from jax.experimental.pallas import tpu as pltpu
from jax.sharding import PartitionSpec as P

ITERS = 2
THETA = 0.5
SOURCE_GAIN = 8.0
ROWS = 8
COSTS = (0, 0, 0, 0)

VMEM = pl.BlockSpec(memory_space=pltpu.VMEM)
SMEM = pl.BlockSpec(memory_space=pltpu.SMEM)


def position(axis):
    index = lax.axis_index(axis)
    even = 1 - lax.rem(index, 2)
    return index, even


def side_layer(side, even, last):
    right = even if side == 0 else 1 - even
    return last * right, right.astype(jnp.float32)


def lane_of(shape):
    return lax.broadcasted_iota(jnp.int32, shape, len(shape) - 1)


def next_z(values):
    size = values.shape[-1]
    moved = pltpu.roll(values, size - 1, 1)
    return jnp.where(lane_of(values.shape) == size - 1, 0.0, moved)


def last_z(values):
    moved = pltpu.roll(values, 1, 1)
    return jnp.where(lane_of(values.shape) == 0, 0.0, moved)


def factors(sigma, wave):
    coupling = wave * sigma
    inverse = THETA / (16.0 + coupling * coupling)
    return coupling, 4.0 * inverse, coupling * inverse


def chunks(size_y):
    return [slice(y, y + ROWS) for y in range(0, size_y, ROWS)]


def behind_row(ref, index, y, size_y):
    now = ref[index + (slice(y, y + ROWS),)]
    if y == 0:
        row = lax.broadcasted_iota(jnp.int32, now.shape, 0)
        return now, jnp.where(row == 0, 0.0, pltpu.roll(now, 1, 0))
    return now, ref[index + (slice(y - 1, y - 1 + ROWS),)]


def ahead_row(ref, index, y, size_y):
    now = ref[index + (slice(y, y + ROWS),)]
    if y + ROWS == size_y:
        row = lax.broadcasted_iota(jnp.int32, now.shape, 0)
        return now, jnp.where(row == ROWS - 1, 0.0, pltpu.roll(now, ROWS - 1, 0))
    return now, ref[index + (slice(y + 1, y + 1 + ROWS),)]


def write_faces(face, out, right, size_y):
    for part in range(2):
        for y in range(0, size_y, ROWS):
            rows = slice(y, y + ROWS)
            ex, ex_next = ahead_row(face, (part, 0), y, size_y)
            out[part, 0, rows] = face[part, 1, rows] + right * (ex_next - ex)
            out[part, 1, rows] = face[part, 2, rows] + right * (next_z(ex) - ex)


def fix(halo, y, right, wave, sig_h, sig_v, size_y):
    _, h_four, h_coup = factors(sig_h, wave)
    _, v_four, v_coup = factors(sig_v, wave)
    extra = []
    for part in range(2):
        u, u_last = behind_row(halo, (part, 0), y, size_y)
        v = halo[part, 1, y : y + ROWS]
        extra.append((right * ((last_z(v) - v) - (u - u_last)), u, v))
    real, imag = [], []
    for comp in range(3):
        four, coup = (h_four, h_coup) if comp < 2 else (v_four, v_coup)
        real.append(four * extra[0][comp] + coup * extra[1][comp])
        imag.append(four * extra[1][comp] - coup * extra[0][comp])
    return real, imag


def twists(field, twist, edge, layers, size_y):
    def one(layer, carry):
        for part in range(2):
            for y in range(0, size_y, ROWS):
                rows = slice(y, y + ROWS)
                ex, ex_next = ahead_row(field, (layer, part, 0), y, size_y)
                ey = field[layer, part, 1, rows]
                ez, ez_next = ahead_row(field, (layer, part, 2), y, size_y)
                ey_right = field[layer + 1, part, 1, rows]
                ez_right = field[layer + 1, part, 2, rows]
                twist[layer + 1, part, 0, rows] = (ez_next - ez) - (next_z(ey) - ey)
                twist[layer + 1, part, 1, rows] = (next_z(ex) - ex) - (ez_right - ez)
                twist[layer + 1, part, 2, rows] = (ey_right - ey) - (ex_next - ex)
        return carry

    lax.fori_loop(0, layers, one, 0)
    for part in range(2):
        for rows in chunks(size_y):
            twist[0, part, 1, rows] = -edge * field[0, part, 2, rows]
            twist[0, part, 2, rows] = edge * field[0, part, 1, rows]


def curled(twist, layer, y, size_y):
    rows = slice(y, y + ROWS)
    result = []
    for part in range(2):
        hx, hx_last = behind_row(twist, (layer + 1, part, 0), y, size_y)
        hz, hz_last = behind_row(twist, (layer + 1, part, 2), y, size_y)
        hy = twist[layer + 1, part, 1, rows]
        hy_left = twist[layer, part, 1, rows]
        hz_left = twist[layer, part, 2, rows]
        result.append(
            (
                (hz - hz_last) - (hy - last_z(hy)),
                (hx - last_z(hx)) - (hz - hz_left),
                (hy - hy_left) - (hx - hx_last),
            )
        )
    return result


def relaxed(field, twist, layer, y, size_y, wave, sig_h, sig_v, source):
    rows = slice(y, y + ROWS)
    sides = (factors(sig_h, wave), factors(sig_v, wave))
    curl = curled(twist, layer, y, size_y)
    real, imag = [], []
    for comp in range(3):
        coupling, four, coup = sides[0] if comp < 2 else sides[1]
        er = field[layer, 0, comp, rows]
        ei = field[layer, 1, comp, rows]
        rr = coupling * ei - curl[0][comp]
        ri = -(coupling * er) - curl[1][comp]
        br, bi = source(0, comp), source(1, comp)
        if br is not None:
            rr = rr + br
        if bi is not None:
            ri = ri + bi
        real.append(er + (four * rr + coup * ri))
        imag.append(ei + (four * ri - coup * rr))
    return real, imag


def zero_layer(field, layer, size_y):
    for part in range(2):
        for comp in (1, 2):
            for rows in chunks(size_y):
                field[layer, part, comp, rows] = jnp.zeros((ROWS, field.shape[-1]), jnp.float32)


def widen(start, field, layers, size_y):
    for layer in range(layers):
        for part in range(2):
            for comp in range(3):
                field[layer, part, comp] = start[part, comp, layer].astype(jnp.float32)


def first_faces_kernel(start, p_send, z_send, got, face, sems):
    _, even = position("gx")
    layers, size_y = start.shape[2], start.shape[3]
    sides = [side_layer(side, even, layers - 1) for side in range(2)]
    copies = [
        pltpu.make_async_copy(start.at[:, :, sides[side][0]], got.at[side], sems.at[side]) for side in range(2)
    ]
    for copy in copies:
        copy.start()
    for side, out in enumerate((p_send, z_send)):
        copies[side].wait()
        for part in range(2):
            for comp in range(3):
                face[part, comp] = got[side, part, comp].astype(jnp.float32)
        write_faces(face, out, sides[side][1], size_y)


def adjoint_faces_kernel(adjoint, p_send, z_send, face):
    _, even = position("gx")
    layers, size_y = adjoint.shape[2], adjoint.shape[3]
    for side, out in enumerate((p_send, z_send)):
        layer, right = side_layer(side, even, layers - 1)
        for part in range(2):
            for comp in range(3):
                face[part, comp] = adjoint[part, comp, layer].astype(jnp.float32)
        write_faces(face, out, right, size_y)


def first_sweep_kernel(
    wave_ref, count_ref, cells_ref, start, sigma_h, sigma_v, e_out, src, field, twist
):
    index, _ = position("gx")
    layers, size_y, size_z = sigma_h.shape
    wave = wave_ref[0]
    edge = jnp.where(index > 0, 1.0, 0.0)
    src[...] = jnp.zeros_like(src)
    gain = SOURCE_GAIN * wave

    def slot(t, carry):
        cell = cells_ref[t]
        layer = cell // (size_y * size_z) - index * layers

        @pl.when((t < count_ref[0]) & (layer >= 0) & (layer < layers))
        def _():
            row = lax.rem(cell // size_z, size_y)
            spot = lane_of((1, size_z)) == lax.rem(cell, size_z)
            old = src[layer, pl.ds(row, 1), :]
            src[layer, pl.ds(row, 1), :] = old + jnp.where(spot, gain, 0.0)

        return carry

    lax.fori_loop(0, cells_ref.shape[0], slot, 0)

    def source(part, comp, layer, rows):
        return src[layer, rows] if part == 1 and comp == 0 else None

    zero_layer(field, layers, size_y)
    whole_sweep(start, field, twist, edge, wave, sigma_h, sigma_v, e_out, source)


def first_adjoint_kernel(wave_ref, adjoint, sigma_h, sigma_v, a_out, field, twist):
    index, _ = position("gx")
    layers, size_y, _ = sigma_h.shape
    edge = jnp.where(index > 0, 1.0, 0.0)
    zero_layer(field, layers, size_y)
    none = lambda part, comp, layer, rows: None
    whole_sweep(adjoint, field, twist, edge, wave_ref[0], sigma_h, sigma_v, a_out, none)


def whole_sweep(values, field, twist, edge, wave, sigma_h, sigma_v, out, source):
    layers, size_y, _ = sigma_h.shape
    widen(values, field, layers, size_y)
    twists(field, twist, edge, layers, size_y)

    def one(layer, carry):
        for y in range(0, size_y, ROWS):
            rows = slice(y, y + ROWS)
            at = lambda part, comp: source(part, comp, layer, rows)
            new = relaxed(field, twist, layer, y, size_y, wave, sigma_h[layer, rows], sigma_v[layer, rows], at)
            for part in range(2):
                for comp in range(3):
                    out[layer, part, comp, rows] = new[part][comp]
        return carry

    lax.fori_loop(0, layers, one, 0)


def second_faces_kernel(side, wave_ref, halo, part_new, sigma_h, sigma_v, face, send):
    _, even = position("gx")
    layers, size_y, _ = sigma_h.shape
    layer, right = side_layer(side, even, layers - 1)
    wave = wave_ref[0]
    for y in range(0, size_y, ROWS):
        rows = slice(y, y + ROWS)
        add = fix(halo, y, right, wave, sigma_h[layer, rows], sigma_v[layer, rows], size_y)
        for part in range(2):
            for comp in range(3):
                face[part, comp, rows] = part_new[layer, part, comp, rows] + add[part][comp]
    write_faces(face, send, right, size_y)


def gather_layers(body, face_p, face_z, field, even, layers):
    p_layer, _ = side_layer(0, even, layers - 1)
    z_layer, _ = side_layer(1, even, layers - 1)
    for part in range(2):
        for comp in range(3):
            for layer in range(1, layers - 1):
                field[layer, part, comp] = body[layer, part, comp]
            field[p_layer, part, comp] = face_p[part, comp]
            field[z_layer, part, comp] = face_z[part, comp]


def rhs_of(part, new, seen):
    return new - seen if part == 0 else seen - new


def second_sweep_kernel(
    wave_ref, e_body, e_p, e_z, a_part, src, observed, sigma_h, sigma_v, e_out, a_out, field, twist
):
    index, even = position("gx")
    layers, size_y, _ = sigma_h.shape
    wave = wave_ref[0]
    edge = jnp.where(index > 0, 1.0, 0.0)
    zero_layer(field, layers, size_y)
    gather_layers(e_body, e_p, e_z, field, even, layers)
    twists(field, twist, edge, layers, size_y)

    def one(layer, carry):
        for y in range(0, size_y, ROWS):
            rows = slice(y, y + ROWS)

            def source(part, comp):
                return src[layer, rows] if part == 1 and comp == 0 else None

            new = relaxed(field, twist, layer, y, size_y, wave, sigma_h[layer, rows], sigma_v[layer, rows], source)
            for part in range(2):
                for comp in range(3):
                    e_out[layer, part, comp, rows] = new[part][comp]
        return carry

    lax.fori_loop(0, layers, one, 0)

    def inner(layer, carry):
        add_rhs(layer, e_out, (layer,), a_part, observed, wave, sigma_h, sigma_v, a_out, (layer,), size_y, None)
        return carry

    lax.fori_loop(1, layers - 1, inner, 0)


def add_rhs(layer, new, at, a_part, observed, wave, sigma_h, sigma_v, a_out, out_at, size_y, extra):
    for y in range(0, size_y, ROWS):
        rows = slice(y, y + ROWS)
        sides = (factors(sigma_h[layer, rows], wave), factors(sigma_v[layer, rows], wave))
        add = extra(y) if extra is not None else None
        for comp in range(3):
            _, four, coup = sides[0] if comp < 2 else sides[1]
            br = rhs_of(0, new[at + (0, comp, rows)], observed[0, comp, layer, rows].astype(jnp.float32))
            bi = rhs_of(1, new[at + (1, comp, rows)], observed[1, comp, layer, rows].astype(jnp.float32))
            real = a_part[layer, 0, comp, rows] + (four * br + coup * bi)
            imag = a_part[layer, 1, comp, rows] + (four * bi - coup * br)
            if add is not None:
                real = real + add[0][comp]
                imag = imag + add[1][comp]
            a_out[out_at + (0, comp, rows)] = real
            a_out[out_at + (1, comp, rows)] = imag


def third_faces_kernel(
    side, wave_ref, e_halo, a_halo, e_part, a_part, observed, sigma_h, sigma_v, e_face, a_face, send
):
    _, even = position("gx")
    layers, size_y, _ = sigma_h.shape
    layer, right = side_layer(side, even, layers - 1)
    wave = wave_ref[0]
    for y in range(0, size_y, ROWS):
        rows = slice(y, y + ROWS)
        add = fix(e_halo, y, right, wave, sigma_h[layer, rows], sigma_v[layer, rows], size_y)
        for part in range(2):
            for comp in range(3):
                e_face[part, comp, rows] = e_part[layer, part, comp, rows] + add[part][comp]

    def extra(y):
        rows = slice(y, y + ROWS)
        return fix(a_halo, y, right, wave, sigma_h[layer, rows], sigma_v[layer, rows], size_y)

    add_rhs(layer, e_face, (), a_part, observed, wave, sigma_h, sigma_v, a_face, (), size_y, extra)
    write_faces(a_face, send, right, size_y)


def grad_rows(wave, field, adjoint):
    terms = [adjoint[0][comp] * field[1][comp] + adjoint[1][comp] * field[0][comp] for comp in range(3)]
    return wave * (terms[0] + terms[1]), wave * terms[2]


def put_rows(out, place, y, pair, share):
    for which in range(2):
        for k in range(ROWS // share):
            out[y // share + k, which, place] = pair[which][k * share : (k + 1) * share]


def last_sweep_kernel(
    wave_ref, e_body, e_p, e_z, a_body, a_p, a_z, observed, sigma_h, sigma_v, final, faces, grad, field, twist
):
    index, even = position("gx")
    layers, size_y, _ = sigma_h.shape
    share = grad.shape[3]
    wave = wave_ref[0]
    edge = jnp.where(index > 0, 1.0, 0.0)
    sides = [side_layer(side, even, layers - 1)[0] for side in range(2)]
    for part in range(2):
        for comp in range(3):
            for layer in range(1, layers - 1):
                final[part, comp, layer] = e_body[layer, part, comp]
            final[part, comp, sides[0]] = e_p[part, comp]
            final[part, comp, sides[1]] = e_z[part, comp]
    zero_layer(field, layers, size_y)
    gather_layers(a_body, a_p, a_z, field, even, layers)
    twists(field, twist, edge, layers, size_y)

    def sweep(layer, y):
        rows = slice(y, y + ROWS)
        now = [[final[part, comp, layer, rows] for comp in range(3)] for part in range(2)]

        def source(part, comp):
            return rhs_of(part, now[part][comp], observed[part, comp, layer, rows].astype(jnp.float32))

        return now, relaxed(field, twist, layer, y, size_y, wave, sigma_h[layer, rows], sigma_v[layer, rows], source)

    def inner(layer, carry):
        for y in range(0, size_y, ROWS):
            now, new = sweep(layer, y)
            put_rows(grad, layer - 1, y, grad_rows(wave, now, new), share)
        return carry

    lax.fori_loop(1, layers - 1, inner, 0)

    def outer(side, carry):
        layer = jnp.where(side == 0, sides[0], sides[1])
        for y in range(0, size_y, ROWS):
            _, new = sweep(layer, y)
            for part in range(2):
                for comp in range(3):
                    faces[side, part, comp, y : y + ROWS] = new[part][comp]
        return carry

    lax.fori_loop(0, 2, outer, 0)


def gradient_kernel(wave_ref, halo_p, halo_z, e_p, e_z, faces, sigma_h, sigma_v, grad):
    _, even = position("gx")
    layers, size_y, _ = sigma_h.shape
    share = grad.shape[3]
    wave = wave_ref[0]
    for side, (halo, now) in enumerate(((halo_p, e_p), (halo_z, e_z))):
        layer, right = side_layer(side, even, layers - 1)
        place = right.astype(jnp.int32)
        for y in range(0, size_y, ROWS):
            rows = slice(y, y + ROWS)
            add = fix(halo, y, right, wave, sigma_h[layer, rows], sigma_v[layer, rows], size_y)
            new = [[faces[side, part, comp, rows] + add[part][comp] for comp in range(3)] for part in range(2)]
            old = [[now[part, comp, rows] for comp in range(3)] for part in range(2)]
            put_rows(grad, place, y, grad_rows(wave, old, new), share)


def total_kernel(outer, inner, out):
    freqs, _, between = inner.shape[:3]
    for which in range(2):
        for part, places in ((outer, (0, between + 1)), (inner, range(1, between + 1))):
            for k, layer in enumerate(places):
                total = part[0, which, k]
                for freq in range(1, freqs):
                    total = total + part[freq, which, k]
                out[which, layer] = total


def call(kernel, name, specs, outs, scratch=(), cost=0):
    return pl.pallas_call(
        kernel,
        name=name,
        out_shape=tuple(jax.ShapeDtypeStruct(shape, jnp.float32) for shape in outs),
        in_specs=specs,
        out_specs=tuple(VMEM for _ in outs),
        scratch_shapes=[s if not isinstance(s, tuple) else pltpu.VMEM(s, jnp.float32) for s in scratch],
        compiler_params=pltpu.CompilerParams(vmem_limit_bytes=24 << 20),
        cost_estimate=pl.CostEstimate(flops=cost, bytes_accessed=cost, transcendentals=0) if cost else None,
    )


def on_device(
    sigma_h, sigma_v, wave_scale, field_start, adjoint_start, observed, tx_count, tx_cells
):
    layers, size_y, size_z = sigma_h.shape
    slabs = lax.axis_size("gx")
    freqs = lax.axis_size("freq")
    share = size_y // freqs
    start = field_start[0]
    adjoint = adjoint_start[0]
    seen = observed[0]

    ends = (
        [(i, i + 1) for i in range(0, slabs - 1, 2)],
        [(i, i + 1) for i in range(1, slabs - 1, 2)],
    )
    swaps = [pairs + [(b, a) for a, b in pairs] for pairs in ends]

    def swap(values, side):
        return lax.ppermute(values, "gx", swaps[side])

    plane = (size_y, size_z)
    half = (2, 2) + plane
    face = (2, 3) + plane
    body = (layers,) + face
    more = (layers + 1,) + face
    hbm = pl.BlockSpec(memory_space=pltpu.HBM)

    e_p, e_z = call(
        first_faces_kernel,
        "first_faces",
        [hbm],
        [half] * 2,
        [pltpu.VMEM((2,) + face, jnp.bfloat16), face, pltpu.SemaphoreType.DMA((2,))],
    )(start)
    e_p_in, e_z_in = swap(e_p, 0), swap(e_z, 1)
    e1, src = call(
        first_sweep_kernel,
        "first_sweep",
        [SMEM] * 3 + [VMEM] * 3,
        [body, (layers,) + plane],
        [more, more],
        COSTS[0],
    )(wave_scale, tx_count, tx_cells, start, sigma_h, sigma_v)
    a_p, a_z = call(adjoint_faces_kernel, "adjoint_faces", [VMEM], [half] * 2, [face])(adjoint)
    a_p, a_z, src = lax.optimization_barrier((a_p, a_z, src))
    a_p_in, a_z_in = swap(a_p, 0), swap(a_z, 1)
    (a1,) = call(
        first_adjoint_kernel, "first_adjoint", [SMEM] + [VMEM] * 3, [body], [more, more], COSTS[1]
    )(wave_scale, adjoint, sigma_h, sigma_v)
    a1, e1, e_p_in = lax.optimization_barrier((a1, e1, e_p_in))

    def second(side, halo):
        return call(
            lambda *refs: second_faces_kernel(side, *refs),
            "second_faces_%d" % side,
            [SMEM] + [VMEM] * 4,
            [face, half],
        )(wave_scale, halo, e1, sigma_h, sigma_v)

    e1_p, e1_p_out = second(0, e_p_in)
    e1_p_in = swap(e1_p_out, 0)
    e1_z, e1_z_out = second(1, e_z_in)
    e1_z_in = swap(e1_z_out, 1)
    e1_z, a_z_in, a_p_in = lax.optimization_barrier((e1_z, a_z_in, a_p_in))
    e2, a1_body = call(
        second_sweep_kernel, "second_sweep", [SMEM] + [VMEM] * 8, [body, body], [more, more], COSTS[2]
    )(wave_scale, e1, e1_p, e1_z, a1, src, seen, sigma_h, sigma_v)
    e2, e1_p_in = lax.optimization_barrier((e2, e1_p_in))

    def third(side, e_halo, a_halo):
        return call(
            lambda *refs: third_faces_kernel(side, *refs),
            "third_faces_%d" % side,
            [SMEM] + [VMEM] * 7,
            [face, face, half],
        )(wave_scale, e_halo, a_halo, e2, a1, seen, sigma_h, sigma_v)

    e2_p, a1_p, a1_p_out = third(0, e1_p_in, a_p_in)
    a1_p_in = swap(a1_p_out, 0)
    e2_z, a1_z, a1_z_out = third(1, e1_z_in, a_z_in)
    a1_z_in = swap(a1_z_out, 1)
    inner_blocks = (freqs, 2, layers - 2, share, size_z)
    outer_blocks = (freqs, 2, 2, share, size_z)
    final, faces, inner = call(
        last_sweep_kernel,
        "last_sweep",
        [SMEM] + [VMEM] * 9,
        [(2, 3, layers) + plane, (2,) + face, inner_blocks],
        [more, more],
        COSTS[3],
    )(wave_scale, e2, e2_p, e2_z, a1_body, a1_p, a1_z, seen, sigma_h, sigma_v)
    faces, a1_p_in = lax.optimization_barrier((faces, a1_p_in))
    inner_in = lax.all_to_all(inner, "freq", 0, 0)
    (outer,) = call(gradient_kernel, "gradient", [SMEM] + [VMEM] * 7, [outer_blocks])(
        wave_scale, a1_p_in, a1_z_in, e2_p, e2_z, faces, sigma_h, sigma_v
    )
    outer_in = lax.all_to_all(outer, "freq", 0, 0)
    (gradient,) = call(total_kernel, "total", [VMEM] * 2, [(2, layers, share, size_z)])(outer_in, inner_in)
    return (gradient, final[None])


def solution(mesh):
    placed = (
        P("gx", None, None),
        P("gx", None, None),
        P("freq"),
        P("freq", None, None, "gx", None, None),
        P("freq", None, None, "gx", None, None),
        P("freq", None, None, "gx", None, None),
        P(),
        P(),
    )
    return jax.shard_map(
        on_device,
        mesh=mesh,
        in_specs=placed,
        out_specs=(P(None, "gx", "freq", None), P("freq", None, None, "gx", None, None)),
        check_vma=False,
    )
```

```python
import jax
import jax.numpy as jnp
from jax import lax
from jax.experimental import pallas as pl
from jax.experimental.pallas import tpu as pltpu
from jax.sharding import PartitionSpec as P

ITERS = 2
THETA = 0.5
SOURCE_GAIN = 8.0
ROWS = 8

VMEM = pl.BlockSpec(memory_space=pltpu.VMEM)


def position(axis):
    index = lax.axis_index(axis)
    even = 1 - lax.rem(index, 2)
    return index, even


def side_layer(side, even, last):
    right = even if side == 0 else 1 - even
    return last * right, right.astype(jnp.float32)


def lane_of(shape):
    return lax.broadcasted_iota(jnp.int32, shape, len(shape) - 1)


def next_z(values):
    size = values.shape[-1]
    moved = pltpu.roll(values, size - 1, 1)
    return jnp.where(lane_of(values.shape) == size - 1, 0.0, moved)


def last_z(values):
    moved = pltpu.roll(values, 1, 1)
    return jnp.where(lane_of(values.shape) == 0, 0.0, moved)


def factors(sigma, wave):
    coupling = wave * sigma
    inverse = THETA / (16.0 + coupling * coupling)
    return coupling, 4.0 * inverse, coupling * inverse


def chunks(size_y):
    return [slice(y, y + ROWS) for y in range(0, size_y, ROWS)]


def behind_row(ref, index, y, size_y):
    now = ref[index + (slice(y, y + ROWS),)]
    if y == 0:
        row = lax.broadcasted_iota(jnp.int32, now.shape, 0)
        return now, jnp.where(row == 0, 0.0, pltpu.roll(now, 1, 0))
    return now, ref[index + (slice(y - 1, y - 1 + ROWS),)]


def ahead_row(ref, index, y, size_y):
    now = ref[index + (slice(y, y + ROWS),)]
    if y + ROWS == size_y:
        row = lax.broadcasted_iota(jnp.int32, now.shape, 0)
        return now, jnp.where(row == ROWS - 1, 0.0, pltpu.roll(now, ROWS - 1, 0))
    return now, ref[index + (slice(y + 1, y + 1 + ROWS),)]


def write_faces(face, out, right, size_y):
    for part in range(2):
        for y in range(0, size_y, ROWS):
            rows = slice(y, y + ROWS)
            ex, ex_next = ahead_row(face, (part, 0), y, size_y)
            out[part, 0, rows] = face[part, 1, rows] + right * (ex_next - ex)
            out[part, 1, rows] = face[part, 2, rows] + right * (next_z(ex) - ex)


def fix(halo, y, right, wave, sig_h, sig_v, size_y):
    _, h_four, h_coup = factors(sig_h, wave)
    _, v_four, v_coup = factors(sig_v, wave)
    extra = []
    for part in range(2):
        u, u_last = behind_row(halo, (part, 0), y, size_y)
        v = halo[part, 1, y : y + ROWS]
        extra.append((right * ((last_z(v) - v) - (u - u_last)), u, v))
    real, imag = [], []
    for comp in range(3):
        four, coup = (h_four, h_coup) if comp < 2 else (v_four, v_coup)
        real.append(four * extra[0][comp] + coup * extra[1][comp])
        imag.append(four * extra[1][comp] - coup * extra[0][comp])
    return real, imag


def twists(field, twist, edge, layers, size_y):
    def one(layer, carry):
        for part in range(2):
            for y in range(0, size_y, ROWS):
                rows = slice(y, y + ROWS)
                ex, ex_next = ahead_row(field, (layer, part, 0), y, size_y)
                ey = field[layer, part, 1, rows]
                ez, ez_next = ahead_row(field, (layer, part, 2), y, size_y)
                ey_right = field[layer + 1, part, 1, rows]
                ez_right = field[layer + 1, part, 2, rows]
                twist[layer + 1, part, 0, rows] = (ez_next - ez) - (next_z(ey) - ey)
                twist[layer + 1, part, 1, rows] = (next_z(ex) - ex) - (ez_right - ez)
                twist[layer + 1, part, 2, rows] = (ey_right - ey) - (ex_next - ex)
        return carry

    lax.fori_loop(0, layers, one, 0)
    for part in range(2):
        for rows in chunks(size_y):
            twist[0, part, 1, rows] = -edge * field[0, part, 2, rows]
            twist[0, part, 2, rows] = edge * field[0, part, 1, rows]


def curled(twist, layer, y, size_y):
    rows = slice(y, y + ROWS)
    result = []
    for part in range(2):
        hx, hx_last = behind_row(twist, (layer + 1, part, 0), y, size_y)
        hz, hz_last = behind_row(twist, (layer + 1, part, 2), y, size_y)
        hy = twist[layer + 1, part, 1, rows]
        hy_left = twist[layer, part, 1, rows]
        hz_left = twist[layer, part, 2, rows]
        result.append(
            (
                (hz - hz_last) - (hy - last_z(hy)),
                (hx - last_z(hx)) - (hz - hz_left),
                (hy - hy_left) - (hx - hx_last),
            )
        )
    return result


def relaxed(field, twist, layer, y, size_y, wave, sig_h, sig_v, source):
    rows = slice(y, y + ROWS)
    sides = (factors(sig_h, wave), factors(sig_v, wave))
    curl = curled(twist, layer, y, size_y)
    real, imag = [], []
    for comp in range(3):
        coupling, four, coup = sides[0] if comp < 2 else sides[1]
        er = field[layer, 0, comp, rows]
        ei = field[layer, 1, comp, rows]
        rr = coupling * ei - curl[0][comp]
        ri = -(coupling * er) - curl[1][comp]
        br, bi = source(0, comp), source(1, comp)
        if br is not None:
            rr = rr + br
        if bi is not None:
            ri = ri + bi
        real.append(er + (four * rr + coup * ri))
        imag.append(ei + (four * ri - coup * rr))
    return real, imag


def zero_layer(field, layer, size_y):
    for part in range(2):
        for comp in (1, 2):
            for rows in chunks(size_y):
                field[layer, part, comp, rows] = jnp.zeros((ROWS, field.shape[-1]), jnp.float32)


def widen(start, field, layers, size_y):
    for layer in range(layers):
        for part in range(2):
            for comp in range(3):
                field[layer, part, comp] = start[part, comp, layer].astype(jnp.float32)


def first_faces_kernel(start, p_send, z_send, got, face, sems):
    _, even = position("gx")
    layers, size_y = start.shape[2], start.shape[3]
    sides = [side_layer(side, even, layers - 1) for side in range(2)]
    copies = [
        pltpu.make_async_copy(start.at[:, :, sides[side][0]], got.at[side], sems.at[side]) for side in range(2)
    ]
    for copy in copies:
        copy.start()
    for side, out in enumerate((p_send, z_send)):
        copies[side].wait()
        for part in range(2):
            for comp in range(3):
                face[part, comp] = got[side, part, comp].astype(jnp.float32)
        write_faces(face, out, sides[side][1], size_y)


def adjoint_faces_kernel(adjoint, p_send, z_send, face):
    _, even = position("gx")
    layers, size_y = adjoint.shape[2], adjoint.shape[3]
    for side, out in enumerate((p_send, z_send)):
        layer, right = side_layer(side, even, layers - 1)
        for part in range(2):
            for comp in range(3):
                face[part, comp] = adjoint[part, comp, layer].astype(jnp.float32)
        write_faces(face, out, right, size_y)


def first_sweep_kernel(wave_ref, count_ref, cells_ref, start, sigma_h, sigma_v, e_out, src, field, twist):
    index, _ = position("gx")
    layers, size_y, size_z = sigma_h.shape
    wave = wave_ref[...]
    edge = jnp.where(index > 0, 1.0, 0.0)
    add_slots(wave, count_ref[...], cells_ref[...], index * (layers * size_y), src)

    def source(part, comp, layer, rows):
        return src[layer, rows] if part == 1 and comp == 0 else None

    zero_layer(field, layers, size_y)
    whole_sweep(start, field, twist, edge, wave, sigma_h, sigma_v, e_out, source)


def add_slots(wave, count, cells, first, src):
    layers, size_y, size_z = src.shape
    slots = cells.shape[1]
    shift = size_z.bit_length() - 1
    assert size_z == 1 << shift
    row = lax.shift_right_logical(cells, shift) - first
    spot = jnp.bitwise_and(cells, size_z - 1)
    live = lane_of((1, slots)) < count
    row = jnp.where(live, row, -1)
    at_row = lax.broadcasted_iota(jnp.int32, (layers * size_y, slots), 0) == row
    at_spot = lax.broadcasted_iota(jnp.int32, (size_z, slots), 0) == spot
    counts = lax.dot_general(
        jnp.where(at_row, 1.0, 0.0).astype(jnp.bfloat16),
        jnp.where(at_spot, 1.0, 0.0).astype(jnp.bfloat16),
        (((1,), (1,)), ((), ())),
        preferred_element_type=jnp.float32,
    )
    gain = SOURCE_GAIN * wave
    for layer in range(layers):
        src[layer] = gain * counts[layer * size_y : (layer + 1) * size_y]


def first_adjoint_kernel(wave_ref, adjoint, sigma_h, sigma_v, a_out, field, twist):
    index, _ = position("gx")
    layers, size_y, _ = sigma_h.shape
    edge = jnp.where(index > 0, 1.0, 0.0)
    zero_layer(field, layers, size_y)
    none = lambda part, comp, layer, rows: None
    whole_sweep(adjoint, field, twist, edge, wave_ref[...], sigma_h, sigma_v, a_out, none)


def whole_sweep(values, field, twist, edge, wave, sigma_h, sigma_v, out, source):
    layers, size_y, _ = sigma_h.shape
    widen(values, field, layers, size_y)
    twists(field, twist, edge, layers, size_y)

    def one(layer, carry):
        for y in range(0, size_y, ROWS):
            rows = slice(y, y + ROWS)
            at = lambda part, comp: source(part, comp, layer, rows)
            new = relaxed(field, twist, layer, y, size_y, wave, sigma_h[layer, rows], sigma_v[layer, rows], at)
            for part in range(2):
                for comp in range(3):
                    out[layer, part, comp, rows] = new[part][comp]
        return carry

    lax.fori_loop(0, layers, one, 0)


def second_faces_kernel(side, wave_ref, halo, part_new, sigma_h, sigma_v, face, send):
    _, even = position("gx")
    layers, size_y, _ = sigma_h.shape
    layer, right = side_layer(side, even, layers - 1)
    wave = wave_ref[...]
    for y in range(0, size_y, ROWS):
        rows = slice(y, y + ROWS)
        add = fix(halo, y, right, wave, sigma_h[layer, rows], sigma_v[layer, rows], size_y)
        for part in range(2):
            for comp in range(3):
                face[part, comp, rows] = part_new[layer, part, comp, rows] + add[part][comp]
    write_faces(face, send, right, size_y)


def gather_layers(body, face_p, face_z, field, even, layers):
    p_layer, _ = side_layer(0, even, layers - 1)
    z_layer, _ = side_layer(1, even, layers - 1)
    for part in range(2):
        for comp in range(3):
            for layer in range(1, layers - 1):
                field[layer, part, comp] = body[layer, part, comp]
            field[p_layer, part, comp] = face_p[part, comp]
            field[z_layer, part, comp] = face_z[part, comp]


def rhs_of(part, new, seen):
    return new - seen if part == 0 else seen - new


def second_sweep_kernel(
    wave_ref, e_body, e_p, e_z, a_part, src, observed, sigma_h, sigma_v, e_out, a_out, field, twist
):
    index, even = position("gx")
    layers, size_y, _ = sigma_h.shape
    wave = wave_ref[...]
    edge = jnp.where(index > 0, 1.0, 0.0)
    zero_layer(field, layers, size_y)
    gather_layers(e_body, e_p, e_z, field, even, layers)
    twists(field, twist, edge, layers, size_y)

    def one(layer, carry):
        for y in range(0, size_y, ROWS):
            rows = slice(y, y + ROWS)

            def source(part, comp):
                return src[layer, rows] if part == 1 and comp == 0 else None

            new = relaxed(field, twist, layer, y, size_y, wave, sigma_h[layer, rows], sigma_v[layer, rows], source)
            for part in range(2):
                for comp in range(3):
                    e_out[layer, part, comp, rows] = new[part][comp]
        return carry

    lax.fori_loop(0, layers, one, 0)

    def inner(layer, carry):
        add_rhs(layer, e_out, (layer,), a_part, observed, wave, sigma_h, sigma_v, a_out, (layer,), size_y, None)
        return carry

    lax.fori_loop(1, layers - 1, inner, 0)


def add_rhs(layer, new, at, a_part, observed, wave, sigma_h, sigma_v, a_out, out_at, size_y, extra):
    for y in range(0, size_y, ROWS):
        rows = slice(y, y + ROWS)
        sides = (factors(sigma_h[layer, rows], wave), factors(sigma_v[layer, rows], wave))
        add = extra(y) if extra is not None else None
        for comp in range(3):
            _, four, coup = sides[0] if comp < 2 else sides[1]
            br = rhs_of(0, new[at + (0, comp, rows)], observed[0, comp, layer, rows].astype(jnp.float32))
            bi = rhs_of(1, new[at + (1, comp, rows)], observed[1, comp, layer, rows].astype(jnp.float32))
            real = a_part[layer, 0, comp, rows] + (four * br + coup * bi)
            imag = a_part[layer, 1, comp, rows] + (four * bi - coup * br)
            if add is not None:
                real = real + add[0][comp]
                imag = imag + add[1][comp]
            a_out[out_at + (0, comp, rows)] = real
            a_out[out_at + (1, comp, rows)] = imag


def third_faces_kernel(
    side, wave_ref, e_halo, a_halo, e_part, a_part, observed, sigma_h, sigma_v, e_face, a_face, send
):
    _, even = position("gx")
    layers, size_y, _ = sigma_h.shape
    layer, right = side_layer(side, even, layers - 1)
    wave = wave_ref[...]
    for y in range(0, size_y, ROWS):
        rows = slice(y, y + ROWS)
        add = fix(e_halo, y, right, wave, sigma_h[layer, rows], sigma_v[layer, rows], size_y)
        for part in range(2):
            for comp in range(3):
                e_face[part, comp, rows] = e_part[layer, part, comp, rows] + add[part][comp]

    def extra(y):
        rows = slice(y, y + ROWS)
        return fix(a_halo, y, right, wave, sigma_h[layer, rows], sigma_v[layer, rows], size_y)

    add_rhs(layer, e_face, (), a_part, observed, wave, sigma_h, sigma_v, a_face, (), size_y, extra)
    write_faces(a_face, send, right, size_y)


def grad_rows(wave, field, adjoint):
    terms = [adjoint[0][comp] * field[1][comp] + adjoint[1][comp] * field[0][comp] for comp in range(3)]
    return wave * (terms[0] + terms[1]), wave * terms[2]


def put_rows(out, place, y, pair, share):
    for which in range(2):
        for k in range(ROWS // share):
            out[y // share + k, which, place] = pair[which][k * share : (k + 1) * share]


def last_sweep_kernel(
    wave_ref, e_body, e_p, e_z, a_body, a_p, a_z, observed, sigma_h, sigma_v, final, faces, grad, field, twist
):
    index, even = position("gx")
    layers, size_y, _ = sigma_h.shape
    share = grad.shape[3]
    wave = wave_ref[...]
    edge = jnp.where(index > 0, 1.0, 0.0)
    sides = [side_layer(side, even, layers - 1)[0] for side in range(2)]
    for part in range(2):
        for comp in range(3):
            for layer in range(1, layers - 1):
                final[part, comp, layer] = e_body[layer, part, comp]
            final[part, comp, sides[0]] = e_p[part, comp]
            final[part, comp, sides[1]] = e_z[part, comp]
    zero_layer(field, layers, size_y)
    gather_layers(a_body, a_p, a_z, field, even, layers)
    twists(field, twist, edge, layers, size_y)

    def sweep(layer, y):
        rows = slice(y, y + ROWS)
        now = [[final[part, comp, layer, rows] for comp in range(3)] for part in range(2)]

        def source(part, comp):
            return rhs_of(part, now[part][comp], observed[part, comp, layer, rows].astype(jnp.float32))

        return now, relaxed(field, twist, layer, y, size_y, wave, sigma_h[layer, rows], sigma_v[layer, rows], source)

    def inner(layer, carry):
        for y in range(0, size_y, ROWS):
            now, new = sweep(layer, y)
            put_rows(grad, layer - 1, y, grad_rows(wave, now, new), share)
        return carry

    lax.fori_loop(1, layers - 1, inner, 0)

    def outer(side, carry):
        layer = jnp.where(side == 0, sides[0], sides[1])
        for y in range(0, size_y, ROWS):
            _, new = sweep(layer, y)
            for part in range(2):
                for comp in range(3):
                    faces[side, part, comp, y : y + ROWS] = new[part][comp]
        return carry

    lax.fori_loop(0, 2, outer, 0)


def gradient_kernel(wave_ref, halo_p, halo_z, e_p, e_z, faces, inner, sigma_h, sigma_v, grad):
    _, even = position("gx")
    layers, size_y, _ = sigma_h.shape
    share = grad.shape[3]
    wave = wave_ref[...]
    for layer in range(1, layers - 1):
        for which in range(2):
            grad[:, which, layer] = inner[:, which, layer - 1]
    for side, (halo, now) in enumerate(((halo_p, e_p), (halo_z, e_z))):
        layer, right = side_layer(side, even, layers - 1)
        for y in range(0, size_y, ROWS):
            rows = slice(y, y + ROWS)
            add = fix(halo, y, right, wave, sigma_h[layer, rows], sigma_v[layer, rows], size_y)
            new = [[faces[side, part, comp, rows] + add[part][comp] for comp in range(3)] for part in range(2)]
            old = [[now[part, comp, rows] for comp in range(3)] for part in range(2)]
            put_rows(grad, layer, y, grad_rows(wave, old, new), share)


def call(kernel, name, specs, outs, scratch=()):
    return pl.pallas_call(
        kernel,
        name=name,
        out_shape=tuple(jax.ShapeDtypeStruct(shape, jnp.float32) for shape in outs),
        in_specs=specs,
        out_specs=tuple(VMEM for _ in outs),
        scratch_shapes=[s if not isinstance(s, tuple) else pltpu.VMEM(s, jnp.float32) for s in scratch],
        compiler_params=pltpu.CompilerParams(vmem_limit_bytes=24 << 20),
    )


def on_device(
    sigma_h, sigma_v, wave_scale, field_start, adjoint_start, observed, tx_count, tx_cells
):
    layers, size_y, size_z = sigma_h.shape
    slabs = lax.axis_size("gx")
    freqs = lax.axis_size("freq")
    share = size_y // freqs
    start = field_start[0]
    adjoint = adjoint_start[0]
    seen = observed[0]
    wave = wave_scale[None]

    ends = (
        [(i, i + 1) for i in range(0, slabs - 1, 2)],
        [(i, i + 1) for i in range(1, slabs - 1, 2)],
    )
    swaps = [pairs + [(b, a) for a, b in pairs] for pairs in ends]

    def swap(values, side):
        return lax.ppermute(values, "gx", swaps[side])

    plane = (size_y, size_z)
    half = (2, 2) + plane
    face = (2, 3) + plane
    body = (layers,) + face
    more = (layers + 1,) + face
    hbm = pl.BlockSpec(memory_space=pltpu.HBM)

    e_p, e_z = call(
        first_faces_kernel,
        "first_faces",
        [hbm],
        [half] * 2,
        [pltpu.VMEM((2,) + face, jnp.bfloat16), face, pltpu.SemaphoreType.DMA((2,))],
    )(start)
    e_p_in, e_z_in = swap(e_p, 0), swap(e_z, 1)
    a_p, a_z = call(adjoint_faces_kernel, "adjoint_faces", [VMEM], [half] * 2, [face])(adjoint)
    a_p_in, a_z_in = swap(a_p, 0), swap(a_z, 1)
    e1, src = call(
        first_sweep_kernel,
        "first_sweep",
        [VMEM] * 6,
        [body, (layers,) + plane],
        [more, more],
    )(wave, tx_count[None], tx_cells[None], start, sigma_h, sigma_v)
    (a1,) = call(
        first_adjoint_kernel, "first_adjoint", [VMEM] * 4, [body], [more, more]
    )(wave, adjoint, sigma_h, sigma_v)
    a1, e1, e_p_in = lax.optimization_barrier((a1, e1, e_p_in))

    def second(side, halo):
        return call(
            lambda *refs: second_faces_kernel(side, *refs),
            "second_faces_%d" % side,
            [VMEM] * 5,
            [face, half],
        )(wave, halo, e1, sigma_h, sigma_v)

    e1_p, e1_p_out = second(0, e_p_in)
    e1_p_in = swap(e1_p_out, 0)
    e1_z, e1_z_out = second(1, e_z_in)
    e1_z_in = swap(e1_z_out, 1)
    e1_z, a_z_in, a_p_in = lax.optimization_barrier((e1_z, a_z_in, a_p_in))
    e2, a1_body = call(
        second_sweep_kernel, "second_sweep", [VMEM] * 9, [body, body], [more, more]
    )(wave, e1, e1_p, e1_z, a1, src, seen, sigma_h, sigma_v)
    e2, e1_p_in = lax.optimization_barrier((e2, e1_p_in))

    def third(side, e_halo, a_halo):
        return call(
            lambda *refs: third_faces_kernel(side, *refs),
            "third_faces_%d" % side,
            [VMEM] * 8,
            [face, face, half],
        )(wave, e_halo, a_halo, e2, a1, seen, sigma_h, sigma_v)

    e2_p, a1_p, a1_p_out = third(0, e1_p_in, a_p_in)
    a1_p_in = swap(a1_p_out, 0)
    e2_z, a1_z, a1_z_out = third(1, e1_z_in, a_z_in)
    a1_z_in = swap(a1_z_out, 1)
    inner_blocks = (freqs, 2, layers - 2, share, size_z)
    blocks = (freqs, 2, layers, share, size_z)
    final, faces, inner = call(
        last_sweep_kernel,
        "last_sweep",
        [VMEM] * 10,
        [(2, 3, layers) + plane, (2,) + face, inner_blocks],
        [more, more],
    )(wave, e2, e2_p, e2_z, a1_body, a1_p, a1_z, seen, sigma_h, sigma_v)
    faces, a1_p_in = lax.optimization_barrier((faces, a1_p_in))
    (terms,) = call(gradient_kernel, "gradient", [VMEM] * 9, [blocks])(
        wave, a1_p_in, a1_z_in, e2_p, e2_z, faces, inner, sigma_h, sigma_v
    )
    gathered = lax.all_to_all(terms, "freq", 0, 0)
    return (jnp.sum(gathered, axis=0), final[None])


def solution(mesh):
    placed = (
        P("gx", None, None),
        P("gx", None, None),
        P("freq"),
        P("freq", None, None, "gx", None, None),
        P("freq", None, None, "gx", None, None),
        P("freq", None, None, "gx", None, None),
        P(),
        P(),
    )
    return jax.shard_map(
        on_device,
        mesh=mesh,
        in_specs=placed,
        out_specs=(P(None, "gx", "freq", None), P("freq", None, None, "gx", None, None)),
        check_vma=False,
    )
```

```python
import jax
import jax.numpy as jnp
from jax import lax
from jax.experimental import pallas as pl
from jax.experimental.pallas import tpu as pltpu
from jax.sharding import PartitionSpec as P

ITERS = 2
THETA = 0.5
SOURCE_GAIN = 8.0
ROWS = 8

VMEM = pl.BlockSpec(memory_space=pltpu.VMEM)


def position(axis):
    index = lax.axis_index(axis)
    even = 1 - lax.rem(index, 2)
    return index, even


def side_layer(side, even, last):
    right = even if side == 0 else 1 - even
    return last * right, right.astype(jnp.float32)


def lane_of(shape):
    return lax.broadcasted_iota(jnp.int32, shape, len(shape) - 1)


def next_z(values):
    size = values.shape[-1]
    moved = pltpu.roll(values, size - 1, 1)
    return jnp.where(lane_of(values.shape) == size - 1, 0.0, moved)


def last_z(values):
    moved = pltpu.roll(values, 1, 1)
    return jnp.where(lane_of(values.shape) == 0, 0.0, moved)


def factors(sigma, wave):
    coupling = wave * sigma
    inverse = THETA / (16.0 + coupling * coupling)
    return coupling, 4.0 * inverse, coupling * inverse


def chunks(size_y):
    return [slice(y, y + ROWS) for y in range(0, size_y, ROWS)]


def behind_row(ref, index, y, size_y):
    now = ref[index + (slice(y, y + ROWS),)]
    if y == 0:
        row = lax.broadcasted_iota(jnp.int32, now.shape, 0)
        return now, jnp.where(row == 0, 0.0, pltpu.roll(now, 1, 0))
    return now, ref[index + (slice(y - 1, y - 1 + ROWS),)]


def ahead_row(ref, index, y, size_y):
    now = ref[index + (slice(y, y + ROWS),)]
    if y + ROWS == size_y:
        row = lax.broadcasted_iota(jnp.int32, now.shape, 0)
        return now, jnp.where(row == ROWS - 1, 0.0, pltpu.roll(now, ROWS - 1, 0))
    return now, ref[index + (slice(y + 1, y + 1 + ROWS),)]


def write_faces(face, out, right, size_y):
    for part in range(2):
        for y in range(0, size_y, ROWS):
            rows = slice(y, y + ROWS)
            ex, ex_next = ahead_row(face, (part, 0), y, size_y)
            out[part, 0, rows] = face[part, 1, rows] + right * (ex_next - ex)
            out[part, 1, rows] = face[part, 2, rows] + right * (next_z(ex) - ex)


def fix(halo, y, right, wave, sig_h, sig_v, size_y):
    _, h_four, h_coup = factors(sig_h, wave)
    _, v_four, v_coup = factors(sig_v, wave)
    extra = []
    for part in range(2):
        u, u_last = behind_row(halo, (part, 0), y, size_y)
        v = halo[part, 1, y : y + ROWS]
        extra.append((right * ((last_z(v) - v) - (u - u_last)), u, v))
    real, imag = [], []
    for comp in range(3):
        four, coup = (h_four, h_coup) if comp < 2 else (v_four, v_coup)
        real.append(four * extra[0][comp] + coup * extra[1][comp])
        imag.append(four * extra[1][comp] - coup * extra[0][comp])
    return real, imag


def twists(field, twist, edge, layers, size_y):
    def one(layer, carry):
        for part in range(2):
            for y in range(0, size_y, ROWS):
                rows = slice(y, y + ROWS)
                ex, ex_next = ahead_row(field, (layer, part, 0), y, size_y)
                ey = field[layer, part, 1, rows]
                ez, ez_next = ahead_row(field, (layer, part, 2), y, size_y)
                ey_right = field[layer + 1, part, 1, rows]
                ez_right = field[layer + 1, part, 2, rows]
                twist[layer + 1, part, 0, rows] = (ez_next - ez) - (next_z(ey) - ey)
                twist[layer + 1, part, 1, rows] = (next_z(ex) - ex) - (ez_right - ez)
                twist[layer + 1, part, 2, rows] = (ey_right - ey) - (ex_next - ex)
        return carry

    lax.fori_loop(0, layers, one, 0)
    for part in range(2):
        for rows in chunks(size_y):
            twist[0, part, 1, rows] = -edge * field[0, part, 2, rows]
            twist[0, part, 2, rows] = edge * field[0, part, 1, rows]


def curled(twist, layer, y, size_y):
    rows = slice(y, y + ROWS)
    result = []
    for part in range(2):
        hx, hx_last = behind_row(twist, (layer + 1, part, 0), y, size_y)
        hz, hz_last = behind_row(twist, (layer + 1, part, 2), y, size_y)
        hy = twist[layer + 1, part, 1, rows]
        hy_left = twist[layer, part, 1, rows]
        hz_left = twist[layer, part, 2, rows]
        result.append(
            (
                (hz - hz_last) - (hy - last_z(hy)),
                (hx - last_z(hx)) - (hz - hz_left),
                (hy - hy_left) - (hx - hx_last),
            )
        )
    return result


def relaxed(field, twist, layer, y, size_y, wave, sig_h, sig_v, source):
    rows = slice(y, y + ROWS)
    sides = (factors(sig_h, wave), factors(sig_v, wave))
    curl = curled(twist, layer, y, size_y)
    real, imag = [], []
    for comp in range(3):
        coupling, four, coup = sides[0] if comp < 2 else sides[1]
        er = field[layer, 0, comp, rows]
        ei = field[layer, 1, comp, rows]
        rr = coupling * ei - curl[0][comp]
        ri = -(coupling * er) - curl[1][comp]
        br, bi = source(0, comp), source(1, comp)
        if br is not None:
            rr = rr + br
        if bi is not None:
            ri = ri + bi
        real.append(er + (four * rr + coup * ri))
        imag.append(ei + (four * ri - coup * rr))
    return real, imag


def zero_layer(field, layer, size_y):
    for part in range(2):
        for comp in (1, 2):
            for rows in chunks(size_y):
                field[layer, part, comp, rows] = jnp.zeros((ROWS, field.shape[-1]), jnp.float32)


def widen(start, field, layers, size_y):
    for layer in range(layers):
        for part in range(2):
            for comp in range(3):
                field[layer, part, comp] = start[part, comp, layer].astype(jnp.float32)


def first_faces_kernel(start, p_send, z_send, got, face, sems):
    _, even = position("gx")
    layers, size_y = start.shape[2], start.shape[3]
    sides = [side_layer(side, even, layers - 1) for side in range(2)]
    copies = [
        pltpu.make_async_copy(start.at[:, :, sides[side][0]], got.at[side], sems.at[side]) for side in range(2)
    ]
    for copy in copies[::-1]:
        copy.start()
    for side, out in ((1, z_send), (0, p_send)):
        copies[side].wait()
        for part in range(2):
            for comp in range(3):
                face[part, comp] = got[side, part, comp].astype(jnp.float32)
        write_faces(face, out, sides[side][1], size_y)


def adjoint_faces_kernel(adjoint, p_send, z_send, face):
    _, even = position("gx")
    layers, size_y = adjoint.shape[2], adjoint.shape[3]
    for side, out in enumerate((p_send, z_send)):
        layer, right = side_layer(side, even, layers - 1)
        for part in range(2):
            for comp in range(3):
                face[part, comp] = adjoint[part, comp, layer].astype(jnp.float32)
        write_faces(face, out, right, size_y)


def first_sweep_kernel(wave_ref, count_ref, cells_ref, start, sigma_h, sigma_v, e_out, src, field, twist):
    index, _ = position("gx")
    layers, size_y, size_z = sigma_h.shape
    wave = wave_ref[...]
    edge = jnp.where(index > 0, 1.0, 0.0)
    add_slots(wave, count_ref[...], cells_ref[...], index * (layers * size_y), src)

    def source(part, comp, layer, rows):
        return src[layer, rows] if part == 1 and comp == 0 else None

    zero_layer(field, layers, size_y)
    whole_sweep(start, field, twist, edge, wave, sigma_h, sigma_v, e_out, source)


def add_slots(wave, count, cells, first, src):
    layers, size_y, size_z = src.shape
    slots = cells.shape[1]
    shift = size_z.bit_length() - 1
    assert size_z == 1 << shift
    row = lax.shift_right_logical(cells, shift) - first
    spot = jnp.bitwise_and(cells, size_z - 1)
    live = lane_of((1, slots)) < count
    row = jnp.where(live, row, -1)
    at_row = lax.broadcasted_iota(jnp.int32, (layers * size_y, slots), 0) == row
    at_spot = lax.broadcasted_iota(jnp.int32, (size_z, slots), 0) == spot
    counts = lax.dot_general(
        jnp.where(at_row, 1.0, 0.0).astype(jnp.bfloat16),
        jnp.where(at_spot, 1.0, 0.0).astype(jnp.bfloat16),
        (((1,), (1,)), ((), ())),
        preferred_element_type=jnp.float32,
    )
    gain = SOURCE_GAIN * wave
    for layer in range(layers):
        src[layer] = gain * counts[layer * size_y : (layer + 1) * size_y]


def first_adjoint_kernel(wave_ref, adjoint, sigma_h, sigma_v, a_out, field, twist):
    index, _ = position("gx")
    layers, size_y, _ = sigma_h.shape
    edge = jnp.where(index > 0, 1.0, 0.0)
    zero_layer(field, layers, size_y)
    none = lambda part, comp, layer, rows: None
    whole_sweep(adjoint, field, twist, edge, wave_ref[...], sigma_h, sigma_v, a_out, none)


def whole_sweep(values, field, twist, edge, wave, sigma_h, sigma_v, out, source):
    layers, size_y, _ = sigma_h.shape
    widen(values, field, layers, size_y)
    twists(field, twist, edge, layers, size_y)

    def one(layer, carry):
        for y in range(0, size_y, ROWS):
            rows = slice(y, y + ROWS)
            at = lambda part, comp: source(part, comp, layer, rows)
            new = relaxed(field, twist, layer, y, size_y, wave, sigma_h[layer, rows], sigma_v[layer, rows], at)
            for part in range(2):
                for comp in range(3):
                    out[layer, part, comp, rows] = new[part][comp]
        return carry

    lax.fori_loop(0, layers, one, 0)


def second_faces_kernel(side, wave_ref, halo, part_new, sigma_h, sigma_v, face, send):
    _, even = position("gx")
    layers, size_y, _ = sigma_h.shape
    layer, right = side_layer(side, even, layers - 1)
    wave = wave_ref[...]
    for y in range(0, size_y, ROWS):
        rows = slice(y, y + ROWS)
        add = fix(halo, y, right, wave, sigma_h[layer, rows], sigma_v[layer, rows], size_y)
        for part in range(2):
            for comp in range(3):
                face[part, comp, rows] = part_new[layer, part, comp, rows] + add[part][comp]
    write_faces(face, send, right, size_y)


def gather_layers(body, face_p, face_z, field, even, layers):
    p_layer, _ = side_layer(0, even, layers - 1)
    z_layer, _ = side_layer(1, even, layers - 1)
    for part in range(2):
        for comp in range(3):
            for layer in range(1, layers - 1):
                field[layer, part, comp] = body[layer, part, comp]
            field[p_layer, part, comp] = face_p[part, comp]
            field[z_layer, part, comp] = face_z[part, comp]


def rhs_of(part, new, seen):
    return new - seen if part == 0 else seen - new


def second_sweep_kernel(
    wave_ref, e_body, e_p, e_z, a_part, src, observed, sigma_h, sigma_v, e_out, a_out, field, twist
):
    index, even = position("gx")
    layers, size_y, _ = sigma_h.shape
    wave = wave_ref[...]
    edge = jnp.where(index > 0, 1.0, 0.0)
    zero_layer(field, layers, size_y)
    gather_layers(e_body, e_p, e_z, field, even, layers)
    twists(field, twist, edge, layers, size_y)

    def one(layer, carry):
        for y in range(0, size_y, ROWS):
            rows = slice(y, y + ROWS)

            def source(part, comp):
                return src[layer, rows] if part == 1 and comp == 0 else None

            new = relaxed(field, twist, layer, y, size_y, wave, sigma_h[layer, rows], sigma_v[layer, rows], source)
            for part in range(2):
                for comp in range(3):
                    e_out[layer, part, comp, rows] = new[part][comp]
        return carry

    lax.fori_loop(0, layers, one, 0)

    def inner(layer, carry):
        add_rhs(layer, e_out, (layer,), a_part, observed, wave, sigma_h, sigma_v, a_out, (layer,), size_y, None)
        return carry

    lax.fori_loop(1, layers - 1, inner, 0)


def add_rhs(layer, new, at, a_part, observed, wave, sigma_h, sigma_v, a_out, out_at, size_y, extra):
    for y in range(0, size_y, ROWS):
        rows = slice(y, y + ROWS)
        sides = (factors(sigma_h[layer, rows], wave), factors(sigma_v[layer, rows], wave))
        add = extra(y) if extra is not None else None
        for comp in range(3):
            _, four, coup = sides[0] if comp < 2 else sides[1]
            br = rhs_of(0, new[at + (0, comp, rows)], observed[0, comp, layer, rows].astype(jnp.float32))
            bi = rhs_of(1, new[at + (1, comp, rows)], observed[1, comp, layer, rows].astype(jnp.float32))
            real = a_part[layer, 0, comp, rows] + (four * br + coup * bi)
            imag = a_part[layer, 1, comp, rows] + (four * bi - coup * br)
            if add is not None:
                real = real + add[0][comp]
                imag = imag + add[1][comp]
            a_out[out_at + (0, comp, rows)] = real
            a_out[out_at + (1, comp, rows)] = imag


def third_faces_kernel(
    side, wave_ref, e_halo, a_halo, e_part, a_part, observed, sigma_h, sigma_v, e_face, a_face, send
):
    _, even = position("gx")
    layers, size_y, _ = sigma_h.shape
    layer, right = side_layer(side, even, layers - 1)
    wave = wave_ref[...]
    for y in range(0, size_y, ROWS):
        rows = slice(y, y + ROWS)
        add = fix(e_halo, y, right, wave, sigma_h[layer, rows], sigma_v[layer, rows], size_y)
        for part in range(2):
            for comp in range(3):
                e_face[part, comp, rows] = e_part[layer, part, comp, rows] + add[part][comp]

    def extra(y):
        rows = slice(y, y + ROWS)
        return fix(a_halo, y, right, wave, sigma_h[layer, rows], sigma_v[layer, rows], size_y)

    add_rhs(layer, e_face, (), a_part, observed, wave, sigma_h, sigma_v, a_face, (), size_y, extra)
    write_faces(a_face, send, right, size_y)


def grad_rows(wave, field, adjoint):
    terms = [adjoint[0][comp] * field[1][comp] + adjoint[1][comp] * field[0][comp] for comp in range(3)]
    return wave * (terms[0] + terms[1]), wave * terms[2]


def put_rows(out, place, y, pair, share):
    for which in range(2):
        for k in range(ROWS // share):
            out[y // share + k, which, place] = pair[which][k * share : (k + 1) * share]


def last_sweep_kernel(
    wave_ref, e_body, e_p, e_z, a_body, a_p, a_z, observed, sigma_h, sigma_v, final, faces, grad, field, twist
):
    index, even = position("gx")
    layers, size_y, _ = sigma_h.shape
    share = grad.shape[3]
    wave = wave_ref[...]
    edge = jnp.where(index > 0, 1.0, 0.0)
    sides = [side_layer(side, even, layers - 1)[0] for side in range(2)]
    for part in range(2):
        for comp in range(3):
            for layer in range(1, layers - 1):
                final[part, comp, layer] = e_body[layer, part, comp]
            final[part, comp, sides[0]] = e_p[part, comp]
            final[part, comp, sides[1]] = e_z[part, comp]
    zero_layer(field, layers, size_y)
    gather_layers(a_body, a_p, a_z, field, even, layers)
    twists(field, twist, edge, layers, size_y)

    def sweep(layer, y):
        rows = slice(y, y + ROWS)
        now = [[final[part, comp, layer, rows] for comp in range(3)] for part in range(2)]

        def source(part, comp):
            return rhs_of(part, now[part][comp], observed[part, comp, layer, rows].astype(jnp.float32))

        return now, relaxed(field, twist, layer, y, size_y, wave, sigma_h[layer, rows], sigma_v[layer, rows], source)

    def inner(layer, carry):
        for y in range(0, size_y, ROWS):
            now, new = sweep(layer, y)
            put_rows(grad, layer - 1, y, grad_rows(wave, now, new), share)
        return carry

    lax.fori_loop(1, layers - 1, inner, 0)

    def outer(side, carry):
        layer = jnp.where(side == 0, sides[0], sides[1])
        for y in range(0, size_y, ROWS):
            _, new = sweep(layer, y)
            for part in range(2):
                for comp in range(3):
                    faces[side, part, comp, y : y + ROWS] = new[part][comp]
        return carry

    lax.fori_loop(0, 2, outer, 0)


def gradient_kernel(wave_ref, halo_p, halo_z, e_p, e_z, faces, inner, sigma_h, sigma_v, grad):
    _, even = position("gx")
    layers, size_y, _ = sigma_h.shape
    share = grad.shape[3]
    wave = wave_ref[...]
    for layer in range(1, layers - 1):
        for which in range(2):
            grad[:, which, layer] = inner[:, which, layer - 1]
    for side, (halo, now) in enumerate(((halo_p, e_p), (halo_z, e_z))):
        layer, right = side_layer(side, even, layers - 1)
        for y in range(0, size_y, ROWS):
            rows = slice(y, y + ROWS)
            add = fix(halo, y, right, wave, sigma_h[layer, rows], sigma_v[layer, rows], size_y)
            new = [[faces[side, part, comp, rows] + add[part][comp] for comp in range(3)] for part in range(2)]
            old = [[now[part, comp, rows] for comp in range(3)] for part in range(2)]
            put_rows(grad, layer, y, grad_rows(wave, old, new), share)


def call(kernel, name, specs, outs, scratch=()):
    return pl.pallas_call(
        kernel,
        name=name,
        out_shape=tuple(jax.ShapeDtypeStruct(shape, jnp.float32) for shape in outs),
        in_specs=specs,
        out_specs=tuple(VMEM for _ in outs),
        scratch_shapes=[s if not isinstance(s, tuple) else pltpu.VMEM(s, jnp.float32) for s in scratch],
        compiler_params=pltpu.CompilerParams(vmem_limit_bytes=24 << 20),
    )


def on_device(
    sigma_h, sigma_v, wave_scale, field_start, adjoint_start, observed, tx_count, tx_cells
):
    layers, size_y, size_z = sigma_h.shape
    slabs = lax.axis_size("gx")
    freqs = lax.axis_size("freq")
    share = size_y // freqs
    start = field_start[0]
    adjoint = adjoint_start[0]
    seen = observed[0]
    wave = wave_scale[None]

    ends = (
        [(i, i + 1) for i in range(0, slabs - 1, 2)],
        [(i, i + 1) for i in range(1, slabs - 1, 2)],
    )
    swaps = [pairs + [(b, a) for a, b in pairs] for pairs in ends]

    def swap(values, side):
        return lax.ppermute(values, "gx", swaps[side])

    plane = (size_y, size_z)
    half = (2, 2) + plane
    face = (2, 3) + plane
    body = (layers,) + face
    more = (layers + 1,) + face
    hbm = pl.BlockSpec(memory_space=pltpu.HBM)

    e_p, e_z = call(
        first_faces_kernel,
        "first_faces",
        [hbm],
        [half] * 2,
        [pltpu.VMEM((2,) + face, jnp.bfloat16), face, pltpu.SemaphoreType.DMA((2,))],
    )(start)
    e_z_in, e_p_in = swap(e_z, 1), swap(e_p, 0)
    a_p, a_z = call(adjoint_faces_kernel, "adjoint_faces", [VMEM], [half] * 2, [face])(adjoint)
    a_z_in = swap(a_z, 1)
    e1, src = call(
        first_sweep_kernel,
        "first_sweep",
        [VMEM] * 6,
        [body, (layers,) + plane],
        [more, more],
    )(wave, tx_count[None], tx_cells[None], start, sigma_h, sigma_v)
    (a1,) = call(
        first_adjoint_kernel, "first_adjoint", [VMEM] * 4, [body], [more, more]
    )(wave, adjoint, sigma_h, sigma_v)
    a1, e1, e_z_in = lax.optimization_barrier((a1, e1, e_z_in))

    def second(side, halo):
        return call(
            lambda *refs: second_faces_kernel(side, *refs),
            "second_faces_%d" % side,
            [VMEM] * 5,
            [face, half],
        )(wave, halo, e1, sigma_h, sigma_v)

    e1_z, e1_z_out = second(1, e_z_in)
    e1_z_in = swap(e1_z_out, 1)
    e1_p, e1_p_out = second(0, e_p_in)
    e1_p_in = swap(e1_p_out, 0)
    e1_p, a_z_in = lax.optimization_barrier((e1_p, a_z_in))
    e2, a1_body = call(
        second_sweep_kernel, "second_sweep", [VMEM] * 9, [body, body], [more, more]
    )(wave, e1, e1_p, e1_z, a1, src, seen, sigma_h, sigma_v)
    e2, a_p = lax.optimization_barrier((e2, a_p))
    a_p_in = swap(a_p, 0)
    e2, e1_z_in = lax.optimization_barrier((e2, e1_z_in))

    def third(side, e_halo, a_halo):
        return call(
            lambda *refs: third_faces_kernel(side, *refs),
            "third_faces_%d" % side,
            [VMEM] * 8,
            [face, face, half],
        )(wave, e_halo, a_halo, e2, a1, seen, sigma_h, sigma_v)

    e2_z, a1_z, a1_z_out = third(1, e1_z_in, a_z_in)
    a1_z_in = swap(a1_z_out, 1)
    e2_p, a1_p, a1_p_out = third(0, e1_p_in, a_p_in)
    a1_p_in = swap(a1_p_out, 0)
    inner_blocks = (freqs, 2, layers - 2, share, size_z)
    blocks = (freqs, 2, layers, share, size_z)
    final, faces, inner = call(
        last_sweep_kernel,
        "last_sweep",
        [VMEM] * 10,
        [(2, 3, layers) + plane, (2,) + face, inner_blocks],
        [more, more],
    )(wave, e2, e2_p, e2_z, a1_body, a1_p, a1_z, seen, sigma_h, sigma_v)
    faces, a1_z_in = lax.optimization_barrier((faces, a1_z_in))
    (terms,) = call(gradient_kernel, "gradient", [VMEM] * 9, [blocks])(
        wave, a1_p_in, a1_z_in, e2_p, e2_z, faces, inner, sigma_h, sigma_v
    )
    gathered = lax.all_to_all(terms, "freq", 0, 0)
    return (jnp.sum(gathered, axis=0), final[None])


def solution(mesh):
    placed = (
        P("gx", None, None),
        P("gx", None, None),
        P("freq"),
        P("freq", None, None, "gx", None, None),
        P("freq", None, None, "gx", None, None),
        P("freq", None, None, "gx", None, None),
        P(),
        P(),
    )
    return jax.shard_map(
        on_device,
        mesh=mesh,
        in_specs=placed,
        out_specs=(P(None, "gx", "freq", None), P("freq", None, None, "gx", None, None)),
        check_vma=False,
    )
```

```python
import jax
import jax.numpy as jnp
from jax import lax
from jax.experimental import pallas as pl
from jax.experimental.pallas import tpu as pltpu
from jax.sharding import PartitionSpec as P

ITERS = 2
THETA = 0.5
SOURCE_GAIN = 8.0
ROWS = 8

VMEM = pl.BlockSpec(memory_space=pltpu.VMEM)


def position(axis):
    index = lax.axis_index(axis)
    even = 1 - lax.rem(index, 2)
    return index, even


def side_layer(side, even, last):
    right = even if side == 0 else 1 - even
    return last * right, right.astype(jnp.float32)


def lane_of(shape):
    return lax.broadcasted_iota(jnp.int32, shape, len(shape) - 1)


def next_z(values):
    size = values.shape[-1]
    moved = pltpu.roll(values, size - 1, 1)
    return jnp.where(lane_of(values.shape) == size - 1, 0.0, moved)


def last_z(values):
    moved = pltpu.roll(values, 1, 1)
    return jnp.where(lane_of(values.shape) == 0, 0.0, moved)


def factors(sigma, wave):
    coupling = wave * sigma
    inverse = THETA / (16.0 + coupling * coupling)
    return coupling, 4.0 * inverse, coupling * inverse


def chunks(size_y):
    return [slice(y, y + ROWS) for y in range(0, size_y, ROWS)]


def behind_row(ref, index, y, size_y):
    now = ref[index + (slice(y, y + ROWS),)]
    if y == 0:
        row = lax.broadcasted_iota(jnp.int32, now.shape, 0)
        return now, jnp.where(row == 0, 0.0, pltpu.roll(now, 1, 0))
    return now, ref[index + (slice(y - 1, y - 1 + ROWS),)]


def ahead_row(ref, index, y, size_y):
    now = ref[index + (slice(y, y + ROWS),)]
    if y + ROWS == size_y:
        row = lax.broadcasted_iota(jnp.int32, now.shape, 0)
        return now, jnp.where(row == ROWS - 1, 0.0, pltpu.roll(now, ROWS - 1, 0))
    return now, ref[index + (slice(y + 1, y + 1 + ROWS),)]


def write_faces(face, out, right, size_y):
    for part in range(2):
        for y in range(0, size_y, ROWS):
            rows = slice(y, y + ROWS)
            ex, ex_next = ahead_row(face, (part, 0), y, size_y)
            out[part, 0, rows] = face[part, 1, rows] + right * (ex_next - ex)
            out[part, 1, rows] = face[part, 2, rows] + right * (next_z(ex) - ex)


def fix(halo, y, right, wave, sig_h, sig_v, size_y):
    _, h_four, h_coup = factors(sig_h, wave)
    _, v_four, v_coup = factors(sig_v, wave)
    extra = []
    for part in range(2):
        u, u_last = behind_row(halo, (part, 0), y, size_y)
        v = halo[part, 1, y : y + ROWS]
        extra.append((right * ((last_z(v) - v) - (u - u_last)), u, v))
    real, imag = [], []
    for comp in range(3):
        four, coup = (h_four, h_coup) if comp < 2 else (v_four, v_coup)
        real.append(four * extra[0][comp] + coup * extra[1][comp])
        imag.append(four * extra[1][comp] - coup * extra[0][comp])
    return real, imag


def twists(field, twist, edge, layers, size_y):
    def one(layer, carry):
        for part in range(2):
            for y in range(0, size_y, ROWS):
                rows = slice(y, y + ROWS)
                ex, ex_next = ahead_row(field, (layer, part, 0), y, size_y)
                ey = field[layer, part, 1, rows]
                ez, ez_next = ahead_row(field, (layer, part, 2), y, size_y)
                ey_right = field[layer + 1, part, 1, rows]
                ez_right = field[layer + 1, part, 2, rows]
                twist[layer + 1, part, 0, rows] = (ez_next - ez) - (next_z(ey) - ey)
                twist[layer + 1, part, 1, rows] = (next_z(ex) - ex) - (ez_right - ez)
                twist[layer + 1, part, 2, rows] = (ey_right - ey) - (ex_next - ex)
        return carry

    lax.fori_loop(0, layers, one, 0)
    for part in range(2):
        for rows in chunks(size_y):
            twist[0, part, 1, rows] = -edge * field[0, part, 2, rows]
            twist[0, part, 2, rows] = edge * field[0, part, 1, rows]


def curled(twist, layer, y, size_y):
    rows = slice(y, y + ROWS)
    result = []
    for part in range(2):
        hx, hx_last = behind_row(twist, (layer + 1, part, 0), y, size_y)
        hz, hz_last = behind_row(twist, (layer + 1, part, 2), y, size_y)
        hy = twist[layer + 1, part, 1, rows]
        hy_left = twist[layer, part, 1, rows]
        hz_left = twist[layer, part, 2, rows]
        result.append(
            (
                (hz - hz_last) - (hy - last_z(hy)),
                (hx - last_z(hx)) - (hz - hz_left),
                (hy - hy_left) - (hx - hx_last),
            )
        )
    return result


def relaxed(field, twist, layer, y, size_y, wave, sig_h, sig_v, source):
    rows = slice(y, y + ROWS)
    sides = (factors(sig_h, wave), factors(sig_v, wave))
    curl = curled(twist, layer, y, size_y)
    real, imag = [], []
    for comp in range(3):
        coupling, four, coup = sides[0] if comp < 2 else sides[1]
        er = field[layer, 0, comp, rows]
        ei = field[layer, 1, comp, rows]
        rr = coupling * ei - curl[0][comp]
        ri = -(coupling * er) - curl[1][comp]
        br, bi = source(0, comp), source(1, comp)
        if br is not None:
            rr = rr + br
        if bi is not None:
            ri = ri + bi
        real.append(er + (four * rr + coup * ri))
        imag.append(ei + (four * ri - coup * rr))
    return real, imag


def zero_layer(field, layer, size_y):
    for part in range(2):
        for comp in (1, 2):
            for rows in chunks(size_y):
                field[layer, part, comp, rows] = jnp.zeros((ROWS, field.shape[-1]), jnp.float32)


def widen(start, field, layers, size_y):
    for layer in range(layers):
        for part in range(2):
            for comp in range(3):
                field[layer, part, comp] = start[part, comp, layer].astype(jnp.float32)


def first_faces_kernel(start, p_send, got, face, sem):
    _, even = position("gx")
    layers, size_y = start.shape[2], start.shape[3]
    layer, right = side_layer(0, even, layers - 1)
    copy = pltpu.make_async_copy(start.at[:, :, layer], got, sem)
    copy.start()
    copy.wait()
    for part in range(2):
        for comp in range(3):
            face[part, comp] = got[part, comp].astype(jnp.float32)
    write_faces(face, p_send, right, size_y)


def faces_of(values, side, even, face, out):
    layers, size_y = values.shape[2], values.shape[3]
    layer, right = side_layer(side, even, layers - 1)
    for part in range(2):
        for comp in range(3):
            face[part, comp] = values[part, comp, layer].astype(jnp.float32)
    write_faces(face, out, right, size_y)


def first_sweep_kernel(
    wave_ref, count_ref, cells_ref, start, sigma_h, sigma_v, e_out, src, z_send, field, twist, face
):
    index, even = position("gx")
    faces_of(start, 1, even, face, z_send)
    layers, size_y, size_z = sigma_h.shape
    wave = wave_ref[...]
    edge = jnp.where(index > 0, 1.0, 0.0)
    add_slots(wave, count_ref[...], cells_ref[...], index * (layers * size_y), src)

    def source(part, comp, layer, rows):
        return src[layer, rows] if part == 1 and comp == 0 else None

    zero_layer(field, layers, size_y)
    whole_sweep(start, field, twist, edge, wave, sigma_h, sigma_v, e_out, source)


def add_slots(wave, count, cells, first, src):
    layers, size_y, size_z = src.shape
    slots = cells.shape[1]
    shift = size_z.bit_length() - 1
    assert size_z == 1 << shift
    row = lax.shift_right_logical(cells, shift) - first
    spot = jnp.bitwise_and(cells, size_z - 1)
    live = lane_of((1, slots)) < count
    row = jnp.where(live, row, -1)
    at_row = lax.broadcasted_iota(jnp.int32, (layers * size_y, slots), 0) == row
    at_spot = lax.broadcasted_iota(jnp.int32, (size_z, slots), 0) == spot
    counts = lax.dot_general(
        jnp.where(at_row, 1.0, 0.0).astype(jnp.bfloat16),
        jnp.where(at_spot, 1.0, 0.0).astype(jnp.bfloat16),
        (((1,), (1,)), ((), ())),
        preferred_element_type=jnp.float32,
    )
    gain = SOURCE_GAIN * wave
    for layer in range(layers):
        src[layer] = gain * counts[layer * size_y : (layer + 1) * size_y]


def first_adjoint_kernel(wave_ref, adjoint, sigma_h, sigma_v, a_out, p_send, z_send, field, twist, face):
    index, even = position("gx")
    faces_of(adjoint, 0, even, face, p_send)
    faces_of(adjoint, 1, even, face, z_send)
    layers, size_y, _ = sigma_h.shape
    edge = jnp.where(index > 0, 1.0, 0.0)
    zero_layer(field, layers, size_y)
    none = lambda part, comp, layer, rows: None
    whole_sweep(adjoint, field, twist, edge, wave_ref[...], sigma_h, sigma_v, a_out, none)


def whole_sweep(values, field, twist, edge, wave, sigma_h, sigma_v, out, source):
    layers, size_y, _ = sigma_h.shape
    widen(values, field, layers, size_y)
    twists(field, twist, edge, layers, size_y)

    def one(layer, carry):
        for y in range(0, size_y, ROWS):
            rows = slice(y, y + ROWS)
            at = lambda part, comp: source(part, comp, layer, rows)
            new = relaxed(field, twist, layer, y, size_y, wave, sigma_h[layer, rows], sigma_v[layer, rows], at)
            for part in range(2):
                for comp in range(3):
                    out[layer, part, comp, rows] = new[part][comp]
        return carry

    lax.fori_loop(0, layers, one, 0)


def second_faces_kernel(side, wave_ref, halo, part_new, sigma_h, sigma_v, face, send):
    _, even = position("gx")
    layers, size_y, _ = sigma_h.shape
    layer, right = side_layer(side, even, layers - 1)
    wave = wave_ref[...]
    for y in range(0, size_y, ROWS):
        rows = slice(y, y + ROWS)
        add = fix(halo, y, right, wave, sigma_h[layer, rows], sigma_v[layer, rows], size_y)
        for part in range(2):
            for comp in range(3):
                face[part, comp, rows] = part_new[layer, part, comp, rows] + add[part][comp]
    write_faces(face, send, right, size_y)


def gather_layers(body, face_p, face_z, field, even, layers):
    p_layer, _ = side_layer(0, even, layers - 1)
    z_layer, _ = side_layer(1, even, layers - 1)
    for part in range(2):
        for comp in range(3):
            for layer in range(1, layers - 1):
                field[layer, part, comp] = body[layer, part, comp]
            field[p_layer, part, comp] = face_p[part, comp]
            field[z_layer, part, comp] = face_z[part, comp]


def rhs_of(part, new, seen):
    return new - seen if part == 0 else seen - new


def second_sweep_kernel(
    wave_ref, e_body, e_p, e_z, a_part, src, observed, sigma_h, sigma_v, e_out, a_out, field, twist
):
    index, even = position("gx")
    layers, size_y, _ = sigma_h.shape
    wave = wave_ref[...]
    edge = jnp.where(index > 0, 1.0, 0.0)
    zero_layer(field, layers, size_y)
    gather_layers(e_body, e_p, e_z, field, even, layers)
    twists(field, twist, edge, layers, size_y)

    def one(layer, carry):
        for y in range(0, size_y, ROWS):
            rows = slice(y, y + ROWS)

            def source(part, comp):
                return src[layer, rows] if part == 1 and comp == 0 else None

            new = relaxed(field, twist, layer, y, size_y, wave, sigma_h[layer, rows], sigma_v[layer, rows], source)
            for part in range(2):
                for comp in range(3):
                    e_out[layer, part, comp, rows] = new[part][comp]
        return carry

    lax.fori_loop(0, layers, one, 0)

    def inner(layer, carry):
        add_rhs(layer, e_out, (layer,), a_part, observed, wave, sigma_h, sigma_v, a_out, (layer,), size_y, None)
        return carry

    lax.fori_loop(1, layers - 1, inner, 0)


def add_rhs(layer, new, at, a_part, observed, wave, sigma_h, sigma_v, a_out, out_at, size_y, extra):
    for y in range(0, size_y, ROWS):
        rows = slice(y, y + ROWS)
        sides = (factors(sigma_h[layer, rows], wave), factors(sigma_v[layer, rows], wave))
        add = extra(y) if extra is not None else None
        for comp in range(3):
            _, four, coup = sides[0] if comp < 2 else sides[1]
            br = rhs_of(0, new[at + (0, comp, rows)], observed[0, comp, layer, rows].astype(jnp.float32))
            bi = rhs_of(1, new[at + (1, comp, rows)], observed[1, comp, layer, rows].astype(jnp.float32))
            real = a_part[layer, 0, comp, rows] + (four * br + coup * bi)
            imag = a_part[layer, 1, comp, rows] + (four * bi - coup * br)
            if add is not None:
                real = real + add[0][comp]
                imag = imag + add[1][comp]
            a_out[out_at + (0, comp, rows)] = real
            a_out[out_at + (1, comp, rows)] = imag


def third_faces_kernel(
    side, wave_ref, e_halo, a_halo, e_part, a_part, observed, sigma_h, sigma_v, e_face, a_face, send
):
    _, even = position("gx")
    layers, size_y, _ = sigma_h.shape
    layer, right = side_layer(side, even, layers - 1)
    wave = wave_ref[...]
    for y in range(0, size_y, ROWS):
        rows = slice(y, y + ROWS)
        add = fix(e_halo, y, right, wave, sigma_h[layer, rows], sigma_v[layer, rows], size_y)
        for part in range(2):
            for comp in range(3):
                e_face[part, comp, rows] = e_part[layer, part, comp, rows] + add[part][comp]

    def extra(y):
        rows = slice(y, y + ROWS)
        return fix(a_halo, y, right, wave, sigma_h[layer, rows], sigma_v[layer, rows], size_y)

    add_rhs(layer, e_face, (), a_part, observed, wave, sigma_h, sigma_v, a_face, (), size_y, extra)
    write_faces(a_face, send, right, size_y)


def grad_rows(wave, field, adjoint):
    terms = [adjoint[0][comp] * field[1][comp] + adjoint[1][comp] * field[0][comp] for comp in range(3)]
    return wave * (terms[0] + terms[1]), wave * terms[2]


def put_rows(out, place, y, pair, share):
    for which in range(2):
        for k in range(ROWS // share):
            out[y // share + k, which, place] = pair[which][k * share : (k + 1) * share]


def last_sweep_kernel(
    wave_ref, e_body, e_p, e_z, a_body, a_p, a_z, observed, sigma_h, sigma_v, final, faces, grad, field, twist
):
    index, even = position("gx")
    layers, size_y, _ = sigma_h.shape
    share = grad.shape[3]
    wave = wave_ref[...]
    edge = jnp.where(index > 0, 1.0, 0.0)
    sides = [side_layer(side, even, layers - 1)[0] for side in range(2)]
    for part in range(2):
        for comp in range(3):
            for layer in range(1, layers - 1):
                final[part, comp, layer] = e_body[layer, part, comp]
            final[part, comp, sides[0]] = e_p[part, comp]
            final[part, comp, sides[1]] = e_z[part, comp]
    zero_layer(field, layers, size_y)
    gather_layers(a_body, a_p, a_z, field, even, layers)
    twists(field, twist, edge, layers, size_y)

    def sweep(layer, y):
        rows = slice(y, y + ROWS)
        now = [[final[part, comp, layer, rows] for comp in range(3)] for part in range(2)]

        def source(part, comp):
            return rhs_of(part, now[part][comp], observed[part, comp, layer, rows].astype(jnp.float32))

        return now, relaxed(field, twist, layer, y, size_y, wave, sigma_h[layer, rows], sigma_v[layer, rows], source)

    def inner(layer, carry):
        for y in range(0, size_y, ROWS):
            now, new = sweep(layer, y)
            put_rows(grad, layer - 1, y, grad_rows(wave, now, new), share)
        return carry

    lax.fori_loop(1, layers - 1, inner, 0)

    def outer(side, carry):
        layer = jnp.where(side == 0, sides[0], sides[1])
        for y in range(0, size_y, ROWS):
            _, new = sweep(layer, y)
            for part in range(2):
                for comp in range(3):
                    faces[side, part, comp, y : y + ROWS] = new[part][comp]
        return carry

    lax.fori_loop(0, 2, outer, 0)


def gradient_kernel(wave_ref, halo_p, halo_z, e_p, e_z, faces, inner, sigma_h, sigma_v, grad):
    _, even = position("gx")
    layers, size_y, _ = sigma_h.shape
    share = grad.shape[3]
    wave = wave_ref[...]
    for layer in range(1, layers - 1):
        for which in range(2):
            grad[:, which, layer] = inner[:, which, layer - 1]
    for side, (halo, now) in enumerate(((halo_p, e_p), (halo_z, e_z))):
        layer, right = side_layer(side, even, layers - 1)
        for y in range(0, size_y, ROWS):
            rows = slice(y, y + ROWS)
            add = fix(halo, y, right, wave, sigma_h[layer, rows], sigma_v[layer, rows], size_y)
            new = [[faces[side, part, comp, rows] + add[part][comp] for comp in range(3)] for part in range(2)]
            old = [[now[part, comp, rows] for comp in range(3)] for part in range(2)]
            put_rows(grad, layer, y, grad_rows(wave, old, new), share)


def call(kernel, name, specs, outs, scratch=()):
    return pl.pallas_call(
        kernel,
        name=name,
        out_shape=tuple(jax.ShapeDtypeStruct(shape, jnp.float32) for shape in outs),
        in_specs=specs,
        out_specs=tuple(VMEM for _ in outs),
        scratch_shapes=[s if not isinstance(s, tuple) else pltpu.VMEM(s, jnp.float32) for s in scratch],
        compiler_params=pltpu.CompilerParams(vmem_limit_bytes=24 << 20),
    )


def on_device(
    sigma_h, sigma_v, wave_scale, field_start, adjoint_start, observed, tx_count, tx_cells
):
    layers, size_y, size_z = sigma_h.shape
    slabs = lax.axis_size("gx")
    freqs = lax.axis_size("freq")
    share = size_y // freqs
    start = field_start[0]
    adjoint = adjoint_start[0]
    seen = observed[0]
    wave = wave_scale[None]

    ends = (
        [(i, i + 1) for i in range(0, slabs - 1, 2)],
        [(i, i + 1) for i in range(1, slabs - 1, 2)],
    )
    swaps = [pairs + [(b, a) for a, b in pairs] for pairs in ends]

    def swap(values, side):
        return lax.ppermute(values, "gx", swaps[side])

    plane = (size_y, size_z)
    half = (2, 2) + plane
    face = (2, 3) + plane
    body = (layers,) + face
    more = (layers + 1,) + face
    hbm = pl.BlockSpec(memory_space=pltpu.HBM)

    (e_p,) = call(
        first_faces_kernel,
        "first_faces",
        [hbm],
        [half],
        [pltpu.VMEM(face, jnp.bfloat16), face, pltpu.SemaphoreType.DMA],
    )(start)
    e_p_in = swap(e_p, 0)
    e1, src, e_z = call(
        first_sweep_kernel,
        "first_sweep",
        [VMEM] * 6,
        [body, (layers,) + plane, half],
        [more, more, face],
    )(wave, tx_count[None], tx_cells[None], start, sigma_h, sigma_v)
    e_z_in = swap(e_z, 1)

    def second(side, halo):
        return call(
            lambda *refs: second_faces_kernel(side, *refs),
            "second_faces_%d" % side,
            [VMEM] * 5,
            [face, half],
        )(wave, halo, e1, sigma_h, sigma_v)

    e1_p, e1_p_out = second(0, e_p_in)
    e1_p_in = swap(e1_p_out, 0)
    adjoint, e1_p = lax.optimization_barrier((adjoint, e1_p))
    a1, a_p, a_z = call(
        first_adjoint_kernel, "first_adjoint", [VMEM] * 4, [body, half, half], [more, more, face]
    )(wave, adjoint, sigma_h, sigma_v)
    a1, e_z_in = lax.optimization_barrier((a1, e_z_in))
    e1_z, e1_z_out = second(1, e_z_in)
    a_p, a_z, e1_z_out = lax.optimization_barrier((a_p, a_z, e1_z_out))
    e1_z_in = swap(e1_z_out, 1)
    a_z_in = swap(a_z, 1)
    e1_z, e1_p_in = lax.optimization_barrier((e1_z, e1_p_in))
    a_p_in = swap(a_p, 0)
    e2, a1_body = call(
        second_sweep_kernel, "second_sweep", [VMEM] * 9, [body, body], [more, more]
    )(wave, e1, e1_p, e1_z, a1, src, seen, sigma_h, sigma_v)
    e2, e1_z_in, a_z_in = lax.optimization_barrier((e2, e1_z_in, a_z_in))

    def third(side, e_halo, a_halo):
        return call(
            lambda *refs: third_faces_kernel(side, *refs),
            "third_faces_%d" % side,
            [VMEM] * 8,
            [face, face, half],
        )(wave, e_halo, a_halo, e2, a1, seen, sigma_h, sigma_v)

    e2_z, a1_z, a1_z_out = third(1, e1_z_in, a_z_in)
    a1_z_in = swap(a1_z_out, 1)
    e2_p, a1_p, a1_p_out = third(0, e1_p_in, a_p_in)
    a1_p_in = swap(a1_p_out, 0)
    inner_blocks = (freqs, 2, layers - 2, share, size_z)
    blocks = (freqs, 2, layers, share, size_z)
    final, faces, inner = call(
        last_sweep_kernel,
        "last_sweep",
        [VMEM] * 10,
        [(2, 3, layers) + plane, (2,) + face, inner_blocks],
        [more, more],
    )(wave, e2, e2_p, e2_z, a1_body, a1_p, a1_z, seen, sigma_h, sigma_v)
    faces, a1_z_in = lax.optimization_barrier((faces, a1_z_in))
    (terms,) = call(gradient_kernel, "gradient", [VMEM] * 9, [blocks])(
        wave, a1_p_in, a1_z_in, e2_p, e2_z, faces, inner, sigma_h, sigma_v
    )
    gathered = lax.all_to_all(terms, "freq", 0, 0)
    return (jnp.sum(gathered, axis=0), final[None])


def solution(mesh):
    placed = (
        P("gx", None, None),
        P("gx", None, None),
        P("freq"),
        P("freq", None, None, "gx", None, None),
        P("freq", None, None, "gx", None, None),
        P("freq", None, None, "gx", None, None),
        P(),
        P(),
    )
    return jax.shard_map(
        on_device,
        mesh=mesh,
        in_specs=placed,
        out_specs=(P(None, "gx", "freq", None), P("freq", None, None, "gx", None, None)),
        check_vma=False,
    )
```

```python
import jax
import jax.numpy as jnp
from jax import lax
from jax.experimental import pallas as pl
from jax.experimental.pallas import tpu as pltpu
from jax.sharding import PartitionSpec as P

ITERS = 2
THETA = 0.5
SOURCE_GAIN = 8.0
ROWS = 8

VMEM = pl.BlockSpec(memory_space=pltpu.VMEM)


def position(axis):
    index = lax.axis_index(axis)
    even = 1 - lax.rem(index, 2)
    return index, even


def side_layer(side, even, last):
    right = even if side == 0 else 1 - even
    return last * right, right.astype(jnp.float32)


def lane_of(shape):
    return lax.broadcasted_iota(jnp.int32, shape, len(shape) - 1)


def next_z(values):
    size = values.shape[-1]
    moved = pltpu.roll(values, size - 1, 1)
    return jnp.where(lane_of(values.shape) == size - 1, 0.0, moved)


def last_z(values):
    moved = pltpu.roll(values, 1, 1)
    return jnp.where(lane_of(values.shape) == 0, 0.0, moved)


def factors(sigma, wave):
    coupling = wave * sigma
    inverse = THETA / (16.0 + coupling * coupling)
    return coupling, 4.0 * inverse, coupling * inverse


def chunks(size_y):
    return [slice(y, y + ROWS) for y in range(0, size_y, ROWS)]


def behind_row(ref, index, y, size_y):
    now = ref[index + (slice(y, y + ROWS),)]
    if y == 0:
        row = lax.broadcasted_iota(jnp.int32, now.shape, 0)
        return now, jnp.where(row == 0, 0.0, pltpu.roll(now, 1, 0))
    return now, ref[index + (slice(y - 1, y - 1 + ROWS),)]


def ahead_row(ref, index, y, size_y):
    now = ref[index + (slice(y, y + ROWS),)]
    if y + ROWS == size_y:
        row = lax.broadcasted_iota(jnp.int32, now.shape, 0)
        return now, jnp.where(row == ROWS - 1, 0.0, pltpu.roll(now, ROWS - 1, 0))
    return now, ref[index + (slice(y + 1, y + 1 + ROWS),)]


def write_faces(face, out, right, size_y):
    for part in range(2):
        for y in range(0, size_y, ROWS):
            rows = slice(y, y + ROWS)
            ex, ex_next = ahead_row(face, (part, 0), y, size_y)
            out[part, 0, rows] = face[part, 1, rows] + right * (ex_next - ex)
            out[part, 1, rows] = face[part, 2, rows] + right * (next_z(ex) - ex)


def fix(halo, y, right, wave, sig_h, sig_v, size_y):
    _, h_four, h_coup = factors(sig_h, wave)
    _, v_four, v_coup = factors(sig_v, wave)
    extra = []
    for part in range(2):
        u, u_last = behind_row(halo, (part, 0), y, size_y)
        v = halo[part, 1, y : y + ROWS]
        extra.append((right * ((last_z(v) - v) - (u - u_last)), u, v))
    real, imag = [], []
    for comp in range(3):
        four, coup = (h_four, h_coup) if comp < 2 else (v_four, v_coup)
        real.append(four * extra[0][comp] + coup * extra[1][comp])
        imag.append(four * extra[1][comp] - coup * extra[0][comp])
    return real, imag


def twists(field, twist, edge, layers, size_y):
    def one(layer, carry):
        for part in range(2):
            for y in range(0, size_y, ROWS):
                rows = slice(y, y + ROWS)
                ex, ex_next = ahead_row(field, (layer, part, 0), y, size_y)
                ey = field[layer, part, 1, rows]
                ez, ez_next = ahead_row(field, (layer, part, 2), y, size_y)
                ey_right = field[layer + 1, part, 1, rows]
                ez_right = field[layer + 1, part, 2, rows]
                twist[layer + 1, part, 0, rows] = (ez_next - ez) - (next_z(ey) - ey)
                twist[layer + 1, part, 1, rows] = (next_z(ex) - ex) - (ez_right - ez)
                twist[layer + 1, part, 2, rows] = (ey_right - ey) - (ex_next - ex)
        return carry

    lax.fori_loop(0, layers, one, 0)
    for part in range(2):
        for rows in chunks(size_y):
            twist[0, part, 1, rows] = -edge * field[0, part, 2, rows]
            twist[0, part, 2, rows] = edge * field[0, part, 1, rows]


def curled(twist, layer, y, size_y):
    rows = slice(y, y + ROWS)
    result = []
    for part in range(2):
        hx, hx_last = behind_row(twist, (layer + 1, part, 0), y, size_y)
        hz, hz_last = behind_row(twist, (layer + 1, part, 2), y, size_y)
        hy = twist[layer + 1, part, 1, rows]
        hy_left = twist[layer, part, 1, rows]
        hz_left = twist[layer, part, 2, rows]
        result.append(
            (
                (hz - hz_last) - (hy - last_z(hy)),
                (hx - last_z(hx)) - (hz - hz_left),
                (hy - hy_left) - (hx - hx_last),
            )
        )
    return result


def relaxed(field, twist, layer, y, size_y, wave, sig_h, sig_v, source):
    rows = slice(y, y + ROWS)
    sides = (factors(sig_h, wave), factors(sig_v, wave))
    curl = curled(twist, layer, y, size_y)
    real, imag = [], []
    for comp in range(3):
        coupling, four, coup = sides[0] if comp < 2 else sides[1]
        er = field[layer, 0, comp, rows]
        ei = field[layer, 1, comp, rows]
        rr = coupling * ei - curl[0][comp]
        ri = -(coupling * er) - curl[1][comp]
        br, bi = source(0, comp), source(1, comp)
        if br is not None:
            rr = rr + br
        if bi is not None:
            ri = ri + bi
        real.append(er + (four * rr + coup * ri))
        imag.append(ei + (four * ri - coup * rr))
    return real, imag


def zero_layer(field, layer, size_y):
    for part in range(2):
        for comp in (1, 2):
            for rows in chunks(size_y):
                field[layer, part, comp, rows] = jnp.zeros((ROWS, field.shape[-1]), jnp.float32)


def widen(start, field, layers, size_y):
    for layer in range(layers):
        for part in range(2):
            for comp in range(3):
                field[layer, part, comp] = start[part, comp, layer].astype(jnp.float32)


def faces_kernel(values, p_send, z_send, face):
    _, even = position("gx")
    faces_of(values, 0, even, face, p_send)
    faces_of(values, 1, even, face, z_send)


def faces_of(values, side, even, face, out):
    layers, size_y = values.shape[2], values.shape[3]
    layer, right = side_layer(side, even, layers - 1)
    for part in range(2):
        for comp in range(3):
            face[part, comp] = values[part, comp, layer].astype(jnp.float32)
    write_faces(face, out, right, size_y)


def first_sweep_kernel(wave_ref, count_ref, cells_ref, start, sigma_h, sigma_v, e_out, src, field, twist):
    index, _ = position("gx")
    layers, size_y, size_z = sigma_h.shape
    wave = wave_ref[...]
    edge = jnp.where(index > 0, 1.0, 0.0)
    add_slots(wave, count_ref[...], cells_ref[...], index * (layers * size_y), src)

    def source(part, comp, layer, rows):
        return src[layer, rows] if part == 1 and comp == 0 else None

    zero_layer(field, layers, size_y)
    whole_sweep(start, field, twist, edge, wave, sigma_h, sigma_v, e_out, source)


def add_slots(wave, count, cells, first, src):
    layers, size_y, size_z = src.shape
    slots = cells.shape[1]
    shift = size_z.bit_length() - 1
    assert size_z == 1 << shift
    row = lax.shift_right_logical(cells, shift) - first
    spot = jnp.bitwise_and(cells, size_z - 1)
    live = lane_of((1, slots)) < count
    row = jnp.where(live, row, -1)
    at_row = lax.broadcasted_iota(jnp.int32, (layers * size_y, slots), 0) == row
    at_spot = lax.broadcasted_iota(jnp.int32, (size_z, slots), 0) == spot
    counts = lax.dot_general(
        jnp.where(at_row, 1.0, 0.0).astype(jnp.bfloat16),
        jnp.where(at_spot, 1.0, 0.0).astype(jnp.bfloat16),
        (((1,), (1,)), ((), ())),
        preferred_element_type=jnp.float32,
    )
    gain = SOURCE_GAIN * wave
    for layer in range(layers):
        src[layer] = gain * counts[layer * size_y : (layer + 1) * size_y]


def first_adjoint_kernel(wave_ref, adjoint, sigma_h, sigma_v, a_out, field, twist):
    index, _ = position("gx")
    layers, size_y, _ = sigma_h.shape
    edge = jnp.where(index > 0, 1.0, 0.0)
    zero_layer(field, layers, size_y)
    none = lambda part, comp, layer, rows: None
    whole_sweep(adjoint, field, twist, edge, wave_ref[...], sigma_h, sigma_v, a_out, none)


def whole_sweep(values, field, twist, edge, wave, sigma_h, sigma_v, out, source):
    layers, size_y, _ = sigma_h.shape
    widen(values, field, layers, size_y)
    twists(field, twist, edge, layers, size_y)

    def one(layer, carry):
        for y in range(0, size_y, ROWS):
            rows = slice(y, y + ROWS)
            at = lambda part, comp: source(part, comp, layer, rows)
            new = relaxed(field, twist, layer, y, size_y, wave, sigma_h[layer, rows], sigma_v[layer, rows], at)
            for part in range(2):
                for comp in range(3):
                    out[layer, part, comp, rows] = new[part][comp]
        return carry

    lax.fori_loop(0, layers, one, 0)


def second_faces_kernel(side, wave_ref, halo, part_new, sigma_h, sigma_v, face, send):
    _, even = position("gx")
    layers, size_y, _ = sigma_h.shape
    layer, right = side_layer(side, even, layers - 1)
    wave = wave_ref[...]
    for y in range(0, size_y, ROWS):
        rows = slice(y, y + ROWS)
        add = fix(halo, y, right, wave, sigma_h[layer, rows], sigma_v[layer, rows], size_y)
        for part in range(2):
            for comp in range(3):
                face[part, comp, rows] = part_new[layer, part, comp, rows] + add[part][comp]
    write_faces(face, send, right, size_y)


def gather_layers(body, face_p, face_z, field, even, layers):
    p_layer, _ = side_layer(0, even, layers - 1)
    z_layer, _ = side_layer(1, even, layers - 1)
    for part in range(2):
        for comp in range(3):
            for layer in range(1, layers - 1):
                field[layer, part, comp] = body[layer, part, comp]
            field[p_layer, part, comp] = face_p[part, comp]
            field[z_layer, part, comp] = face_z[part, comp]


def rhs_of(part, new, seen):
    return new - seen if part == 0 else seen - new


def second_sweep_kernel(
    wave_ref, e_body, e_p, e_z, a_part, src, observed, sigma_h, sigma_v, e_out, a_out, field, twist
):
    index, even = position("gx")
    layers, size_y, _ = sigma_h.shape
    wave = wave_ref[...]
    edge = jnp.where(index > 0, 1.0, 0.0)
    zero_layer(field, layers, size_y)
    gather_layers(e_body, e_p, e_z, field, even, layers)
    twists(field, twist, edge, layers, size_y)

    def one(layer, carry):
        for y in range(0, size_y, ROWS):
            rows = slice(y, y + ROWS)

            def source(part, comp):
                return src[layer, rows] if part == 1 and comp == 0 else None

            new = relaxed(field, twist, layer, y, size_y, wave, sigma_h[layer, rows], sigma_v[layer, rows], source)
            for part in range(2):
                for comp in range(3):
                    e_out[layer, part, comp, rows] = new[part][comp]
        return carry

    lax.fori_loop(0, layers, one, 0)

    def inner(layer, carry):
        add_rhs(layer, e_out, (layer,), a_part, observed, wave, sigma_h, sigma_v, a_out, (layer,), size_y, None)
        return carry

    lax.fori_loop(1, layers - 1, inner, 0)


def add_rhs(layer, new, at, a_part, observed, wave, sigma_h, sigma_v, a_out, out_at, size_y, extra):
    for y in range(0, size_y, ROWS):
        rows = slice(y, y + ROWS)
        sides = (factors(sigma_h[layer, rows], wave), factors(sigma_v[layer, rows], wave))
        add = extra(y) if extra is not None else None
        for comp in range(3):
            _, four, coup = sides[0] if comp < 2 else sides[1]
            br = rhs_of(0, new[at + (0, comp, rows)], observed[0, comp, layer, rows].astype(jnp.float32))
            bi = rhs_of(1, new[at + (1, comp, rows)], observed[1, comp, layer, rows].astype(jnp.float32))
            real = a_part[layer, 0, comp, rows] + (four * br + coup * bi)
            imag = a_part[layer, 1, comp, rows] + (four * bi - coup * br)
            if add is not None:
                real = real + add[0][comp]
                imag = imag + add[1][comp]
            a_out[out_at + (0, comp, rows)] = real
            a_out[out_at + (1, comp, rows)] = imag


def third_faces_kernel(
    side, wave_ref, e_halo, a_halo, e_part, a_part, observed, sigma_h, sigma_v, e_face, a_face, send
):
    _, even = position("gx")
    layers, size_y, _ = sigma_h.shape
    layer, right = side_layer(side, even, layers - 1)
    wave = wave_ref[...]
    for y in range(0, size_y, ROWS):
        rows = slice(y, y + ROWS)
        add = fix(e_halo, y, right, wave, sigma_h[layer, rows], sigma_v[layer, rows], size_y)
        for part in range(2):
            for comp in range(3):
                e_face[part, comp, rows] = e_part[layer, part, comp, rows] + add[part][comp]

    def extra(y):
        rows = slice(y, y + ROWS)
        return fix(a_halo, y, right, wave, sigma_h[layer, rows], sigma_v[layer, rows], size_y)

    add_rhs(layer, e_face, (), a_part, observed, wave, sigma_h, sigma_v, a_face, (), size_y, extra)
    write_faces(a_face, send, right, size_y)


def grad_rows(wave, field, adjoint):
    terms = [adjoint[0][comp] * field[1][comp] + adjoint[1][comp] * field[0][comp] for comp in range(3)]
    return wave * (terms[0] + terms[1]), wave * terms[2]


def put_rows(out, place, y, pair, share):
    for which in range(2):
        for k in range(ROWS // share):
            out[y // share + k, which, place] = pair[which][k * share : (k + 1) * share]


def last_sweep_kernel(
    wave_ref, e_body, e_p, e_z, a_body, a_p, a_z, observed, sigma_h, sigma_v, final, faces, grad, field, twist
):
    index, even = position("gx")
    layers, size_y, _ = sigma_h.shape
    share = grad.shape[3]
    wave = wave_ref[...]
    edge = jnp.where(index > 0, 1.0, 0.0)
    sides = [side_layer(side, even, layers - 1)[0] for side in range(2)]
    for part in range(2):
        for comp in range(3):
            for layer in range(1, layers - 1):
                final[part, comp, layer] = e_body[layer, part, comp]
            final[part, comp, sides[0]] = e_p[part, comp]
            final[part, comp, sides[1]] = e_z[part, comp]
    zero_layer(field, layers, size_y)
    gather_layers(a_body, a_p, a_z, field, even, layers)
    twists(field, twist, edge, layers, size_y)

    def sweep(layer, y):
        rows = slice(y, y + ROWS)
        now = [[final[part, comp, layer, rows] for comp in range(3)] for part in range(2)]

        def source(part, comp):
            return rhs_of(part, now[part][comp], observed[part, comp, layer, rows].astype(jnp.float32))

        return now, relaxed(field, twist, layer, y, size_y, wave, sigma_h[layer, rows], sigma_v[layer, rows], source)

    def inner(layer, carry):
        for y in range(0, size_y, ROWS):
            now, new = sweep(layer, y)
            put_rows(grad, layer - 1, y, grad_rows(wave, now, new), share)
        return carry

    lax.fori_loop(1, layers - 1, inner, 0)

    def outer(side, carry):
        layer = jnp.where(side == 0, sides[0], sides[1])
        for y in range(0, size_y, ROWS):
            _, new = sweep(layer, y)
            for part in range(2):
                for comp in range(3):
                    faces[side, part, comp, y : y + ROWS] = new[part][comp]
        return carry

    lax.fori_loop(0, 2, outer, 0)


def gradient_kernel(wave_ref, halo_p, halo_z, e_p, e_z, faces, inner, sigma_h, sigma_v, grad):
    _, even = position("gx")
    layers, size_y, _ = sigma_h.shape
    share = grad.shape[3]
    wave = wave_ref[...]
    for layer in range(1, layers - 1):
        for which in range(2):
            grad[:, which, layer] = inner[:, which, layer - 1]
    for side, (halo, now) in enumerate(((halo_p, e_p), (halo_z, e_z))):
        layer, right = side_layer(side, even, layers - 1)
        for y in range(0, size_y, ROWS):
            rows = slice(y, y + ROWS)
            add = fix(halo, y, right, wave, sigma_h[layer, rows], sigma_v[layer, rows], size_y)
            new = [[faces[side, part, comp, rows] + add[part][comp] for comp in range(3)] for part in range(2)]
            old = [[now[part, comp, rows] for comp in range(3)] for part in range(2)]
            put_rows(grad, layer, y, grad_rows(wave, old, new), share)


def call(kernel, name, specs, outs, scratch=()):
    return pl.pallas_call(
        kernel,
        name=name,
        out_shape=tuple(jax.ShapeDtypeStruct(shape, jnp.float32) for shape in outs),
        in_specs=specs,
        out_specs=tuple(VMEM for _ in outs),
        scratch_shapes=[s if not isinstance(s, tuple) else pltpu.VMEM(s, jnp.float32) for s in scratch],
        compiler_params=pltpu.CompilerParams(vmem_limit_bytes=24 << 20),
    )


def on_device(
    sigma_h, sigma_v, wave_scale, field_start, adjoint_start, observed, tx_count, tx_cells
):
    layers, size_y, size_z = sigma_h.shape
    slabs = lax.axis_size("gx")
    freqs = lax.axis_size("freq")
    share = size_y // freqs
    start = field_start[0]
    adjoint = adjoint_start[0]
    seen = observed[0]
    wave = wave_scale[None]

    ends = (
        [(i, i + 1) for i in range(0, slabs - 1, 2)],
        [(i, i + 1) for i in range(1, slabs - 1, 2)],
    )
    swaps = [pairs + [(b, a) for a, b in pairs] for pairs in ends]

    def swap(values, side):
        return lax.ppermute(values, "gx", swaps[side])

    plane = (size_y, size_z)
    half = (2, 2) + plane
    face = (2, 3) + plane
    body = (layers,) + face
    more = (layers + 1,) + face

    count = tx_count[None]
    e_p, e_z = call(faces_kernel, "first_faces", [VMEM], [half] * 2, [face])(start)
    e_p_in = swap(e_p, 0)
    a_p, a_z = call(faces_kernel, "adjoint_faces", [VMEM], [half] * 2, [face])(adjoint)
    e_z, a_p, a_z, wave, count, e1_start = lax.optimization_barrier((e_z, a_p, a_z, wave, count, start))
    e_z_in = swap(e_z, 1)
    e1, src = call(
        first_sweep_kernel,
        "first_sweep",
        [VMEM] * 6,
        [body, (layers,) + plane],
        [more, more],
    )(wave, count, tx_cells[None], e1_start, sigma_h, sigma_v)

    def second(side, halo):
        return call(
            lambda *refs: second_faces_kernel(side, *refs),
            "second_faces_%d" % side,
            [VMEM] * 5,
            [face, half],
        )(wave, halo, e1, sigma_h, sigma_v)

    e1_p, e1_p_out = second(0, e_p_in)
    e1_p_in = swap(e1_p_out, 0)
    adjoint, e1_p = lax.optimization_barrier((adjoint, e1_p))
    (a1,) = call(first_adjoint_kernel, "first_adjoint", [VMEM] * 4, [body], [more, more])(
        wave, adjoint, sigma_h, sigma_v
    )
    a1, e_z_in = lax.optimization_barrier((a1, e_z_in))
    e1_z, e1_z_out = second(1, e_z_in)
    a_p, a_z, e1_z_out = lax.optimization_barrier((a_p, a_z, e1_z_out))
    e1_z_in = swap(e1_z_out, 1)
    a_z_in = swap(a_z, 1)
    e1_z, e1_p_in = lax.optimization_barrier((e1_z, e1_p_in))
    a_p_in = swap(a_p, 0)
    e2, a1_body = call(
        second_sweep_kernel, "second_sweep", [VMEM] * 9, [body, body], [more, more]
    )(wave, e1, e1_p, e1_z, a1, src, seen, sigma_h, sigma_v)
    e2, e1_z_in, a_z_in = lax.optimization_barrier((e2, e1_z_in, a_z_in))

    def third(side, e_halo, a_halo):
        return call(
            lambda *refs: third_faces_kernel(side, *refs),
            "third_faces_%d" % side,
            [VMEM] * 8,
            [face, face, half],
        )(wave, e_halo, a_halo, e2, a1, seen, sigma_h, sigma_v)

    e2_z, a1_z, a1_z_out = third(1, e1_z_in, a_z_in)
    a1_z_in = swap(a1_z_out, 1)
    e2_p, a1_p, a1_p_out = third(0, e1_p_in, a_p_in)
    a1_p_in = swap(a1_p_out, 0)
    inner_blocks = (freqs, 2, layers - 2, share, size_z)
    blocks = (freqs, 2, layers, share, size_z)
    final, faces, inner = call(
        last_sweep_kernel,
        "last_sweep",
        [VMEM] * 10,
        [(2, 3, layers) + plane, (2,) + face, inner_blocks],
        [more, more],
    )(wave, e2, e2_p, e2_z, a1_body, a1_p, a1_z, seen, sigma_h, sigma_v)
    faces, a1_z_in = lax.optimization_barrier((faces, a1_z_in))
    (terms,) = call(gradient_kernel, "gradient", [VMEM] * 9, [blocks])(
        wave, a1_p_in, a1_z_in, e2_p, e2_z, faces, inner, sigma_h, sigma_v
    )
    gathered = lax.all_to_all(terms, "freq", 0, 0)
    return (jnp.sum(gathered, axis=0), final[None])


def solution(mesh):
    placed = (
        P("gx", None, None),
        P("gx", None, None),
        P("freq"),
        P("freq", None, None, "gx", None, None),
        P("freq", None, None, "gx", None, None),
        P("freq", None, None, "gx", None, None),
        P(),
        P(),
    )
    return jax.shard_map(
        on_device,
        mesh=mesh,
        in_specs=placed,
        out_specs=(P(None, "gx", "freq", None), P("freq", None, None, "gx", None, None)),
        check_vma=False,
    )
```

```python
import jax
import jax.numpy as jnp
from jax import lax
from jax.experimental import pallas as pl
from jax.experimental.pallas import tpu as pltpu
from jax.sharding import PartitionSpec as P

ITERS = 2
THETA = 0.5
SOURCE_GAIN = 8.0
ROWS = 8

VMEM = pl.BlockSpec(memory_space=pltpu.VMEM)


def position(axis):
    index = lax.axis_index(axis)
    even = 1 - lax.rem(index, 2)
    return index, even


def side_layer(side, even, last):
    right = even if side == 0 else 1 - even
    return last * right, right.astype(jnp.float32)


def lane_of(shape):
    return lax.broadcasted_iota(jnp.int32, shape, len(shape) - 1)


def next_z(values):
    size = values.shape[-1]
    moved = pltpu.roll(values, size - 1, 1)
    return jnp.where(lane_of(values.shape) == size - 1, 0.0, moved)


def last_z(values):
    moved = pltpu.roll(values, 1, 1)
    return jnp.where(lane_of(values.shape) == 0, 0.0, moved)


def factors(sigma, wave):
    coupling = wave * sigma
    inverse = THETA / (16.0 + coupling * coupling)
    return coupling, 4.0 * inverse, coupling * inverse


def chunks(size_y):
    return [slice(y, y + ROWS) for y in range(0, size_y, ROWS)]


def behind_row(ref, index, y, size_y):
    now = ref[index + (slice(y, y + ROWS),)]
    if y == 0:
        row = lax.broadcasted_iota(jnp.int32, now.shape, 0)
        return now, jnp.where(row == 0, 0.0, pltpu.roll(now, 1, 0))
    return now, ref[index + (slice(y - 1, y - 1 + ROWS),)]


def ahead_row(ref, index, y, size_y):
    now = ref[index + (slice(y, y + ROWS),)]
    if y + ROWS == size_y:
        row = lax.broadcasted_iota(jnp.int32, now.shape, 0)
        return now, jnp.where(row == ROWS - 1, 0.0, pltpu.roll(now, ROWS - 1, 0))
    return now, ref[index + (slice(y + 1, y + 1 + ROWS),)]


def write_faces(face, out, right, size_y):
    for part in range(2):
        for y in range(0, size_y, ROWS):
            rows = slice(y, y + ROWS)
            ex, ex_next = ahead_row(face, (part, 0), y, size_y)
            out[part, 0, rows] = face[part, 1, rows] + right * (ex_next - ex)
            out[part, 1, rows] = face[part, 2, rows] + right * (next_z(ex) - ex)


def fix(halo, y, right, wave, sig_h, sig_v, size_y):
    _, h_four, h_coup = factors(sig_h, wave)
    _, v_four, v_coup = factors(sig_v, wave)
    extra = []
    for part in range(2):
        u, u_last = behind_row(halo, (part, 0), y, size_y)
        v = halo[part, 1, y : y + ROWS]
        extra.append((right * ((last_z(v) - v) - (u - u_last)), u, v))
    real, imag = [], []
    for comp in range(3):
        four, coup = (h_four, h_coup) if comp < 2 else (v_four, v_coup)
        real.append(four * extra[0][comp] + coup * extra[1][comp])
        imag.append(four * extra[1][comp] - coup * extra[0][comp])
    return real, imag


def twists(field, twist, edge, layers, size_y):
    def one(layer, carry):
        for part in range(2):
            for y in range(0, size_y, ROWS):
                rows = slice(y, y + ROWS)
                ex, ex_next = ahead_row(field, (layer, part, 0), y, size_y)
                ey = field[layer, part, 1, rows]
                ez, ez_next = ahead_row(field, (layer, part, 2), y, size_y)
                ey_right = field[layer + 1, part, 1, rows]
                ez_right = field[layer + 1, part, 2, rows]
                twist[layer + 1, part, 0, rows] = (ez_next - ez) - (next_z(ey) - ey)
                twist[layer + 1, part, 1, rows] = (next_z(ex) - ex) - (ez_right - ez)
                twist[layer + 1, part, 2, rows] = (ey_right - ey) - (ex_next - ex)
        return carry

    lax.fori_loop(0, layers, one, 0)
    for part in range(2):
        for rows in chunks(size_y):
            twist[0, part, 1, rows] = -edge * field[0, part, 2, rows]
            twist[0, part, 2, rows] = edge * field[0, part, 1, rows]


def curled(twist, layer, y, size_y):
    rows = slice(y, y + ROWS)
    result = []
    for part in range(2):
        hx, hx_last = behind_row(twist, (layer + 1, part, 0), y, size_y)
        hz, hz_last = behind_row(twist, (layer + 1, part, 2), y, size_y)
        hy = twist[layer + 1, part, 1, rows]
        hy_left = twist[layer, part, 1, rows]
        hz_left = twist[layer, part, 2, rows]
        result.append(
            (
                (hz - hz_last) - (hy - last_z(hy)),
                (hx - last_z(hx)) - (hz - hz_left),
                (hy - hy_left) - (hx - hx_last),
            )
        )
    return result


def relaxed(field, twist, layer, y, size_y, wave, sig_h, sig_v, source):
    rows = slice(y, y + ROWS)
    sides = (factors(sig_h, wave), factors(sig_v, wave))
    curl = curled(twist, layer, y, size_y)
    real, imag = [], []
    for comp in range(3):
        coupling, four, coup = sides[0] if comp < 2 else sides[1]
        er = field[layer, 0, comp, rows]
        ei = field[layer, 1, comp, rows]
        rr = coupling * ei - curl[0][comp]
        ri = -(coupling * er) - curl[1][comp]
        br, bi = source(0, comp), source(1, comp)
        if br is not None:
            rr = rr + br
        if bi is not None:
            ri = ri + bi
        real.append(er + (four * rr + coup * ri))
        imag.append(ei + (four * ri - coup * rr))
    return real, imag


def zero_layer(field, layer, size_y):
    for part in range(2):
        for comp in (1, 2):
            for rows in chunks(size_y):
                field[layer, part, comp, rows] = jnp.zeros((ROWS, field.shape[-1]), jnp.float32)


def widen(start, field, layers, size_y):
    for layer in range(layers):
        for part in range(2):
            for comp in range(3):
                field[layer, part, comp] = start[part, comp, layer].astype(jnp.float32)


def faces_kernel(values, p_send, z_send, face):
    _, even = position("gx")
    faces_of(values, 0, even, face, p_send)
    faces_of(values, 1, even, face, z_send)


def faces_of(values, side, even, face, out):
    layers, size_y = values.shape[2], values.shape[3]
    layer, right = side_layer(side, even, layers - 1)
    for part in range(2):
        for comp in range(3):
            face[part, comp] = values[part, comp, layer].astype(jnp.float32)
    write_faces(face, out, right, size_y)


def source_kernel(wave_ref, count_ref, cells_ref, src):
    index, _ = position("gx")
    layers, size_y, _ = src.shape
    add_slots(wave_ref[...], count_ref[...], cells_ref[...], index * (layers * size_y), src)


def first_sweep_kernel(wave_ref, src, start, sigma_h, sigma_v, e_out, field, twist):
    index, _ = position("gx")
    layers, size_y, size_z = sigma_h.shape
    wave = wave_ref[...]
    edge = jnp.where(index > 0, 1.0, 0.0)

    def source(part, comp, layer, rows):
        return src[layer, rows] if part == 1 and comp == 0 else None

    zero_layer(field, layers, size_y)
    whole_sweep(start, field, twist, edge, wave, sigma_h, sigma_v, e_out, source)


def add_slots(wave, count, cells, first, src):
    layers, size_y, size_z = src.shape
    slots = cells.shape[1]
    shift = size_z.bit_length() - 1
    assert size_z == 1 << shift
    row = lax.shift_right_logical(cells, shift) - first
    spot = jnp.bitwise_and(cells, size_z - 1)
    live = lane_of((1, slots)) < count
    row = jnp.where(live, row, -1)
    at_row = lax.broadcasted_iota(jnp.int32, (layers * size_y, slots), 0) == row
    at_spot = lax.broadcasted_iota(jnp.int32, (size_z, slots), 0) == spot
    counts = lax.dot_general(
        jnp.where(at_row, 1.0, 0.0).astype(jnp.bfloat16),
        jnp.where(at_spot, 1.0, 0.0).astype(jnp.bfloat16),
        (((1,), (1,)), ((), ())),
        preferred_element_type=jnp.float32,
    )
    gain = SOURCE_GAIN * wave
    for layer in range(layers):
        src[layer] = gain * counts[layer * size_y : (layer + 1) * size_y]


def first_adjoint_kernel(wave_ref, adjoint, sigma_h, sigma_v, a_out, field, twist):
    index, _ = position("gx")
    layers, size_y, _ = sigma_h.shape
    edge = jnp.where(index > 0, 1.0, 0.0)
    zero_layer(field, layers, size_y)
    none = lambda part, comp, layer, rows: None
    whole_sweep(adjoint, field, twist, edge, wave_ref[...], sigma_h, sigma_v, a_out, none)


def whole_sweep(values, field, twist, edge, wave, sigma_h, sigma_v, out, source):
    layers, size_y, _ = sigma_h.shape
    widen(values, field, layers, size_y)
    twists(field, twist, edge, layers, size_y)

    def one(layer, carry):
        for y in range(0, size_y, ROWS):
            rows = slice(y, y + ROWS)
            at = lambda part, comp: source(part, comp, layer, rows)
            new = relaxed(field, twist, layer, y, size_y, wave, sigma_h[layer, rows], sigma_v[layer, rows], at)
            for part in range(2):
                for comp in range(3):
                    out[layer, part, comp, rows] = new[part][comp]
        return carry

    lax.fori_loop(0, layers, one, 0)


def second_faces_kernel(side, wave_ref, halo, part_new, sigma_h, sigma_v, face, send):
    _, even = position("gx")
    layers, size_y, _ = sigma_h.shape
    layer, right = side_layer(side, even, layers - 1)
    wave = wave_ref[...]
    for y in range(0, size_y, ROWS):
        rows = slice(y, y + ROWS)
        add = fix(halo, y, right, wave, sigma_h[layer, rows], sigma_v[layer, rows], size_y)
        for part in range(2):
            for comp in range(3):
                face[part, comp, rows] = part_new[layer, part, comp, rows] + add[part][comp]
    write_faces(face, send, right, size_y)


def gather_layers(body, face_p, face_z, field, even, layers):
    p_layer, _ = side_layer(0, even, layers - 1)
    z_layer, _ = side_layer(1, even, layers - 1)
    for part in range(2):
        for comp in range(3):
            for layer in range(1, layers - 1):
                field[layer, part, comp] = body[layer, part, comp]
            field[p_layer, part, comp] = face_p[part, comp]
            field[z_layer, part, comp] = face_z[part, comp]


def rhs_of(part, new, seen):
    return new - seen if part == 0 else seen - new


def second_sweep_kernel(
    wave_ref, e_body, e_p, e_z, a_part, src, observed, sigma_h, sigma_v, e_out, a_out, field, twist
):
    index, even = position("gx")
    layers, size_y, _ = sigma_h.shape
    wave = wave_ref[...]
    edge = jnp.where(index > 0, 1.0, 0.0)
    zero_layer(field, layers, size_y)
    gather_layers(e_body, e_p, e_z, field, even, layers)
    twists(field, twist, edge, layers, size_y)

    def one(layer, carry):
        for y in range(0, size_y, ROWS):
            rows = slice(y, y + ROWS)

            def source(part, comp):
                return src[layer, rows] if part == 1 and comp == 0 else None

            new = relaxed(field, twist, layer, y, size_y, wave, sigma_h[layer, rows], sigma_v[layer, rows], source)
            for part in range(2):
                for comp in range(3):
                    e_out[layer, part, comp, rows] = new[part][comp]
        return carry

    lax.fori_loop(0, layers, one, 0)

    def inner(layer, carry):
        add_rhs(layer, e_out, (layer,), a_part, observed, wave, sigma_h, sigma_v, a_out, (layer,), size_y, None)
        return carry

    lax.fori_loop(1, layers - 1, inner, 0)


def add_rhs(layer, new, at, a_part, observed, wave, sigma_h, sigma_v, a_out, out_at, size_y, extra):
    for y in range(0, size_y, ROWS):
        rows = slice(y, y + ROWS)
        sides = (factors(sigma_h[layer, rows], wave), factors(sigma_v[layer, rows], wave))
        add = extra(y) if extra is not None else None
        for comp in range(3):
            _, four, coup = sides[0] if comp < 2 else sides[1]
            br = rhs_of(0, new[at + (0, comp, rows)], observed[0, comp, layer, rows].astype(jnp.float32))
            bi = rhs_of(1, new[at + (1, comp, rows)], observed[1, comp, layer, rows].astype(jnp.float32))
            real = a_part[layer, 0, comp, rows] + (four * br + coup * bi)
            imag = a_part[layer, 1, comp, rows] + (four * bi - coup * br)
            if add is not None:
                real = real + add[0][comp]
                imag = imag + add[1][comp]
            a_out[out_at + (0, comp, rows)] = real
            a_out[out_at + (1, comp, rows)] = imag


def third_faces_kernel(
    side, wave_ref, e_halo, a_halo, e_part, a_part, observed, sigma_h, sigma_v, e_face, a_face, send
):
    _, even = position("gx")
    layers, size_y, _ = sigma_h.shape
    layer, right = side_layer(side, even, layers - 1)
    wave = wave_ref[...]
    for y in range(0, size_y, ROWS):
        rows = slice(y, y + ROWS)
        add = fix(e_halo, y, right, wave, sigma_h[layer, rows], sigma_v[layer, rows], size_y)
        for part in range(2):
            for comp in range(3):
                e_face[part, comp, rows] = e_part[layer, part, comp, rows] + add[part][comp]

    def extra(y):
        rows = slice(y, y + ROWS)
        return fix(a_halo, y, right, wave, sigma_h[layer, rows], sigma_v[layer, rows], size_y)

    add_rhs(layer, e_face, (), a_part, observed, wave, sigma_h, sigma_v, a_face, (), size_y, extra)
    write_faces(a_face, send, right, size_y)


def grad_rows(wave, field, adjoint):
    terms = [adjoint[0][comp] * field[1][comp] + adjoint[1][comp] * field[0][comp] for comp in range(3)]
    return wave * (terms[0] + terms[1]), wave * terms[2]


def put_rows(out, place, y, pair, share):
    for which in range(2):
        for k in range(ROWS // share):
            out[y // share + k, which, place] = pair[which][k * share : (k + 1) * share]


def last_sweep_kernel(
    wave_ref, e_body, e_p, e_z, a_body, a_p, a_z, observed, sigma_h, sigma_v, final, faces, grad, field, twist
):
    index, even = position("gx")
    layers, size_y, _ = sigma_h.shape
    share = grad.shape[3]
    wave = wave_ref[...]
    edge = jnp.where(index > 0, 1.0, 0.0)
    sides = [side_layer(side, even, layers - 1)[0] for side in range(2)]
    for part in range(2):
        for comp in range(3):
            for layer in range(1, layers - 1):
                final[part, comp, layer] = e_body[layer, part, comp]
            final[part, comp, sides[0]] = e_p[part, comp]
            final[part, comp, sides[1]] = e_z[part, comp]
    zero_layer(field, layers, size_y)
    gather_layers(a_body, a_p, a_z, field, even, layers)
    twists(field, twist, edge, layers, size_y)

    def sweep(layer, y):
        rows = slice(y, y + ROWS)
        now = [[final[part, comp, layer, rows] for comp in range(3)] for part in range(2)]

        def source(part, comp):
            return rhs_of(part, now[part][comp], observed[part, comp, layer, rows].astype(jnp.float32))

        return now, relaxed(field, twist, layer, y, size_y, wave, sigma_h[layer, rows], sigma_v[layer, rows], source)

    def inner(layer, carry):
        for y in range(0, size_y, ROWS):
            now, new = sweep(layer, y)
            put_rows(grad, layer - 1, y, grad_rows(wave, now, new), share)
        return carry

    lax.fori_loop(1, layers - 1, inner, 0)

    def outer(side, carry):
        layer = jnp.where(side == 0, sides[0], sides[1])
        for y in range(0, size_y, ROWS):
            _, new = sweep(layer, y)
            for part in range(2):
                for comp in range(3):
                    faces[side, part, comp, y : y + ROWS] = new[part][comp]
        return carry

    lax.fori_loop(0, 2, outer, 0)


def gradient_kernel(wave_ref, halo_p, halo_z, e_p, e_z, faces, inner, sigma_h, sigma_v, grad):
    _, even = position("gx")
    layers, size_y, _ = sigma_h.shape
    share = grad.shape[3]
    wave = wave_ref[...]
    for layer in range(1, layers - 1):
        for which in range(2):
            grad[:, which, layer] = inner[:, which, layer - 1]
    for side, (halo, now) in enumerate(((halo_p, e_p), (halo_z, e_z))):
        layer, right = side_layer(side, even, layers - 1)
        for y in range(0, size_y, ROWS):
            rows = slice(y, y + ROWS)
            add = fix(halo, y, right, wave, sigma_h[layer, rows], sigma_v[layer, rows], size_y)
            new = [[faces[side, part, comp, rows] + add[part][comp] for comp in range(3)] for part in range(2)]
            old = [[now[part, comp, rows] for comp in range(3)] for part in range(2)]
            put_rows(grad, layer, y, grad_rows(wave, old, new), share)


def call(kernel, name, specs, outs, scratch=()):
    return pl.pallas_call(
        kernel,
        name=name,
        out_shape=tuple(jax.ShapeDtypeStruct(shape, jnp.float32) for shape in outs),
        in_specs=specs,
        out_specs=tuple(VMEM for _ in outs),
        scratch_shapes=[s if not isinstance(s, tuple) else pltpu.VMEM(s, jnp.float32) for s in scratch],
        compiler_params=pltpu.CompilerParams(vmem_limit_bytes=24 << 20),
    )


def on_device(
    sigma_h, sigma_v, wave_scale, field_start, adjoint_start, observed, tx_count, tx_cells
):
    layers, size_y, size_z = sigma_h.shape
    slabs = lax.axis_size("gx")
    freqs = lax.axis_size("freq")
    share = size_y // freqs
    start = field_start[0]
    adjoint = adjoint_start[0]
    seen = observed[0]
    wave = wave_scale[None]

    ends = (
        [(i, i + 1) for i in range(0, slabs - 1, 2)],
        [(i, i + 1) for i in range(1, slabs - 1, 2)],
    )
    swaps = [pairs + [(b, a) for a, b in pairs] for pairs in ends]

    def swap(values, side):
        return lax.ppermute(values, "gx", swaps[side])

    plane = (size_y, size_z)
    half = (2, 2) + plane
    face = (2, 3) + plane
    body = (layers,) + face
    more = (layers + 1,) + face

    e_p, e_z = call(faces_kernel, "first_faces", [VMEM], [half] * 2, [face])(start)
    e_p_in = swap(e_p, 0)
    a_p, a_z = call(faces_kernel, "adjoint_faces", [VMEM], [half] * 2, [face])(adjoint)
    (src,) = call(source_kernel, "source", [VMEM] * 3, [(layers,) + plane])(
        wave, tx_count[None], tx_cells[None]
    )
    e_z, a_p, a_z, src, e1_start = lax.optimization_barrier((e_z, a_p, a_z, src, start))
    e_z_in = swap(e_z, 1)
    (e1,) = call(first_sweep_kernel, "first_sweep", [VMEM] * 5, [body], [more, more])(
        wave, src, e1_start, sigma_h, sigma_v
    )

    def second(side, halo):
        return call(
            lambda *refs: second_faces_kernel(side, *refs),
            "second_faces_%d" % side,
            [VMEM] * 5,
            [face, half],
        )(wave, halo, e1, sigma_h, sigma_v)

    e1_p, e1_p_out = second(0, e_p_in)
    e1_p_in = swap(e1_p_out, 0)
    adjoint, e1_p = lax.optimization_barrier((adjoint, e1_p))
    (a1,) = call(first_adjoint_kernel, "first_adjoint", [VMEM] * 4, [body], [more, more])(
        wave, adjoint, sigma_h, sigma_v
    )
    a1, e_z_in = lax.optimization_barrier((a1, e_z_in))
    e1_z, e1_z_out = second(1, e_z_in)
    a_p, e1_z_out = lax.optimization_barrier((a_p, e1_z_out))
    e1_z_in = swap(e1_z_out, 1)
    a_p_in = swap(a_p, 0)
    e1_z, e1_z_in, e1_p_in = lax.optimization_barrier((e1_z, e1_z_in, e1_p_in))
    e2, a1_body = call(
        second_sweep_kernel, "second_sweep", [VMEM] * 9, [body, body], [more, more]
    )(wave, e1, e1_p, e1_z, a1, src, seen, sigma_h, sigma_v)
    e2, a_z = lax.optimization_barrier((e2, a_z))
    a_z_in = swap(a_z, 1)

    def third(side, e_halo, a_halo):
        return call(
            lambda *refs: third_faces_kernel(side, *refs),
            "third_faces_%d" % side,
            [VMEM] * 8,
            [face, face, half],
        )(wave, e_halo, a_halo, e2, a1, seen, sigma_h, sigma_v)

    e2_p, a1_p, a1_p_out = third(0, e1_p_in, a_p_in)
    a1_p_in = swap(a1_p_out, 0)
    a1_p, a_z_in = lax.optimization_barrier((a1_p, a_z_in))
    e2_z, a1_z, a1_z_out = third(1, e1_z_in, a_z_in)
    a1_z_in = swap(a1_z_out, 1)
    inner_blocks = (freqs, 2, layers - 2, share, size_z)
    blocks = (freqs, 2, layers, share, size_z)
    final, faces, inner = call(
        last_sweep_kernel,
        "last_sweep",
        [VMEM] * 10,
        [(2, 3, layers) + plane, (2,) + face, inner_blocks],
        [more, more],
    )(wave, e2, e2_p, e2_z, a1_body, a1_p, a1_z, seen, sigma_h, sigma_v)
    faces, a1_p_in = lax.optimization_barrier((faces, a1_p_in))
    (terms,) = call(gradient_kernel, "gradient", [VMEM] * 9, [blocks])(
        wave, a1_p_in, a1_z_in, e2_p, e2_z, faces, inner, sigma_h, sigma_v
    )
    gathered = lax.all_to_all(terms, "freq", 0, 0)
    return (jnp.sum(gathered, axis=0), final[None])


def solution(mesh):
    placed = (
        P("gx", None, None),
        P("gx", None, None),
        P("freq"),
        P("freq", None, None, "gx", None, None),
        P("freq", None, None, "gx", None, None),
        P("freq", None, None, "gx", None, None),
        P(),
        P(),
    )
    return jax.shard_map(
        on_device,
        mesh=mesh,
        in_specs=placed,
        out_specs=(P(None, "gx", "freq", None), P("freq", None, None, "gx", None, None)),
        check_vma=False,
    )
```

```python
import jax
import jax.numpy as jnp
from jax import lax
from jax.experimental import pallas as pl
from jax.experimental.pallas import tpu as pltpu
from jax.sharding import PartitionSpec as P

ITERS = 2
THETA = 0.5
SOURCE_GAIN = 8.0
ROWS = 8

VMEM = pl.BlockSpec(memory_space=pltpu.VMEM)


def position(axis):
    index = lax.axis_index(axis)
    even = 1 - lax.rem(index, 2)
    return index, even


def side_layer(side, even, last):
    right = even if side == 0 else 1 - even
    return last * right, right.astype(jnp.float32)


def lane_of(shape):
    return lax.broadcasted_iota(jnp.int32, shape, len(shape) - 1)


def next_z(values):
    size = values.shape[-1]
    moved = pltpu.roll(values, size - 1, 1)
    return jnp.where(lane_of(values.shape) == size - 1, 0.0, moved)


def last_z(values):
    moved = pltpu.roll(values, 1, 1)
    return jnp.where(lane_of(values.shape) == 0, 0.0, moved)


def factors(sigma, wave):
    coupling = wave * sigma
    inverse = THETA / (16.0 + coupling * coupling)
    return coupling, 4.0 * inverse, coupling * inverse


def chunks(size_y):
    return [slice(y, y + ROWS) for y in range(0, size_y, ROWS)]


def behind_row(ref, index, y, size_y):
    now = ref[index + (slice(y, y + ROWS),)]
    if y == 0:
        row = lax.broadcasted_iota(jnp.int32, now.shape, 0)
        return now, jnp.where(row == 0, 0.0, pltpu.roll(now, 1, 0))
    return now, ref[index + (slice(y - 1, y - 1 + ROWS),)]


def ahead_row(ref, index, y, size_y):
    now = ref[index + (slice(y, y + ROWS),)]
    if y + ROWS == size_y:
        row = lax.broadcasted_iota(jnp.int32, now.shape, 0)
        return now, jnp.where(row == ROWS - 1, 0.0, pltpu.roll(now, ROWS - 1, 0))
    return now, ref[index + (slice(y + 1, y + 1 + ROWS),)]


def write_faces(face, out, right, size_y):
    for part in range(2):
        for y in range(0, size_y, ROWS):
            rows = slice(y, y + ROWS)
            ex, ex_next = ahead_row(face, (part, 0), y, size_y)
            out[part, 0, rows] = face[part, 1, rows] + right * (ex_next - ex)
            out[part, 1, rows] = face[part, 2, rows] + right * (next_z(ex) - ex)


def fix(halo, y, right, wave, sig_h, sig_v, size_y):
    _, h_four, h_coup = factors(sig_h, wave)
    _, v_four, v_coup = factors(sig_v, wave)
    extra = []
    for part in range(2):
        u, u_last = behind_row(halo, (part, 0), y, size_y)
        v = halo[part, 1, y : y + ROWS]
        extra.append((right * ((last_z(v) - v) - (u - u_last)), u, v))
    real, imag = [], []
    for comp in range(3):
        four, coup = (h_four, h_coup) if comp < 2 else (v_four, v_coup)
        real.append(four * extra[0][comp] + coup * extra[1][comp])
        imag.append(four * extra[1][comp] - coup * extra[0][comp])
    return real, imag


def twists(field, twist, edge, layers, size_y):
    def one(layer, carry):
        for part in range(2):
            for y in range(0, size_y, ROWS):
                rows = slice(y, y + ROWS)
                ex, ex_next = ahead_row(field, (layer, part, 0), y, size_y)
                ey = field[layer, part, 1, rows]
                ez, ez_next = ahead_row(field, (layer, part, 2), y, size_y)
                ey_right = field[layer + 1, part, 1, rows]
                ez_right = field[layer + 1, part, 2, rows]
                twist[layer + 1, part, 0, rows] = (ez_next - ez) - (next_z(ey) - ey)
                twist[layer + 1, part, 1, rows] = (next_z(ex) - ex) - (ez_right - ez)
                twist[layer + 1, part, 2, rows] = (ey_right - ey) - (ex_next - ex)
        return carry

    lax.fori_loop(0, layers, one, 0)
    for part in range(2):
        for rows in chunks(size_y):
            twist[0, part, 1, rows] = -edge * field[0, part, 2, rows]
            twist[0, part, 2, rows] = edge * field[0, part, 1, rows]


def curled(twist, layer, y, size_y):
    rows = slice(y, y + ROWS)
    result = []
    for part in range(2):
        hx, hx_last = behind_row(twist, (layer + 1, part, 0), y, size_y)
        hz, hz_last = behind_row(twist, (layer + 1, part, 2), y, size_y)
        hy = twist[layer + 1, part, 1, rows]
        hy_left = twist[layer, part, 1, rows]
        hz_left = twist[layer, part, 2, rows]
        result.append(
            (
                (hz - hz_last) - (hy - last_z(hy)),
                (hx - last_z(hx)) - (hz - hz_left),
                (hy - hy_left) - (hx - hx_last),
            )
        )
    return result


def relaxed(field, twist, layer, y, size_y, wave, sig_h, sig_v, source):
    rows = slice(y, y + ROWS)
    sides = (factors(sig_h, wave), factors(sig_v, wave))
    curl = curled(twist, layer, y, size_y)
    real, imag = [], []
    for comp in range(3):
        coupling, four, coup = sides[0] if comp < 2 else sides[1]
        er = field[layer, 0, comp, rows]
        ei = field[layer, 1, comp, rows]
        rr = coupling * ei - curl[0][comp]
        ri = -(coupling * er) - curl[1][comp]
        br, bi = source(0, comp), source(1, comp)
        if br is not None:
            rr = rr + br
        if bi is not None:
            ri = ri + bi
        real.append(er + (four * rr + coup * ri))
        imag.append(ei + (four * ri - coup * rr))
    return real, imag


def zero_layer(field, layer, size_y):
    for part in range(2):
        for comp in (1, 2):
            for rows in chunks(size_y):
                field[layer, part, comp, rows] = jnp.zeros((ROWS, field.shape[-1]), jnp.float32)


def widen(start, field, layers, size_y):
    for layer in range(layers):
        for part in range(2):
            for comp in range(3):
                field[layer, part, comp] = start[part, comp, layer].astype(jnp.float32)


def faces_kernel(values, p_send, z_send, face):
    _, even = position("gx")
    faces_of(values, 0, even, face, p_send)
    faces_of(values, 1, even, face, z_send)


def faces_of(values, side, even, face, out):
    layers, size_y = values.shape[2], values.shape[3]
    layer, right = side_layer(side, even, layers - 1)
    for part in range(2):
        for comp in range(3):
            face[part, comp] = values[part, comp, layer].astype(jnp.float32)
    write_faces(face, out, right, size_y)


def source_kernel(wave_ref, count_ref, cells_ref, src):
    index, _ = position("gx")
    layers, size_y, _ = src.shape
    add_slots(wave_ref[...], count_ref[...], cells_ref[...], index * (layers * size_y), src)


def first_sweep_kernel(wave_ref, src, start, sigma_h, sigma_v, e_out, field, twist):
    index, _ = position("gx")
    layers, size_y, size_z = sigma_h.shape
    wave = wave_ref[...]
    edge = jnp.where(index > 0, 1.0, 0.0)

    def source(part, comp, layer, rows):
        return src[layer, rows] if part == 1 and comp == 0 else None

    zero_layer(field, layers, size_y)
    whole_sweep(start, field, twist, edge, wave, sigma_h, sigma_v, e_out, source)


def add_slots(wave, count, cells, first, src):
    layers, size_y, size_z = src.shape
    slots = cells.shape[1]
    shift = size_z.bit_length() - 1
    assert size_z == 1 << shift
    row = lax.shift_right_logical(cells, shift) - first
    spot = jnp.bitwise_and(cells, size_z - 1)
    live = lane_of((1, slots)) < count
    row = jnp.where(live, row, -1)
    at_row = lax.broadcasted_iota(jnp.int32, (layers * size_y, slots), 0) == row
    at_spot = lax.broadcasted_iota(jnp.int32, (size_z, slots), 0) == spot
    counts = lax.dot_general(
        jnp.where(at_row, 1.0, 0.0).astype(jnp.bfloat16),
        jnp.where(at_spot, 1.0, 0.0).astype(jnp.bfloat16),
        (((1,), (1,)), ((), ())),
        preferred_element_type=jnp.float32,
    )
    gain = SOURCE_GAIN * wave
    for layer in range(layers):
        src[layer] = gain * counts[layer * size_y : (layer + 1) * size_y]


def first_adjoint_kernel(wave_ref, adjoint, sigma_h, sigma_v, a_out, field, twist):
    index, _ = position("gx")
    layers, size_y, _ = sigma_h.shape
    edge = jnp.where(index > 0, 1.0, 0.0)
    zero_layer(field, layers, size_y)
    none = lambda part, comp, layer, rows: None
    whole_sweep(adjoint, field, twist, edge, wave_ref[...], sigma_h, sigma_v, a_out, none)


def whole_sweep(values, field, twist, edge, wave, sigma_h, sigma_v, out, source):
    layers, size_y, _ = sigma_h.shape
    widen(values, field, layers, size_y)
    twists(field, twist, edge, layers, size_y)

    def one(layer, carry):
        for y in range(0, size_y, ROWS):
            rows = slice(y, y + ROWS)
            at = lambda part, comp: source(part, comp, layer, rows)
            new = relaxed(field, twist, layer, y, size_y, wave, sigma_h[layer, rows], sigma_v[layer, rows], at)
            for part in range(2):
                for comp in range(3):
                    out[layer, part, comp, rows] = new[part][comp]
        return carry

    lax.fori_loop(0, layers, one, 0)


def second_faces_kernel(side, wave_ref, halo, part_new, sigma_h, sigma_v, face, send):
    _, even = position("gx")
    layers, size_y, _ = sigma_h.shape
    layer, right = side_layer(side, even, layers - 1)
    wave = wave_ref[...]
    for y in range(0, size_y, ROWS):
        rows = slice(y, y + ROWS)
        add = fix(halo, y, right, wave, sigma_h[layer, rows], sigma_v[layer, rows], size_y)
        for part in range(2):
            for comp in range(3):
                face[part, comp, rows] = part_new[layer, part, comp, rows] + add[part][comp]
    write_faces(face, send, right, size_y)


def gather_layers(body, face_p, face_z, field, even, layers):
    p_layer, _ = side_layer(0, even, layers - 1)
    z_layer, _ = side_layer(1, even, layers - 1)
    for part in range(2):
        for comp in range(3):
            for layer in range(1, layers - 1):
                field[layer, part, comp] = body[layer, part, comp]
            field[p_layer, part, comp] = face_p[part, comp]
            field[z_layer, part, comp] = face_z[part, comp]


def rhs_of(part, new, seen):
    return new - seen if part == 0 else seen - new


def second_sweep_kernel(
    wave_ref, e_body, e_p, e_z, a_part, src, observed, sigma_h, sigma_v, e_out, a_out, field, twist
):
    index, even = position("gx")
    layers, size_y, _ = sigma_h.shape
    wave = wave_ref[...]
    edge = jnp.where(index > 0, 1.0, 0.0)
    zero_layer(field, layers, size_y)
    gather_layers(e_body, e_p, e_z, field, even, layers)
    twists(field, twist, edge, layers, size_y)

    def one(layer, carry):
        for y in range(0, size_y, ROWS):
            rows = slice(y, y + ROWS)

            def source(part, comp):
                return src[layer, rows] if part == 1 and comp == 0 else None

            new = relaxed(field, twist, layer, y, size_y, wave, sigma_h[layer, rows], sigma_v[layer, rows], source)
            for part in range(2):
                for comp in range(3):
                    e_out[layer, part, comp, rows] = new[part][comp]
        return carry

    lax.fori_loop(0, layers, one, 0)

    def inner(layer, carry):
        add_rhs(layer, e_out, (layer,), a_part, observed, wave, sigma_h, sigma_v, a_out, (layer,), size_y, None)
        return carry

    lax.fori_loop(1, layers - 1, inner, 0)


def add_rhs(layer, new, at, a_part, observed, wave, sigma_h, sigma_v, a_out, out_at, size_y, extra):
    for y in range(0, size_y, ROWS):
        rows = slice(y, y + ROWS)
        sides = (factors(sigma_h[layer, rows], wave), factors(sigma_v[layer, rows], wave))
        add = extra(y) if extra is not None else None
        for comp in range(3):
            _, four, coup = sides[0] if comp < 2 else sides[1]
            br = rhs_of(0, new[at + (0, comp, rows)], observed[0, comp, layer, rows].astype(jnp.float32))
            bi = rhs_of(1, new[at + (1, comp, rows)], observed[1, comp, layer, rows].astype(jnp.float32))
            real = a_part[layer, 0, comp, rows] + (four * br + coup * bi)
            imag = a_part[layer, 1, comp, rows] + (four * bi - coup * br)
            if add is not None:
                real = real + add[0][comp]
                imag = imag + add[1][comp]
            a_out[out_at + (0, comp, rows)] = real
            a_out[out_at + (1, comp, rows)] = imag


def third_faces_kernel(
    side, wave_ref, e_halo, a_halo, e_part, a_part, observed, sigma_h, sigma_v, e_face, a_face, send
):
    _, even = position("gx")
    layers, size_y, _ = sigma_h.shape
    layer, right = side_layer(side, even, layers - 1)
    wave = wave_ref[...]
    for y in range(0, size_y, ROWS):
        rows = slice(y, y + ROWS)
        add = fix(e_halo, y, right, wave, sigma_h[layer, rows], sigma_v[layer, rows], size_y)
        for part in range(2):
            for comp in range(3):
                e_face[part, comp, rows] = e_part[layer, part, comp, rows] + add[part][comp]

    def extra(y):
        rows = slice(y, y + ROWS)
        return fix(a_halo, y, right, wave, sigma_h[layer, rows], sigma_v[layer, rows], size_y)

    add_rhs(layer, e_face, (), a_part, observed, wave, sigma_h, sigma_v, a_face, (), size_y, extra)
    write_faces(a_face, send, right, size_y)


def grad_rows(wave, field, adjoint):
    terms = [adjoint[0][comp] * field[1][comp] + adjoint[1][comp] * field[0][comp] for comp in range(3)]
    return wave * (terms[0] + terms[1]), wave * terms[2]


def put_rows(halves, place, y, pair, share, core):
    for which in range(2):
        for k in range(ROWS // share):
            block = y // share + k
            half = core if block % 2 == 0 else 1 - core
            halves[half, block // 2, which, place] = pair[which][k * share : (k + 1) * share]


def last_sweep_kernel(
    wave_ref, e_body, e_p, e_z, a_body, a_p, a_z, observed, sigma_h, sigma_v,
    final, faces, keep, send, field, twist, halves,
):
    index, even = position("gx")
    layers, size_y, _ = sigma_h.shape
    share = keep.shape[3]
    core = lax.rem(lax.axis_index("freq"), 2)
    wave = wave_ref[...]
    edge = jnp.where(index > 0, 1.0, 0.0)
    sides = [side_layer(side, even, layers - 1)[0] for side in range(2)]
    for part in range(2):
        for comp in range(3):
            for layer in range(1, layers - 1):
                final[part, comp, layer] = e_body[layer, part, comp]
            final[part, comp, sides[0]] = e_p[part, comp]
            final[part, comp, sides[1]] = e_z[part, comp]
    zero_layer(field, layers, size_y)
    gather_layers(a_body, a_p, a_z, field, even, layers)
    twists(field, twist, edge, layers, size_y)

    def sweep(layer, y):
        rows = slice(y, y + ROWS)
        now = [[final[part, comp, layer, rows] for comp in range(3)] for part in range(2)]

        def source(part, comp):
            return rhs_of(part, now[part][comp], observed[part, comp, layer, rows].astype(jnp.float32))

        return now, relaxed(field, twist, layer, y, size_y, wave, sigma_h[layer, rows], sigma_v[layer, rows], source)

    def inner(layer, carry):
        for y in range(0, size_y, ROWS):
            now, new = sweep(layer, y)
            put_rows(halves, layer - 1, y, grad_rows(wave, now, new), share, core)
        return carry

    lax.fori_loop(1, layers - 1, inner, 0)
    keep[...] = halves[0]
    send[...] = halves[1]

    def outer(side, carry):
        layer = jnp.where(side == 0, sides[0], sides[1])
        for y in range(0, size_y, ROWS):
            _, new = sweep(layer, y)
            for part in range(2):
                for comp in range(3):
                    faces[side, part, comp, y : y + ROWS] = new[part][comp]
        return carry

    lax.fori_loop(0, 2, outer, 0)


def gradient_kernel(wave_ref, halo_p, halo_z, e_p, e_z, faces, sigma_h, sigma_v, keep, send, halves):
    _, even = position("gx")
    layers, size_y, _ = sigma_h.shape
    share = keep.shape[3]
    core = lax.rem(lax.axis_index("freq"), 2)
    wave = wave_ref[...]
    for side, (halo, now) in enumerate(((halo_p, e_p), (halo_z, e_z))):
        layer, right = side_layer(side, even, layers - 1)
        place = right.astype(jnp.int32)
        for y in range(0, size_y, ROWS):
            rows = slice(y, y + ROWS)
            add = fix(halo, y, right, wave, sigma_h[layer, rows], sigma_v[layer, rows], size_y)
            new = [[faces[side, part, comp, rows] + add[part][comp] for comp in range(3)] for part in range(2)]
            old = [[now[part, comp, rows] for comp in range(3)] for part in range(2)]
            put_rows(halves, place, y, grad_rows(wave, old, new), share, core)
    keep[...] = halves[0]
    send[...] = halves[1]


def pair_sum_kernel(inner, inner_other, outer, outer_other, terms):
    between = inner.shape[2]
    for which in range(2):
        for k in range(between):
            terms[:, which, k + 1] = inner[:, which, k] + inner_other[:, which, k]
        for k, layer in ((0, 0), (1, between + 1)):
            terms[:, which, layer] = outer[:, which, k] + outer_other[:, which, k]


def call(kernel, name, specs, outs, scratch=()):
    return pl.pallas_call(
        kernel,
        name=name,
        out_shape=tuple(jax.ShapeDtypeStruct(shape, jnp.float32) for shape in outs),
        in_specs=specs,
        out_specs=tuple(VMEM for _ in outs),
        scratch_shapes=[s if not isinstance(s, tuple) else pltpu.VMEM(s, jnp.float32) for s in scratch],
        compiler_params=pltpu.CompilerParams(vmem_limit_bytes=24 << 20),
    )


def on_device(
    sigma_h, sigma_v, wave_scale, field_start, adjoint_start, observed, tx_count, tx_cells
):
    layers, size_y, size_z = sigma_h.shape
    slabs = lax.axis_size("gx")
    freqs = lax.axis_size("freq")
    share = size_y // freqs
    start = field_start[0]
    adjoint = adjoint_start[0]
    seen = observed[0]
    wave = wave_scale[None]

    ends = (
        [(i, i + 1) for i in range(0, slabs - 1, 2)],
        [(i, i + 1) for i in range(1, slabs - 1, 2)],
    )
    swaps = [pairs + [(b, a) for a, b in pairs] for pairs in ends]

    def swap(values, side):
        return lax.ppermute(values, "gx", swaps[side])

    plane = (size_y, size_z)
    half = (2, 2) + plane
    face = (2, 3) + plane
    body = (layers,) + face
    more = (layers + 1,) + face

    e_p, e_z = call(faces_kernel, "first_faces", [VMEM], [half] * 2, [face])(start)
    e_p_in = swap(e_p, 0)
    a_p, a_z = call(faces_kernel, "adjoint_faces", [VMEM], [half] * 2, [face])(adjoint)
    (src,) = call(source_kernel, "source", [VMEM] * 3, [(layers,) + plane])(
        wave, tx_count[None], tx_cells[None]
    )
    e_z, a_p, a_z, src, e1_start = lax.optimization_barrier((e_z, a_p, a_z, src, start))
    e_z_in = swap(e_z, 1)
    (e1,) = call(first_sweep_kernel, "first_sweep", [VMEM] * 5, [body], [more, more])(
        wave, src, e1_start, sigma_h, sigma_v
    )

    def second(side, halo):
        return call(
            lambda *refs: second_faces_kernel(side, *refs),
            "second_faces_%d" % side,
            [VMEM] * 5,
            [face, half],
        )(wave, halo, e1, sigma_h, sigma_v)

    e1_p, e1_p_out = second(0, e_p_in)
    e1_p_in = swap(e1_p_out, 0)
    adjoint, e1_p = lax.optimization_barrier((adjoint, e1_p))
    (a1,) = call(first_adjoint_kernel, "first_adjoint", [VMEM] * 4, [body], [more, more])(
        wave, adjoint, sigma_h, sigma_v
    )
    a1, e_z_in = lax.optimization_barrier((a1, e_z_in))
    e1_z, e1_z_out = second(1, e_z_in)
    a_p, e1_z_out = lax.optimization_barrier((a_p, e1_z_out))
    e1_z_in = swap(e1_z_out, 1)
    a_p_in = swap(a_p, 0)
    e1_z, e1_z_in, e1_p_in = lax.optimization_barrier((e1_z, e1_z_in, e1_p_in))
    e2, a1_body = call(
        second_sweep_kernel, "second_sweep", [VMEM] * 9, [body, body], [more, more]
    )(wave, e1, e1_p, e1_z, a1, src, seen, sigma_h, sigma_v)
    e2, a_z = lax.optimization_barrier((e2, a_z))
    a_z_in = swap(a_z, 1)

    def third(side, e_halo, a_halo):
        return call(
            lambda *refs: third_faces_kernel(side, *refs),
            "third_faces_%d" % side,
            [VMEM] * 8,
            [face, face, half],
        )(wave, e_halo, a_halo, e2, a1, seen, sigma_h, sigma_v)

    e2_p, a1_p, a1_p_out = third(0, e1_p_in, a_p_in)
    a1_p_in = swap(a1_p_out, 0)
    a1_p, a_z_in = lax.optimization_barrier((a1_p, a_z_in))
    e2_z, a1_z, a1_z_out = third(1, e1_z_in, a_z_in)
    a1_z_in = swap(a1_z_out, 1)
    half_blocks = (freqs // 2, 2, 2, share, size_z)
    blocks = (freqs // 2, 2, layers, share, size_z)
    cores = [(i, i ^ 1) for i in range(freqs)]
    final, faces, inner, inner_out = call(
        last_sweep_kernel,
        "last_sweep",
        [VMEM] * 10,
        [(2, 3, layers) + plane, (2,) + face, half_blocks, half_blocks],
        [more, more, (2,) + half_blocks],
    )(wave, e2, e2_p, e2_z, a1_body, a1_p, a1_z, seen, sigma_h, sigma_v)
    faces, a1_p_in = lax.optimization_barrier((faces, a1_p_in))
    inner_in = lax.ppermute(inner_out, "freq", cores)
    a1_z_in, inner_in = lax.optimization_barrier((a1_z_in, inner_in))
    outer, outer_out = call(
        gradient_kernel, "gradient", [VMEM] * 8, [half_blocks] * 2, [(2,) + half_blocks]
    )(wave, a1_p_in, a1_z_in, e2_p, e2_z, faces, sigma_h, sigma_v)
    outer_in = lax.ppermute(outer_out, "freq", cores)
    (terms,) = call(pair_sum_kernel, "pair_sum", [VMEM] * 4, [blocks])(inner, inner_in, outer, outer_in)
    groups = [list(range(core, freqs, 2)) for core in range(2)]
    gathered = lax.all_to_all(terms, "freq", 0, 0, axis_index_groups=groups)
    return (jnp.sum(gathered, axis=0), final[None])


def solution(mesh):
    placed = (
        P("gx", None, None),
        P("gx", None, None),
        P("freq"),
        P("freq", None, None, "gx", None, None),
        P("freq", None, None, "gx", None, None),
        P("freq", None, None, "gx", None, None),
        P(),
        P(),
    )
    return jax.shard_map(
        on_device,
        mesh=mesh,
        in_specs=placed,
        out_specs=(P(None, "gx", "freq", None), P("freq", None, None, "gx", None, None)),
        check_vma=False,
    )
```

```python
import jax
import jax.numpy as jnp
from jax import lax
from jax.experimental import pallas as pl
from jax.experimental.pallas import tpu as pltpu
from jax.sharding import PartitionSpec as P

ITERS = 2
THETA = 0.5
SOURCE_GAIN = 8.0
ROWS = 8

VMEM = pl.BlockSpec(memory_space=pltpu.VMEM)


def position(axis):
    index = lax.axis_index(axis)
    even = 1 - lax.rem(index, 2)
    return index, even


def side_layer(side, even, last):
    right = even if side == 0 else 1 - even
    return last * right, right.astype(jnp.float32)


def lane_of(shape):
    return lax.broadcasted_iota(jnp.int32, shape, len(shape) - 1)


def next_z(values):
    size = values.shape[-1]
    moved = pltpu.roll(values, size - 1, 1)
    return jnp.where(lane_of(values.shape) == size - 1, 0.0, moved)


def last_z(values):
    moved = pltpu.roll(values, 1, 1)
    return jnp.where(lane_of(values.shape) == 0, 0.0, moved)


def factors(sigma, wave):
    coupling = wave * sigma
    inverse = THETA / (16.0 + coupling * coupling)
    return coupling, 4.0 * inverse, coupling * inverse


def chunks(size_y):
    return [slice(y, y + ROWS) for y in range(0, size_y, ROWS)]


def behind_row(ref, index, y, size_y):
    now = ref[index + (slice(y, y + ROWS),)]
    if y == 0:
        row = lax.broadcasted_iota(jnp.int32, now.shape, 0)
        return now, jnp.where(row == 0, 0.0, pltpu.roll(now, 1, 0))
    return now, ref[index + (slice(y - 1, y - 1 + ROWS),)]


def ahead_row(ref, index, y, size_y):
    now = ref[index + (slice(y, y + ROWS),)]
    if y + ROWS == size_y:
        row = lax.broadcasted_iota(jnp.int32, now.shape, 0)
        return now, jnp.where(row == ROWS - 1, 0.0, pltpu.roll(now, ROWS - 1, 0))
    return now, ref[index + (slice(y + 1, y + 1 + ROWS),)]


def write_faces(face, out, right, size_y):
    for part in range(2):
        for y in range(0, size_y, ROWS):
            rows = slice(y, y + ROWS)
            ex, ex_next = ahead_row(face, (part, 0), y, size_y)
            out[part, 0, rows] = face[part, 1, rows] + right * (ex_next - ex)
            out[part, 1, rows] = face[part, 2, rows] + right * (next_z(ex) - ex)


def fix(halo, y, right, wave, sig_h, sig_v, size_y):
    _, h_four, h_coup = factors(sig_h, wave)
    _, v_four, v_coup = factors(sig_v, wave)
    extra = []
    for part in range(2):
        u, u_last = behind_row(halo, (part, 0), y, size_y)
        v = halo[part, 1, y : y + ROWS]
        extra.append((right * ((last_z(v) - v) - (u - u_last)), u, v))
    real, imag = [], []
    for comp in range(3):
        four, coup = (h_four, h_coup) if comp < 2 else (v_four, v_coup)
        real.append(four * extra[0][comp] + coup * extra[1][comp])
        imag.append(four * extra[1][comp] - coup * extra[0][comp])
    return real, imag


def twists(field, twist, edge, layers, size_y):
    def one(layer, carry):
        for part in range(2):
            for y in range(0, size_y, ROWS):
                rows = slice(y, y + ROWS)
                ex, ex_next = ahead_row(field, (layer, part, 0), y, size_y)
                ey = field[layer, part, 1, rows]
                ez, ez_next = ahead_row(field, (layer, part, 2), y, size_y)
                ey_right = field[layer + 1, part, 1, rows]
                ez_right = field[layer + 1, part, 2, rows]
                twist[layer + 1, part, 0, rows] = (ez_next - ez) - (next_z(ey) - ey)
                twist[layer + 1, part, 1, rows] = (next_z(ex) - ex) - (ez_right - ez)
                twist[layer + 1, part, 2, rows] = (ey_right - ey) - (ex_next - ex)
        return carry

    lax.fori_loop(0, layers, one, 0)
    for part in range(2):
        for rows in chunks(size_y):
            twist[0, part, 1, rows] = -edge * field[0, part, 2, rows]
            twist[0, part, 2, rows] = edge * field[0, part, 1, rows]


def curled(twist, layer, y, size_y):
    rows = slice(y, y + ROWS)
    result = []
    for part in range(2):
        hx, hx_last = behind_row(twist, (layer + 1, part, 0), y, size_y)
        hz, hz_last = behind_row(twist, (layer + 1, part, 2), y, size_y)
        hy = twist[layer + 1, part, 1, rows]
        hy_left = twist[layer, part, 1, rows]
        hz_left = twist[layer, part, 2, rows]
        result.append(
            (
                (hz - hz_last) - (hy - last_z(hy)),
                (hx - last_z(hx)) - (hz - hz_left),
                (hy - hy_left) - (hx - hx_last),
            )
        )
    return result


def relaxed(field, twist, layer, y, size_y, wave, sig_h, sig_v, source):
    rows = slice(y, y + ROWS)
    sides = (factors(sig_h, wave), factors(sig_v, wave))
    curl = curled(twist, layer, y, size_y)
    real, imag = [], []
    for comp in range(3):
        coupling, four, coup = sides[0] if comp < 2 else sides[1]
        er = field[layer, 0, comp, rows]
        ei = field[layer, 1, comp, rows]
        rr = coupling * ei - curl[0][comp]
        ri = -(coupling * er) - curl[1][comp]
        br, bi = source(0, comp), source(1, comp)
        if br is not None:
            rr = rr + br
        if bi is not None:
            ri = ri + bi
        real.append(er + (four * rr + coup * ri))
        imag.append(ei + (four * ri - coup * rr))
    return real, imag


def zero_layer(field, layer, size_y):
    for part in range(2):
        for comp in (1, 2):
            for rows in chunks(size_y):
                field[layer, part, comp, rows] = jnp.zeros((ROWS, field.shape[-1]), jnp.float32)


def widen(start, field, layers, size_y):
    for layer in range(layers):
        for part in range(2):
            for comp in range(3):
                field[layer, part, comp] = start[part, comp, layer].astype(jnp.float32)


def faces_kernel(values, p_send, z_send, face):
    _, even = position("gx")
    faces_of(values, 0, even, face, p_send)
    faces_of(values, 1, even, face, z_send)


def faces_of(values, side, even, face, out):
    layers, size_y = values.shape[2], values.shape[3]
    layer, right = side_layer(side, even, layers - 1)
    for part in range(2):
        for comp in range(3):
            face[part, comp] = values[part, comp, layer].astype(jnp.float32)
    write_faces(face, out, right, size_y)


def source_kernel(wave_ref, count_ref, cells_ref, src):
    index, _ = position("gx")
    layers, size_y, _ = src.shape
    add_slots(wave_ref[...], count_ref[...], cells_ref[...], index * (layers * size_y), src)


def first_sweep_kernel(wave_ref, src, start, sigma_h, sigma_v, e_out, field, twist):
    index, _ = position("gx")
    layers, size_y, size_z = sigma_h.shape
    wave = wave_ref[...]
    edge = jnp.where(index > 0, 1.0, 0.0)

    def source(part, comp, layer, rows):
        return src[layer, rows] if part == 1 and comp == 0 else None

    zero_layer(field, layers, size_y)
    whole_sweep(start, field, twist, edge, wave, sigma_h, sigma_v, e_out, source)


def add_slots(wave, count, cells, first, src):
    layers, size_y, size_z = src.shape
    slots = cells.shape[1]
    shift = size_z.bit_length() - 1
    assert size_z == 1 << shift
    row = lax.shift_right_logical(cells, shift) - first
    spot = jnp.bitwise_and(cells, size_z - 1)
    live = lane_of((1, slots)) < count
    row = jnp.where(live, row, -1)
    at_row = lax.broadcasted_iota(jnp.int32, (layers * size_y, slots), 0) == row
    at_spot = lax.broadcasted_iota(jnp.int32, (size_z, slots), 0) == spot
    counts = lax.dot_general(
        jnp.where(at_row, 1.0, 0.0).astype(jnp.bfloat16),
        jnp.where(at_spot, 1.0, 0.0).astype(jnp.bfloat16),
        (((1,), (1,)), ((), ())),
        preferred_element_type=jnp.float32,
    )
    gain = SOURCE_GAIN * wave
    for layer in range(layers):
        src[layer] = gain * counts[layer * size_y : (layer + 1) * size_y]


def first_adjoint_kernel(wave_ref, adjoint, sigma_h, sigma_v, a_out, field, twist):
    index, _ = position("gx")
    layers, size_y, _ = sigma_h.shape
    edge = jnp.where(index > 0, 1.0, 0.0)
    zero_layer(field, layers, size_y)
    none = lambda part, comp, layer, rows: None
    whole_sweep(adjoint, field, twist, edge, wave_ref[...], sigma_h, sigma_v, a_out, none)


def whole_sweep(values, field, twist, edge, wave, sigma_h, sigma_v, out, source):
    layers, size_y, _ = sigma_h.shape
    widen(values, field, layers, size_y)
    twists(field, twist, edge, layers, size_y)

    def one(layer, carry):
        for y in range(0, size_y, ROWS):
            rows = slice(y, y + ROWS)
            at = lambda part, comp: source(part, comp, layer, rows)
            new = relaxed(field, twist, layer, y, size_y, wave, sigma_h[layer, rows], sigma_v[layer, rows], at)
            for part in range(2):
                for comp in range(3):
                    out[layer, part, comp, rows] = new[part][comp]
        return carry

    lax.fori_loop(0, layers, one, 0)


def second_faces_kernel(side, wave_ref, halo, part_new, sigma_h, sigma_v, face, send):
    _, even = position("gx")
    layers, size_y, _ = sigma_h.shape
    layer, right = side_layer(side, even, layers - 1)
    wave = wave_ref[...]
    for y in range(0, size_y, ROWS):
        rows = slice(y, y + ROWS)
        add = fix(halo, y, right, wave, sigma_h[layer, rows], sigma_v[layer, rows], size_y)
        for part in range(2):
            for comp in range(3):
                face[part, comp, rows] = part_new[layer, part, comp, rows] + add[part][comp]
    write_faces(face, send, right, size_y)


def gather_layers(body, face_p, face_z, field, even, layers):
    p_layer, _ = side_layer(0, even, layers - 1)
    z_layer, _ = side_layer(1, even, layers - 1)
    for part in range(2):
        for comp in range(3):
            for layer in range(1, layers - 1):
                field[layer, part, comp] = body[layer, part, comp]
            field[p_layer, part, comp] = face_p[part, comp]
            field[z_layer, part, comp] = face_z[part, comp]


def rhs_of(part, new, seen):
    return new - seen if part == 0 else seen - new


def second_sweep_kernel(
    wave_ref, e_body, e_p, e_z, a_part, src, observed, sigma_h, sigma_v, e_out, a_out, field, twist
):
    index, even = position("gx")
    layers, size_y, _ = sigma_h.shape
    wave = wave_ref[...]
    edge = jnp.where(index > 0, 1.0, 0.0)
    zero_layer(field, layers, size_y)
    gather_layers(e_body, e_p, e_z, field, even, layers)
    twists(field, twist, edge, layers, size_y)

    def one(layer, carry):
        for y in range(0, size_y, ROWS):
            rows = slice(y, y + ROWS)

            def source(part, comp):
                return src[layer, rows] if part == 1 and comp == 0 else None

            new = relaxed(field, twist, layer, y, size_y, wave, sigma_h[layer, rows], sigma_v[layer, rows], source)
            for part in range(2):
                for comp in range(3):
                    e_out[layer, part, comp, rows] = new[part][comp]
        return carry

    lax.fori_loop(0, layers, one, 0)

    def inner(layer, carry):
        add_rhs(layer, e_out, (layer,), a_part, observed, wave, sigma_h, sigma_v, a_out, (layer,), size_y, None)
        return carry

    lax.fori_loop(1, layers - 1, inner, 0)


def add_rhs(layer, new, at, a_part, observed, wave, sigma_h, sigma_v, a_out, out_at, size_y, extra):
    for y in range(0, size_y, ROWS):
        rows = slice(y, y + ROWS)
        sides = (factors(sigma_h[layer, rows], wave), factors(sigma_v[layer, rows], wave))
        add = extra(y) if extra is not None else None
        for comp in range(3):
            _, four, coup = sides[0] if comp < 2 else sides[1]
            br = rhs_of(0, new[at + (0, comp, rows)], observed[0, comp, layer, rows].astype(jnp.float32))
            bi = rhs_of(1, new[at + (1, comp, rows)], observed[1, comp, layer, rows].astype(jnp.float32))
            real = a_part[layer, 0, comp, rows] + (four * br + coup * bi)
            imag = a_part[layer, 1, comp, rows] + (four * bi - coup * br)
            if add is not None:
                real = real + add[0][comp]
                imag = imag + add[1][comp]
            a_out[out_at + (0, comp, rows)] = real
            a_out[out_at + (1, comp, rows)] = imag


def third_faces_kernel(
    side, wave_ref, e_halo, a_halo, e_part, a_part, observed, sigma_h, sigma_v, e_face, a_face, send
):
    _, even = position("gx")
    layers, size_y, _ = sigma_h.shape
    layer, right = side_layer(side, even, layers - 1)
    wave = wave_ref[...]
    for y in range(0, size_y, ROWS):
        rows = slice(y, y + ROWS)
        add = fix(e_halo, y, right, wave, sigma_h[layer, rows], sigma_v[layer, rows], size_y)
        for part in range(2):
            for comp in range(3):
                e_face[part, comp, rows] = e_part[layer, part, comp, rows] + add[part][comp]

    def extra(y):
        rows = slice(y, y + ROWS)
        return fix(a_halo, y, right, wave, sigma_h[layer, rows], sigma_v[layer, rows], size_y)

    add_rhs(layer, e_face, (), a_part, observed, wave, sigma_h, sigma_v, a_face, (), size_y, extra)
    write_faces(a_face, send, right, size_y)


def grad_rows(wave, field, adjoint):
    terms = [adjoint[0][comp] * field[1][comp] + adjoint[1][comp] * field[0][comp] for comp in range(3)]
    return wave * (terms[0] + terms[1]), wave * terms[2]


def put_rows(out, place, y, pair, share):
    for which in range(2):
        for k in range(ROWS // share):
            out[y // share + k, which, place] = pair[which][k * share : (k + 1) * share]


def last_sweep_kernel(
    wave_ref, e_body, e_p, e_z, a_body, a_p, a_z, observed, sigma_h, sigma_v, final, faces, grad, field, twist
):
    index, even = position("gx")
    layers, size_y, _ = sigma_h.shape
    share = grad.shape[3]
    wave = wave_ref[...]
    edge = jnp.where(index > 0, 1.0, 0.0)
    sides = [side_layer(side, even, layers - 1)[0] for side in range(2)]
    for part in range(2):
        for comp in range(3):
            for layer in range(1, layers - 1):
                final[part, comp, layer] = e_body[layer, part, comp]
            final[part, comp, sides[0]] = e_p[part, comp]
            final[part, comp, sides[1]] = e_z[part, comp]
    zero_layer(field, layers, size_y)
    gather_layers(a_body, a_p, a_z, field, even, layers)
    twists(field, twist, edge, layers, size_y)

    def sweep(layer, y):
        rows = slice(y, y + ROWS)
        now = [[final[part, comp, layer, rows] for comp in range(3)] for part in range(2)]

        def source(part, comp):
            return rhs_of(part, now[part][comp], observed[part, comp, layer, rows].astype(jnp.float32))

        return now, relaxed(field, twist, layer, y, size_y, wave, sigma_h[layer, rows], sigma_v[layer, rows], source)

    def inner(layer, carry):
        for y in range(0, size_y, ROWS):
            now, new = sweep(layer, y)
            put_rows(grad, layer - 1, y, grad_rows(wave, now, new), share)
        return carry

    lax.fori_loop(1, layers - 1, inner, 0)

    def outer(side, carry):
        layer = jnp.where(side == 0, sides[0], sides[1])
        for y in range(0, size_y, ROWS):
            _, new = sweep(layer, y)
            for part in range(2):
                for comp in range(3):
                    faces[side, part, comp, y : y + ROWS] = new[part][comp]
        return carry

    lax.fori_loop(0, 2, outer, 0)


def gradient_kernel(wave_ref, halo_p, halo_z, e_p, e_z, faces, inner, sigma_h, sigma_v, grad):
    _, even = position("gx")
    layers, size_y, _ = sigma_h.shape
    share = grad.shape[3]
    wave = wave_ref[...]
    for layer in range(1, layers - 1):
        for which in range(2):
            grad[:, which, layer] = inner[:, which, layer - 1]
    for side, (halo, now) in enumerate(((halo_p, e_p), (halo_z, e_z))):
        layer, right = side_layer(side, even, layers - 1)
        for y in range(0, size_y, ROWS):
            rows = slice(y, y + ROWS)
            add = fix(halo, y, right, wave, sigma_h[layer, rows], sigma_v[layer, rows], size_y)
            new = [[faces[side, part, comp, rows] + add[part][comp] for comp in range(3)] for part in range(2)]
            old = [[now[part, comp, rows] for comp in range(3)] for part in range(2)]
            put_rows(grad, layer, y, grad_rows(wave, old, new), share)


def call(kernel, name, specs, outs, scratch=()):
    return pl.pallas_call(
        kernel,
        name=name,
        out_shape=tuple(jax.ShapeDtypeStruct(shape, jnp.float32) for shape in outs),
        in_specs=specs,
        out_specs=tuple(VMEM for _ in outs),
        scratch_shapes=[s if not isinstance(s, tuple) else pltpu.VMEM(s, jnp.float32) for s in scratch],
        compiler_params=pltpu.CompilerParams(vmem_limit_bytes=24 << 20),
    )


def on_device(
    sigma_h, sigma_v, wave_scale, field_start, adjoint_start, observed, tx_count, tx_cells
):
    layers, size_y, size_z = sigma_h.shape
    slabs = lax.axis_size("gx")
    freqs = lax.axis_size("freq")
    share = size_y // freqs
    start = field_start[0]
    adjoint = adjoint_start[0]
    seen = observed[0]
    wave = wave_scale[None]

    ends = (
        [(i, i + 1) for i in range(0, slabs - 1, 2)],
        [(i, i + 1) for i in range(1, slabs - 1, 2)],
    )
    swaps = [pairs + [(b, a) for a, b in pairs] for pairs in ends]

    def swap(values, side):
        return lax.ppermute(values, "gx", swaps[side])

    plane = (size_y, size_z)
    half = (2, 2) + plane
    face = (2, 3) + plane
    body = (layers,) + face
    more = (layers + 1,) + face

    e_p, e_z = call(faces_kernel, "first_faces", [VMEM], [half] * 2, [face])(start)
    e_p_in = swap(e_p, 0)
    a_p, a_z = call(faces_kernel, "adjoint_faces", [VMEM], [half] * 2, [face])(adjoint)
    (src,) = call(source_kernel, "source", [VMEM] * 3, [(layers,) + plane])(
        wave, tx_count[None], tx_cells[None]
    )
    e_z, a_p, a_z, src, e1_start = lax.optimization_barrier((e_z, a_p, a_z, src, start))
    e_z_in = swap(e_z, 1)
    (e1,) = call(first_sweep_kernel, "first_sweep", [VMEM] * 5, [body], [more, more])(
        wave, src, e1_start, sigma_h, sigma_v
    )

    def second(side, halo):
        return call(
            lambda *refs: second_faces_kernel(side, *refs),
            "second_faces_%d" % side,
            [VMEM] * 5,
            [face, half],
        )(wave, halo, e1, sigma_h, sigma_v)

    e1_p, e1_p_out = second(0, e_p_in)
    e1_p_in = swap(e1_p_out, 0)
    adjoint, e1_p = lax.optimization_barrier((adjoint, e1_p))
    (a1,) = call(first_adjoint_kernel, "first_adjoint", [VMEM] * 4, [body], [more, more])(
        wave, adjoint, sigma_h, sigma_v
    )
    a1, e_z_in = lax.optimization_barrier((a1, e_z_in))
    e1_z, e1_z_out = second(1, e_z_in)
    a_p, e1_z_out = lax.optimization_barrier((a_p, e1_z_out))
    e1_z_in = swap(e1_z_out, 1)
    a_p_in = swap(a_p, 0)
    e2, a1_body = call(
        second_sweep_kernel, "second_sweep", [VMEM] * 9, [body, body], [more, more]
    )(wave, e1, e1_p, e1_z, a1, src, seen, sigma_h, sigma_v)
    e2, a_z, e1_p_in, e1_z_in = lax.optimization_barrier((e2, a_z, e1_p_in, e1_z_in))
    a_z_in = swap(a_z, 1)

    def third(side, e_halo, a_halo):
        return call(
            lambda *refs: third_faces_kernel(side, *refs),
            "third_faces_%d" % side,
            [VMEM] * 8,
            [face, face, half],
        )(wave, e_halo, a_halo, e2, a1, seen, sigma_h, sigma_v)

    e2_p, a1_p, a1_p_out = third(0, e1_p_in, a_p_in)
    a1_p_in = swap(a1_p_out, 0)
    a1_p, a_z_in = lax.optimization_barrier((a1_p, a_z_in))
    e2_z, a1_z, a1_z_out = third(1, e1_z_in, a_z_in)
    a1_z_in = swap(a1_z_out, 1)
    inner_blocks = (freqs, 2, layers - 2, share, size_z)
    blocks = (freqs, 2, layers, share, size_z)
    final, faces, inner = call(
        last_sweep_kernel,
        "last_sweep",
        [VMEM] * 10,
        [(2, 3, layers) + plane, (2,) + face, inner_blocks],
        [more, more],
    )(wave, e2, e2_p, e2_z, a1_body, a1_p, a1_z, seen, sigma_h, sigma_v)
    faces, a1_p_in = lax.optimization_barrier((faces, a1_p_in))
    (terms,) = call(gradient_kernel, "gradient", [VMEM] * 9, [blocks])(
        wave, a1_p_in, a1_z_in, e2_p, e2_z, faces, inner, sigma_h, sigma_v
    )
    gathered = lax.all_to_all(terms, "freq", 0, 0)
    return (jnp.sum(gathered, axis=0), final[None])


def solution(mesh):
    placed = (
        P("gx", None, None),
        P("gx", None, None),
        P("freq"),
        P("freq", None, None, "gx", None, None),
        P("freq", None, None, "gx", None, None),
        P("freq", None, None, "gx", None, None),
        P(),
        P(),
    )
    return jax.shard_map(
        on_device,
        mesh=mesh,
        in_specs=placed,
        out_specs=(P(None, "gx", "freq", None), P("freq", None, None, "gx", None, None)),
        check_vma=False,
    )
```
